32 devices in a mesh: dp: 8 (over y, x, core), expert: 4 (over z).
Axes of the slice: x: 2, y: 2, z: 4, core: 2. Of those that a mesh axis runs over, the one named last changes fastest.
Arguments:
- tokens: bfloat16 [8192, 2048], P(('dp', 'expert')), may hold values from -6 to 6
- cotangent: bfloat16 [8192, 2048], P(('dp', 'expert')), may hold values from -6 to 6
- routes: int32 [8192, 2], P(('dp', 'expert')), may hold values from 0 to 3, all different within a row; in each aligned block of 256 rows (0 to 255, 256 to 511, ...) at most 192 rows name the same one
- gate_probs: float32 [8192, 2], P(('dp', 'expert')), may hold values from 0.2 to 1
- w_up: bfloat16 [4, 2048, 768], P('expert'), may hold values from -0.125 to 0.125
- w_down: bfloat16 [4, 768, 2048], P('expert'), may hold values from -0.21875 to 0.21875
- decay_rate: float32 [4, 768], P('expert'), may hold values from 0.3 to 0.95
Outputs:
- layer_out: bfloat16 [8192, 2048], P(('dp', 'expert'))
- token_grad: bfloat16 [8192, 2048], P(('dp', 'expert'))
- gate_grad: float32 [8192, 2], P(('dp', 'expert'))
- up_grad: float32 [4, 2048, 768], P('expert', 'dp')
- down_grad: float32 [4, 768, 2048], P('expert', None, 'dp')
The draws below stay inside these ranges and needn't reach their ends.
Inputs may be any that keep to these rules, and one draw needn't show every extreme that they name: `routes`: each token names two different experts; among the 256 rows of one device no expert is named by more than 192 rows, and in every draw some expert is named by exactly 192 rows of some device.
All inputs are finite; a program needn't handle non-finite values.
Results may differ from the reference program's by a relative error of at most 0.015.
Values may be sent and summed in bfloat16 or wider, within the bound.
A program may use at most 128 MiB of HBM per device.

```python
import math
from functools import partial
import jax
import jax.numpy as jnp
import numpy as np
from jax import lax

D = 2048
FF = 768
STEPS = 4
TOK_DEV = 256
EXPERTS = 4
CAP = 192
TOKENS = 8192


def strengthened(array, key, source, target, shards_of, factor):
    owner, partner = [(jnp.arange(array.shape[dim]) // (array.shape[dim] // shards_of)).reshape([-1 if axis == dim else 1 for axis in range(array.ndim)]) for dim in (source, target)]
    chosen = jax.random.permutation(key, shards_of)[partner]
    strong = (owner == chosen) | (owner == (partner + shards_of // 2) % shards_of)
    return jnp.where(strong, factor * array, array)


def levels(own_key, shape, shards, smallest, largest):
    def one(axis_at, blocks):
        draws = jax.random.uniform(jax.random.fold_in(jax.random.fold_in(own_key, 6), axis_at), (blocks,), jnp.float32, smallest / len(shards), largest / len(shards))
        return jnp.repeat(jnp.exp(draws), shape[axis_at] // blocks).reshape((-1,) + (1,) * (len(shape) - axis_at - 1))

    loudness = one(*shards[0])
    for cut in shards[1:]:
        loudness = loudness * one(*cut)
    return loudness


def deal_out(stream_key, own, number, rows, count, top, limit, skew):
    order = jax.random.permutation(stream_key, count)
    packed, ordinary = load_shares(count, rows * top, limit, skew, True), load_shares(count, rows * top, limit, skew, False)
    places = jnp.arange(count)

    def named(sizes, turn):
        used = int((sizes > 0).sum())
        fixed = max(1, used // 4)
        passed = fixed + (places - fixed + turn * (used - fixed)) % max(1, count - fixed)
        return jnp.zeros((count,), jnp.int32).at[order[jnp.where(places < fixed, places, passed)]].set(jnp.asarray(sizes, jnp.int32))

    sizes = jnp.where(number % 4 == 0, named(packed, number // 4), named(ordinary, number - number // 4 - 1))
    mixed = jax.random.permutation(jax.random.fold_in(own, 3), count)
    source_of, receiver = mixed[0:count // 2 * 2:2], mixed[1:count // 2 * 2:2]
    margin = jnp.minimum(sizes[source_of] - 1, limit - sizes[receiver]) // 2
    margin = jnp.where((source_of == order[0]) | (receiver == order[0]) | (sizes[receiver] == 0), 0, jnp.maximum(margin, 0))
    passed = jax.random.randint(jax.random.fold_in(own, 4), (count // 2,), 0, 1 << 20) % (margin + 1)
    sizes = sizes.at[source_of].add(-passed).at[receiver].add(passed)
    members = jnp.searchsorted(jnp.cumsum(sizes), jnp.arange(rows * top), side="right").astype(jnp.int32)
    listing = members.reshape(top, rows).T
    listing = listing[jax.random.permutation(jax.random.fold_in(own, 1), rows)]
    turn = jax.random.randint(jax.random.fold_in(own, 2), (rows, 1), 0, top)
    return jnp.take_along_axis(listing, (jnp.arange(top)[None, :] + turn) % top, axis=1)


def load_shares(count, total, limit, skew, full):
    portions = [(1 << 20) // math.isqrt(rank ** skew) + 1 for rank in range(1, count + 1)]
    largest = limit if full else min(limit, max(-(-total // count), total * portions[0] // sum(portions)))
    least = 1 if total - largest >= count - 1 else 0
    counts, spare = [largest] + [least] * (count - 1), total - largest - least * (count - 1)
    while spare > 0:
        candidates = [i for i in range(1, count) if counts[i] < largest] or [i for i in range(1, count) if counts[i] < limit]
        whole, remaining = sum([portions[i] for i in candidates]), spare
        for i in candidates:
            more = min(limit - counts[i], max(1, remaining * portions[i] // whole), spare)
            counts[i] = counts[i] + more
            spare = spare - more
    return np.array(counts)


def noise(stream_key, extent, scale, limit, shards=(), kind=jnp.bfloat16):
    drawn = jax.random.normal(stream_key, extent, jnp.float32) * scale
    if len(shards) > 0:
        drawn = levels(stream_key, extent, shards, -0.22, 0.18) * drawn
    return jnp.clip(drawn, min=-limit, max=limit).astype(kind)


def noise_with(key, shape, width, reach, pieces, heavy, kind=jnp.bfloat16):
    array = width * jax.random.normal(key, shape, jnp.float32)
    if pieces:
        array = array * levels(key, shape, pieces, -0.22, 0.18)
    return jnp.clip(strengthened(array, jax.random.fold_in(key, 3), *heavy), -reach, reach).astype(kind)


def setup_inputs(seed: int = 0) -> dict:
    arg_keys = jax.random.split(jax.random.key(seed), 8)
    tokens = noise_with(arg_keys[0], (TOKENS, D), 1.0, 6.0, ((0, 32),), (0, 1, 32, 2.75))
    cotangent = noise_with(arg_keys[1], (TOKENS, D), 1.0, 6.0, ((0, 32),), (0, 1, 32, 2.75))
    routes_keys = jax.random.split(jax.random.fold_in(arg_keys[2], 1), TOKENS // TOK_DEV)
    routes_turns = jax.random.permutation(jax.random.fold_in(arg_keys[2], 3), TOKENS // TOK_DEV)
    routes = jax.vmap(lambda own, number: deal_out(jax.random.fold_in(arg_keys[2], 2), own, number, TOK_DEV, EXPERTS, 2, CAP, 2))(routes_keys, routes_turns).reshape((TOKENS, 2))
    gate_probs = jnp.clip(0.2 + 0.8 * jax.random.uniform(arg_keys[3], (TOKENS, 2), jnp.float32) ** levels(arg_keys[3], (TOKENS, 2), ((0, 32),), -0.2, 0.2), 0.2, 1.0)
    w_up = noise(arg_keys[4], (EXPERTS, D, FF), D ** -0.5, 0.125, ((0, 4),))
    w_down = noise(arg_keys[5], (EXPERTS, FF, D), FF ** -0.5, 0.21875, ((0, 4),))
    decay_rate = jnp.clip(jnp.exp(math.log(0.95) - 1.1526795 * jax.random.uniform(arg_keys[6], (EXPERTS, FF), jnp.float32) ** levels(arg_keys[6], (EXPERTS, FF), ((0, 4),), -0.2, 0.2)), 0.3, 0.95)
    return {"tokens": tokens, "cotangent": cotangent, "routes": routes, "gate_probs": gate_probs, "w_up": w_up, "w_down": w_down, "decay_rate": decay_rate}


sharpness = 4.0

def spike_rate(current, decay_rate):
    potential = jnp.zeros_like(current)
    running = jnp.zeros_like(current)
    for tick_index in range(STEPS):
        potential = decay_rate * potential + current
        spikes = jax.nn.sigmoid(sharpness * (potential - 1.0))
        potential = potential - spikes
        running = running + spikes
    return running / STEPS

def place_slots(route_rows, experts_here, capacity):
    chosen = route_rows.reshape(-1).astype(jnp.int32)
    onehot = (chosen[:, None] == jnp.arange(experts_here, dtype=jnp.int32)[None, :]).astype(jnp.int32)
    rank_table = (jnp.cumsum(onehot, axis=0) - 1).astype(jnp.int32)
    return chosen * capacity + lax.optimization_barrier(jnp.sum(rank_table * onehot, axis=1)).astype(jnp.int32)

def fill_slots(position, slot_count):
    order = jnp.arange(position.shape[0], dtype=jnp.int32)
    slot_owner = jnp.zeros((slot_count,), jnp.int32).at[position].set(order)
    live_slots = jnp.zeros((slot_count,), jnp.int32).at[position].set(1)
    return (slot_owner, live_slots)

def expert_pass(recv_rows, rows_grad, weight_up, weight_down, rates_decay):
    current = jnp.dot(recv_rows, weight_up, preferred_element_type=jnp.float32)
    rates, pullback = jax.vjp(partial(spike_rate, decay_rate=rates_decay), current)
    rates_low = rates.astype(jnp.bfloat16)
    outputs = jnp.dot(rates_low, weight_down, preferred_element_type=jnp.float32).astype(jnp.bfloat16)
    rate_grad = jnp.dot(rows_grad, weight_down.T, preferred_element_type=jnp.float32)
    current_grad = pullback(rate_grad)[0].astype(jnp.bfloat16)
    rows_back = jnp.dot(current_grad, weight_up.T, preferred_element_type=jnp.float32).astype(jnp.bfloat16)
    return (outputs, rows_back, rates_low, current_grad)

def reference(tokens, cotangent, routes, gate_probs, w_up, w_down, decay_rate):
    blocks = TOKENS // TOK_DEV
    slot_count = EXPERTS * CAP
    position = jax.vmap(partial(place_slots, experts_here=EXPERTS, capacity=CAP))(routes.reshape(blocks, TOK_DEV * 2))
    slot_owner, live_slots = jax.vmap(partial(fill_slots, slot_count=slot_count))(position)
    token_blocks = tokens.reshape(blocks, TOK_DEV, D)
    cot_blocks = cotangent.reshape(blocks, TOK_DEV, D)
    gate_blocks = gate_probs.reshape(blocks, TOK_DEV * 2)
    take_rows = jax.vmap(lambda source, index: source[index])

    def one_expert(operands):
        weight_up, weight_down, rates_decay, expert_id = operands
        owners = lax.dynamic_slice_in_dim(slot_owner, expert_id * CAP, CAP, 1)
        live = lax.dynamic_slice_in_dim(live_slots, expert_id * CAP, CAP, 1) > 0
        token_index = owners // 2
        zero = jnp.zeros((), jnp.bfloat16)
        recv_rows = jnp.where(live[:, :, None], take_rows(token_blocks, token_index), zero)
        slot_gates = take_rows(gate_blocks, owners)
        scaled = (slot_gates[:, :, None] * take_rows(cot_blocks, token_index).astype(jnp.float32)).astype(jnp.bfloat16)
        rows_grad = jnp.where(live[:, :, None], scaled, zero)
        flat_rows = recv_rows.reshape(blocks * CAP, D)
        flat_grad = rows_grad.reshape(blocks * CAP, D)
        outputs, rows_back, rates_low, current_grad = expert_pass(flat_rows, flat_grad, weight_up, weight_down, rates_decay)
        grad_up = jnp.dot(flat_rows.T, current_grad, preferred_element_type=jnp.float32)
        grad_down = jnp.dot(rates_low.T, flat_grad, preferred_element_type=jnp.float32)
        return (outputs.reshape(blocks, CAP, D), rows_back.reshape(blocks, CAP, D), grad_up, grad_down)
    expert_ids = jnp.arange(EXPERTS, dtype=jnp.int32)
    expert_out, expert_back, up_grad, down_grad = lax.map(one_expert, (w_up, w_down, decay_rate, expert_ids))
    chosen = routes.reshape(blocks, TOK_DEV * 2).astype(jnp.int32)
    block_ids = jnp.arange(blocks, dtype=jnp.int32)[:, None]
    assign_index = ((chosen * blocks + block_ids) * CAP + (position - chosen * CAP)).reshape(-1)
    flat_out = expert_out.reshape(-1, D)[assign_index].reshape(TOKENS, 2, D).astype(jnp.float32)
    flat_back = expert_back.reshape(-1, D)[assign_index].reshape(TOKENS, 2, D).astype(jnp.float32)
    layer_out = lax.optimization_barrier(jnp.sum(gate_probs[:, :, None] * flat_out, axis=1)).astype(jnp.bfloat16)
    gate_grad = lax.optimization_barrier(jnp.sum(cotangent[:, None, :].astype(jnp.float32) * flat_out, axis=2))
    token_grad = lax.optimization_barrier(jnp.sum(flat_back, axis=1)).astype(jnp.bfloat16)
    return (layer_out, token_grad, gate_grad, up_grad, down_grad)
```

```python
from functools import partial

import jax
import jax.numpy as jnp
from jax import lax
from jax.experimental import pallas as pl
from jax.experimental.pallas import tpu as pltpu
from jax.sharding import PartitionSpec as P

STEPS = 4
SHARP = 4.0

BF = jnp.bfloat16
F32 = jnp.float32


def rate_and_slope(current, decay):
    v = jnp.zeros_like(current)
    dv = jnp.zeros_like(current)
    total = jnp.zeros_like(current)
    slope = jnp.zeros_like(current)
    for _ in range(STEPS):
        v = decay * v + current
        dv = decay * dv + 1.0
        s = jax.nn.sigmoid(SHARP * (v - 1.0))
        ds = SHARP * s * (1.0 - s) * dv
        v = v - s
        dv = dv - ds
        total = total + s
        slope = slope + ds
    return total / STEPS, slope / STEPS


def mm(a, b, dims):
    return lax.dot_general(a, b, (dims, ((), ())), preferred_element_type=F32)


def expert_block(x, cot, gate, w_up, w_down, decay):
    rates, slope = rate_and_slope(mm(x, w_up, ((1,), (0,))), decay)
    rates = rates.astype(BF)
    cot32 = cot.astype(F32)
    scaled = (gate[:, None] * cot32).astype(BF)
    out = mm(rates, w_down, ((1,), (0,))).astype(BF).astype(F32)
    layer = gate[:, None] * out
    dots = jnp.sum(cot32 * out, axis=1)
    rate_grad = mm(scaled, w_down, ((1,), (1,)))
    current_grad = (rate_grad * slope).astype(BF)
    back = mm(current_grad, w_up, ((1,), (1,))).astype(BF).astype(F32)
    return layer, dots, back, rates, scaled, current_grad


def flip(pos, mask):
    for k in range(mask.bit_length()):
        b = 1 << k
        if mask & b:
            pos = pos + b * (1 - 2 * ((pos // b) % 2))
    return pos


def bit_orders(parts):
    bits = [1 << k for k in range(parts.bit_length() - 1)]
    rest = bits[1:]
    cut = len(rest) // 2
    return bits[:1] + rest[:cut] + rest[cut:], bits[:1] + rest[cut:] + rest[:cut]


def greet(n, parts):
    ex, dp = lax.axis_index("expert"), lax.axis_index("dp")
    barrier = pltpu.get_barrier_semaphore()
    masks = list(range(1, n // 2 + 1))
    for d in masks:
        pl.semaphore_signal(barrier, inc=1, device_id={"expert": flip(ex, d)}, device_id_type=pl.DeviceIdType.MESH)
    bits = bit_orders(parts)[0]
    for b in bits:
        pl.semaphore_signal(barrier, inc=1, device_id={"dp": flip(dp, b)}, device_id_type=pl.DeviceIdType.MESH)
    pl.semaphore_wait(barrier, len(masks) + len(bits))
    return ex, dp


class Sender:
    def __init__(self, send, recv):
        self.send, self.recv, self.count, self.all = send, recv, 0, []

    def start(self, src, dst, axis, target):
        k = self.count
        self.count += 1
        copy = pltpu.make_async_remote_copy(
            src_ref=src, dst_ref=dst, send_sem=self.send.at[k], recv_sem=self.recv.at[k],
            device_id={axis: target}, device_id_type=pl.DeviceIdType.MESH,
        )
        copy.start()
        self.all.append(copy)
        return copy

    def drain(self):
        for copy in self.all:
            copy.wait_send()


def dispatch_kernel(n, parts, x, c, t, up, down, dec, xo, co, to, upo, downo, deco, send, recv):
    ex, dp = greet(n, parts)
    half = n // 2
    s = Sender(send, recv)
    mate = flip(ex, half)
    first_up = s.start(up.at[dp], upo.at[dp], "expert", mate)
    first_down = s.start(down.at[dp], downo.at[dp], "expert", mate)
    late = [s.start(dec, deco, "expert", mate)]
    for d in range(1, half):
        to_dev = flip(ex, d)
        late.append(s.start(t, to.at[d - 1], "expert", to_dev))
        late.append(s.start(x, xo.at[d - 1], "expert", to_dev))
        late.append(s.start(c, co.at[d - 1], "expert", to_dev))
    orders = [o[::-1] for o in bit_orders(parts)]
    waiting = [[first_up], [first_down]]
    held = [[0], [0]]
    for stage in range(len(orders[0])):
        for a, buf in ((0, upo), (1, downo)):
            for copy in waiting[a]:
                copy.wait_recv()
            b = orders[a][stage]
            waiting[a] = []
            for r in held[a]:
                place = flip(dp, r)
                waiting[a].append(s.start(buf.at[place], buf.at[place], "dp", flip(dp, b)))
            held[a] = held[a] + [r ^ b for r in held[a]]
    for copy in waiting[0] + waiting[1] + late:
        copy.wait_recv()
    s.drain()


def dispatch(n, parts, x, c, t, up, down, dec):
    half = n // 2
    stack = lambda v: jax.ShapeDtypeStruct((half - 1,) + v.shape, v.dtype)
    same = lambda v: jax.ShapeDtypeStruct(v.shape, v.dtype)
    copies = 3 + 3 * (half - 1) + 2 * (parts - 1)
    anywhere = pl.BlockSpec(memory_space=pl.ANY)
    return pl.pallas_call(
        partial(dispatch_kernel, n, parts),
        out_shape=(stack(x), stack(c), stack(t), same(up), same(down), same(dec)),
        in_specs=[anywhere] * 6,
        out_specs=[anywhere] * 6,
        scratch_shapes=[pltpu.SemaphoreType.DMA((copies,)), pltpu.SemaphoreType.DMA((copies,))],
        compiler_params=pltpu.CompilerParams(collective_id=0, has_side_effects=True),
        name="dispatch",
    )(x, c, t, up, down, dec)


def add_rows(rows, read_a, read_b, write):
    step = 32 if rows % 32 == 0 else rows

    @pl.loop(0, rows // step)
    def _(i):
        cut = pl.ds(pl.multiple_of(i * step, step), step)
        write(cut, read_a(cut).astype(F32) + read_b(cut).astype(F32))


def return_kernel(n, parts, x, cg1, sc1, rt1, cg2, sc2, rt2, lay, bak, dots, upo, downo, layo, bako,
                  dotso, products, slots, far, send, recv):
    ex, dp = greet(n, parts)
    half = n // 2
    s = Sender(send, recv)
    rows = slots.shape[2]
    grads = [products.at[a] for a in range(4)]
    pairs = ((x, cg1), (sc1, rt1), (x, cg2), (sc2, rt2))
    tile = 256
    per = tile // rows

    def multiply(a):
        left, right = pairs[a]

        @pl.loop(0, left.shape[1] // tile)
        def _(i):
            cols = pl.ds(pl.multiple_of(i * tile, tile), tile)
            res = mm(left[:, cols], right[...], ((0,), (0,))).astype(BF)
            for k in range(per):
                products[a, i * per + k] = res[k * rows:(k + 1) * rows]

    orders = bit_orders(parts)
    orders = (orders[0], orders[1], orders[0], orders[1])
    stages = len(orders[0])
    place, keep = [], []
    for a in range(4):
        ids, kept, live, k = {}, [], list(range(parts)), 0
        for st in range(stages):
            live = [r for r in live if not r & orders[a][st]]
            kept.append(live)
            for r in live:
                ids[(st, r)] = k
                k += 1
        place.append(ids)
        keep.append(kept)

    def begin(a, st):
        b = orders[a][st]
        out = []
        for r in keep[a][st]:
            far_r = r ^ b
            src = grads[a].at[flip(dp, far_r)] if st == 0 else slots.at[a, place[a][(st - 1, far_r)]]
            out.append(s.start(src, slots.at[a, place[a][(st, r)]], "dp", flip(dp, b)))
        return out

    def finish(a, st, copies):
        for copy in copies:
            copy.wait_recv()
        for r in keep[a][st]:
            k = place[a][(st, r)]
            if st == 0:
                chunk = flip(dp, r)
                other = lambda cut: products[a, chunk, cut, :]
            else:
                old = place[a][(st - 1, r)]
                other = lambda cut: slots[a, old, cut, :]
            if st == stages - 1 and a < 2:
                out = (upo, downo)[a]
                def write(cut, v):
                    out[cut, :] = v
            else:
                def write(cut, v):
                    slots[a, k, cut, :] = v.astype(BF)
            add_rows(rows, lambda cut: slots[a, k, cut, :], other, write)

    late = []
    run = {}
    for d in range(1, half):
        to_dev = flip(ex, d)
        late.append(s.start(lay.at[d - 1], layo.at[d - 1], "expert", to_dev))
        late.append(s.start(bak.at[d - 1], bako.at[d - 1], "expert", to_dev))
        late.append(s.start(dots.at[d - 1], dotso.at[d - 1], "expert", to_dev))
    for a in (2, 3):
        multiply(a)
        run[a] = begin(a, 0)
    swaps = []
    for st in range(stages):
        for a in (2, 3):
            finish(a, st, run[a])
            if st + 1 < stages:
                run[a] = begin(a, st + 1)
            else:
                k = place[a][(st, 0)]
                swaps.append(s.start(slots.at[a, k], far.at[a - 2], "expert", flip(ex, half)))
        for a in (0, 1):
            if st == 0:
                multiply(a)
                run[a] = begin(a, 0)
            else:
                finish(a, st - 1, run[a])
                run[a] = begin(a, st)
    for a in (0, 1):
        finish(a, stages - 1, run[a])
    for a, out in ((0, upo), (1, downo)):
        swaps[a].wait_recv()

        def write(cut, v, out=out):
            out[cut, :] = v

        add_rows(rows, lambda cut: out[cut, :], lambda cut: far[a, cut, :], write)
    for copy in late:
        copy.wait_recv()
    s.drain()


def give_back(n, parts, factors, lay, bak, dots):
    half = n // 2
    same = lambda v: jax.ShapeDtypeStruct(v.shape, v.dtype)
    rows, cols = factors[0].shape[1] // parts, factors[1].shape[1]
    copies = 4 * (parts - 1) + 2 + 3 * (half - 1)
    anywhere = pl.BlockSpec(memory_space=pl.ANY)
    vmem = pl.BlockSpec(memory_space=pltpu.VMEM)
    shard = jax.ShapeDtypeStruct((rows, cols), F32)
    return pl.pallas_call(
        partial(return_kernel, n, parts),
        out_shape=(shard, shard, same(lay), same(bak), same(dots)),
        in_specs=[vmem] * 7 + [anywhere] * 3,
        out_specs=[vmem] * 2 + [anywhere] * 3,
        scratch_shapes=[
            pltpu.VMEM((4, parts, rows, cols), BF),
            pltpu.VMEM((4, parts - 1, rows, cols), BF),
            pltpu.VMEM((2, rows, cols), BF),
            pltpu.SemaphoreType.DMA((copies,)),
            pltpu.SemaphoreType.DMA((copies,)),
        ],
        compiler_params=pltpu.CompilerParams(
            collective_id=1, has_side_effects=True, vmem_limit_bytes=50 * 2**20
        ),
        name="give_back",
    )(*factors, lay, bak, dots)


def local_wide(tokens, cotangent, routes, gate_probs, w_up, w_down, decay_rate):
    rows, width = tokens.shape
    n = lax.axis_size("expert")
    parts = lax.axis_size("dp")
    half = n // 2
    me = lax.axis_index("expert")
    w_up, w_down, decay = w_up[0], w_down[0], decay_rate[0]
    hidden = w_up.shape[1]
    ids = jnp.arange(n, dtype=jnp.int32)
    hit = routes[None, :, :] == ids[:, None, None]
    table = jnp.sum(jnp.where(hit, gate_probs[None, :, :], 0.0), axis=2)
    x_far, cot_far, tab_far, w_up2, w_down2, decay2 = dispatch(
        n, parts, tokens, cotangent, table,
        w_up.reshape(parts, width // parts, hidden),
        w_down.reshape(parts, hidden // parts, width),
        decay[None],
    )
    w_up2 = w_up2.reshape(width, hidden)
    w_down2 = w_down2.reshape(hidden, width)
    decay2 = decay2[0]
    x_all = jnp.concatenate([tokens, x_far.reshape(-1, width)], axis=0)
    cot_all = jnp.concatenate([cotangent, cot_far.reshape(-1, width)], axis=0)
    tabs = jnp.concatenate([table[None], tab_far], axis=0)
    other = me ^ half

    def gate_of(expert):
        pick = (ids == expert)[None, :, None]
        return jnp.sum(jnp.where(pick, tabs, 0.0), axis=1).reshape(-1)

    layer1, dots1, back1, rates1, scaled1, cg1 = expert_block(
        x_all, cot_all, gate_of(me), w_up, w_down, decay
    )
    layer2, dots2, back2, rates2, scaled2, cg2 = expert_block(
        x_all, cot_all, gate_of(other), w_up2, w_down2, decay2
    )
    factors = (x_all, cg1, scaled1, rates1, cg2, scaled2, rates2)
    layer = (layer1 + layer2).reshape(half, rows, width)
    back = (back1 + back2).reshape(half, rows, width)
    dots = jnp.where((ids == me)[None, :, None], dots1.reshape(half, 1, rows), 0.0) + jnp.where(
        (ids == other)[None, :, None], dots2.reshape(half, 1, rows), 0.0
    )
    up_grad, down_grad, layer_far, back_far, dots_far = give_back(
        n, parts, factors, layer[1:].astype(BF), back[1:].astype(BF), dots[1:]
    )
    layer_out = layer[0] + jnp.sum(layer_far.astype(F32), axis=0)
    token_grad = back[0] + jnp.sum(back_far.astype(F32), axis=0)
    own = dots[0] + jnp.sum(dots_far, axis=0)
    gate_grad = jnp.sum(jnp.where(hit, own[:, :, None], 0.0), axis=0)
    return (layer_out.astype(BF), token_grad.astype(BF), gate_grad, up_grad[None], down_grad.T[None])


def lif(current, decay):
    two = current + current
    k = decay + (two - 2.0)
    a = two - 2.0
    dv = None
    for step in range(STEPS):
        if step > 0:
            a = decay * q + k
        t = jnp.tanh(a)
        q = a - t
        t2 = t * t
        if step == 0:
            e = t2
            total, slope = t, 1.0 - t2
        else:
            dv = decay * e + 1.0
            e = t2 * dv
            total, slope = total + t, slope + (dv - e)
    return 0.5 + (0.5 / STEPS) * total, (1.0 / STEPS) * slope


def fused_kernel(x, c, rt, gp, wu, wd, dec,
                 lay_out, tok_out, gg_out, upo, dno,
                 xall, call, wub, wdb, decf, tab_s, tab_r, dot_s, dot_r, gcol, dacc, s_cur, s_u,
                 gr, cg, lo, bo, ls, bs, lr, br, products, slots, far, lsem, send, recv):
    ex, dp = lax.axis_index("expert"), lax.axis_index("dp")
    pair, mate = flip(ex, 1), flip(ex, 2)
    rows, width = x.shape
    hidden = wu.shape[1]
    blk = rows // 2
    s = Sender(send, recv)

    loads = [
        pltpu.make_async_copy(x, xall.at[pl.ds(0, rows)], lsem.at[0]),
        pltpu.make_async_copy(wu, wub.at[0], lsem.at[1]),
        pltpu.make_async_copy(c, call.at[pl.ds(0, rows)], lsem.at[2]),
        pltpu.make_async_copy(wd, wdb.at[pl.ds(0, hidden)], lsem.at[3]),
    ]
    for copy in loads:
        copy.start()

    def gate_row(expert):
        return jnp.where(rt[0:1, :] == expert, gp[0:1, :], 0.0) + jnp.where(rt[1:2, :] == expert, gp[1:2, :], 0.0)

    tab_s[...] = jnp.zeros_like(tab_s)
    tab_s[0:1, :] = gate_row(pair)
    tab_s[1:2, :] = gate_row(flip(pair, 2))

    barrier = pltpu.get_barrier_semaphore()
    for axis, dev in (("expert", pair), ("expert", mate), ("dp", flip(dp, 1)), ("dp", flip(dp, 2)), ("dp", flip(dp, 4))):
        pl.semaphore_signal(barrier, inc=1, device_id={axis: dev}, device_id_type=pl.DeviceIdType.MESH)
    pl.semaphore_wait(barrier, 5)

    up_rows, dn_rows = width // 8, hidden // 8
    def up_cut(chunk, part):
        return pl.ds(pl.multiple_of(chunk * up_rows + part * (up_rows // 2), 16), up_rows // 2)

    def dn_cut(chunk, part, base=0):
        return pl.ds(pl.multiple_of(base + chunk * dn_rows + part * (dn_rows // 2), 16), dn_rows // 2)

    def send_weights(part):
        return [
            s.start(wu.at[up_cut(dp, part)], wub.at[1, up_cut(dp, part)], "expert", mate),
            s.start(wd.at[dn_cut(dp, part)], wdb.at[dn_cut(dp, part, hidden)], "expert", mate),
        ]

    def send_tokens(b):
        cut = pl.ds(b * blk, blk)
        there = pl.ds(rows + b * blk, blk)
        return [
            s.start(x.at[cut], xall.at[there], "expert", pair),
            s.start(c.at[cut], call.at[there], "expert", pair),
        ]

    first = s.start(dec, decf, "expert", mate)
    w_in = [send_weights(0), None]
    tab_in = s.start(tab_s, tab_r, "expert", pair)
    t_in = [send_tokens(0), None]

    def set_gates(slot, e, row):
        gcol[e, slot * rows:(slot + 1) * rows, :] = jnp.transpose(jnp.broadcast_to(row, (128, rows)))

    set_gates(0, 0, gate_row(ex))
    set_gates(0, 1, gate_row(mate))

    def half_pass(e, row0, m):
        @pl.loop(0, hidden // 256)
        def _(i):
            cols = pl.ds(pl.multiple_of(i * 256, 256), 256)
            far_cols = pl.ds(pl.multiple_of(e * hidden + i * 256, 256), 256)
            s_cur[0:m, cols] = mm(xall[row0:row0 + m, :], wub[e, :, cols], ((1,), (0,)))
            s_u[0:m, cols] = mm(call[row0:row0 + m, :], wdb[far_cols, :], ((1,), (1,)))

        d_ref = decf if e else dec

        @pl.loop(0, m // 16)
        def _(i):
            here = pl.ds(pl.multiple_of(i * 16, 16), 16)
            there = pl.ds(pl.multiple_of(row0 + i * 16, 16), 16)
            gate = gcol[e, there, :]
            dots = None
            for j in range(hidden // 128):
                cols = slice(j * 128, (j + 1) * 128)
                u = s_u[here, cols]
                rate, slope = lif(s_cur[here, cols], d_ref[0:1, cols])
                out = slice(e * hidden + j * 128, e * hidden + (j + 1) * 128)
                gr[there, out] = (gate * rate).astype(BF)
                cg[there, out] = (gate * u * slope).astype(BF)
                dots = rate * u if dots is None else dots + rate * u
            dacc[e, there, :] = dots

    def out_pass(row0, m, write):
        @pl.loop(0, width // 512)
        def _(i):
            cols = pl.ds(pl.multiple_of(i * 512, 512), 512)
            write(cols, mm(gr[row0:row0 + m, :], wdb[:, cols], ((1,), (0,))),
                  mm(cg[row0:row0 + m, 0:hidden], wub[0, cols, :], ((1,), (1,)))
                  + mm(cg[row0:row0 + m, hidden:2 * hidden], wub[1, cols, :], ((1,), (1,))))

    for copy in loads:
        copy.wait()
    half_pass(0, 0, rows)

    orders = ((4, 2), (2, 4))

    def forward(a, part, r, axes):
        chunk = flip(dp, r)
        ref = wub.at[1, up_cut(chunk, part)] if a == 0 else wdb.at[dn_cut(chunk, part, hidden)]
        return [s.start(ref, ref, "dp", flip(dp, b)) for b in axes]

    ring = {}

    def gather_first(part):
        for a in (0, 1):
            w_in[part][a].wait_recv()
            b1, b2 = orders[a]
            ring[a, part] = [forward(a, part, 0, (b1, b2, 1))]

    def gather_second(part):
        for a in (0, 1):
            b1, b2 = orders[a]
            ring[a, part][0][0].wait_recv()
            ring[a, part].append(forward(a, part, b1, (b2, 1)))

    def gather_third(part):
        for a in (0, 1):
            b1, b2 = orders[a]
            ring[a, part][0][1].wait_recv()
            ring[a, part].append(forward(a, part, b2, (1,)))
            ring[a, part][1][0].wait_recv()
            ring[a, part].append(forward(a, part, b1 | b2, (1,)))

    def gather_last(part):
        for a in (0, 1):
            for group in ring[a, part]:
                group[-1].wait_recv()

    gather_first(0)
    w_in[1] = send_weights(1)
    gather_second(0)
    gather_first(1)
    t_in[1] = send_tokens(1)
    gather_third(0)
    gather_second(1)
    tab_in.wait_recv()
    set_gates(1, 0, tab_r[0:1, :])
    set_gates(1, 1, tab_r[1:2, :])
    for copy in t_in[0]:
        copy.wait_recv()
    half_pass(0, rows, blk)
    gather_third(1)
    first.wait_recv()
    gather_last(0)
    gather_last(1)
    half_pass(1, 0, rows)
    half_pass(1, rows, blk)

    def keep(cols, lay, back):
        lo[:, cols] = lay
        bo[:, cols] = back

    out_pass(0, rows, keep)

    def leave(b):
        def write(cols, lay, back):
            ls[b * blk:(b + 1) * blk, cols] = lay.astype(BF)
            bs[b * blk:(b + 1) * blk, cols] = back.astype(BF)
        out_pass(rows + b * blk, blk, write)

    def send_back(b):
        cut = pl.ds(b * blk, blk)
        return [
            s.start(ls.at[cut], lr.at[cut], "expert", pair),
            s.start(bs.at[cut], br.at[cut], "expert", pair),
        ]

    leave(0)
    for copy in t_in[1]:
        copy.wait_recv()
    back_in = [send_back(0), None]
    half_pass(1, rows + blk, blk)
    half_pass(0, rows + blk, blk)

    tile = up_rows
    lefts = (xall, call, xall, call)
    axes = ((2, 4), (4, 2), (2, 4), (4, 2))
    run = {}

    def product(a, r):
        cols = pl.ds(pl.multiple_of(flip_by(dp, r) * tile, tile), tile)
        right = gr if a % 2 else cg
        e = a // 2
        products[a, r] = mm(lefts[a][:, cols], right[:, e * hidden:(e + 1) * hidden], ((0,), (0,))).astype(BF)

    def multiply(a):
        b1, b2 = axes[a]
        base = s.count
        s.count += 4

        def copy_of(i, r):
            return pltpu.make_async_remote_copy(
                src_ref=products.at[a, r], dst_ref=slots.at[a, r // 2], send_sem=send.at[base + i],
                recv_sem=recv.at[base + i], device_id={"dp": flip(dp, 1)}, device_id_type=pl.DeviceIdType.MESH,
            )

        @pl.loop(0, 4)
        def _(i):
            r = 1 + b1 - b1 * (i // 2) + b2 * (i % 2)
            product(a, r)
            copy_of(i, r).start()

        @pl.loop(0, 4)
        def _(i):
            product(a, b1 - b1 * (i // 2) + b2 * (i % 2))

        for i in range(4):
            r = 1 + b1 - b1 * (i // 2) + b2 * (i % 2)
            copy = copy_of(i, r)
            s.all.append(copy)
            run[a, 0, r - 1] = copy

    def total(a, k, other, write=None):
        def store(cut, v):
            slots[a, k, cut, :] = v.astype(BF)
        add_rows(tile, lambda cut: slots[a, k, cut, :], other, write or store)

    def stage0(a):
        b1, b2 = axes[a]
        for r in (b1, b1 | b2, 0, b2):
            run[a, 0, r].wait_recv()
            total(a, r // 2, lambda cut: products[a, r, cut, :])
            if r & b1:
                run[a, 1, r ^ b1] = s.start(slots.at[a, r // 2], slots.at[a, 4 + (r != b1)], "dp", flip(dp, b1))

    def stage1(a):
        b1, b2 = axes[a]
        for r in (b2, 0):
            run[a, 1, r].wait_recv()
            total(a, 4 + (r != 0), lambda cut: slots[a, r // 2, cut, :])
            if r:
                run[a, 2, 0] = s.start(slots.at[a, 5], slots.at[a, 6], "dp", flip(dp, b2))

    def stage2(a):
        run[a, 2, 0].wait_recv()
        if a < 2:
            out = (upo, dno)[a]

            def write(cut, v):
                out[cut, :] = v

            total(a, 6, lambda cut: slots[a, 4, cut, :], write)
        else:
            total(a, 6, lambda cut: slots[a, 4, cut, :])
            run[a, 3] = s.start(slots.at[a, 6], far.at[a - 2], "expert", mate)

    multiply(2)
    multiply(3)
    stage0(2)
    stage0(3)
    leave(1)
    dot_s[...] = jnp.zeros_like(dot_s)
    for e in (0, 1):
        dot_s[e:e + 1, :] = jnp.sum(jnp.transpose(dacc[e, rows:2 * rows, :]), axis=0, keepdims=True)
    back_in[1] = send_back(1)
    dots_in = s.start(dot_s, dot_r, "expert", pair)
    multiply(0)
    stage0(0)
    multiply(1)
    stage0(1)
    own = [jnp.sum(jnp.transpose(dacc[e, 0:rows, :]), axis=0, keepdims=True) for e in (0, 1)]
    stage1(2)
    stage1(3)

    def finish_rows(b):
        for copy in back_in[b]:
            copy.wait_recv()

        @pl.loop(0, blk // 16)
        def _(i):
            cut = pl.ds(pl.multiple_of(b * blk + i * 16, 16), 16)
            lay_out[cut, :] = (lo[cut, :] + lr[cut, :].astype(F32)).astype(BF)
            tok_out[cut, :] = (bo[cut, :] + br[cut, :].astype(F32)).astype(BF)

    stage2(2)
    stage2(3)
    finish_rows(0)
    stage1(0)
    stage1(1)
    finish_rows(1)
    dots_in.wait_recv()
    for k in (0, 1):
        chosen = rt[k:k + 1, :]
        acc = jnp.zeros((1, rows), F32)
        for expert, d in ((ex, own[0]), (mate, own[1]), (pair, dot_r[0:1, :]), (flip(pair, 2), dot_r[1:2, :])):
            acc = acc + jnp.where(chosen == expert, d, 0.0)
        gg_out[k:k + 1, :] = acc
    stage2(0)
    stage2(1)
    for a, out in ((0, upo), (1, dno)):
        run[a + 2, 3].wait_recv()

        def write(cut, v, out=out):
            out[cut, :] = v

        add_rows(tile, lambda cut: out[cut, :], lambda cut: far[a, cut, :], write)
    s.drain()


def flip_by(pos, mask):
    out = pos
    for b in (1, 2, 4):
        out = out + b * ((mask // b) % 2) * (1 - 2 * ((pos // b) % 2))
    return out


def local_fused(tokens, cotangent, routes, gate_probs, w_up, w_down, decay_rate):
    rows, width = tokens.shape
    hidden = w_up.shape[2]
    tile = width // 8
    sds = jax.ShapeDtypeStruct
    copies = 1 + 4 + 1 + 4 + 4 * 7 + 6 + 4 * 7 - 2 + 4
    copies = copies + 16
    anywhere = pl.BlockSpec(memory_space=pl.ANY)
    vmem = pl.BlockSpec(memory_space=pltpu.VMEM)
    layer_out, token_grad, gate_grad, up_grad, down_grad = pl.pallas_call(
        fused_kernel,
        out_shape=(
            sds((rows, width), BF), sds((rows, width), BF), sds((2, rows), F32),
            sds((tile, hidden), F32), sds((tile, hidden), F32),
        ),
        in_specs=[anywhere, anywhere, vmem, vmem, anywhere, anywhere, vmem],
        out_specs=[vmem] * 5,
        scratch_shapes=[
            pltpu.VMEM((2 * rows, width), BF),
            pltpu.VMEM((2 * rows, width), BF),
            pltpu.VMEM((2, width, hidden), BF),
            pltpu.VMEM((2 * hidden, width), BF),
            pltpu.VMEM((1, hidden), F32),
            pltpu.VMEM((8, rows), F32),
            pltpu.VMEM((8, rows), F32),
            pltpu.VMEM((8, rows), F32),
            pltpu.VMEM((8, rows), F32),
            pltpu.VMEM((2, 2 * rows, 128), F32),
            pltpu.VMEM((2, 2 * rows, 128), F32),
            pltpu.VMEM((rows, hidden), F32),
            pltpu.VMEM((rows, hidden), F32),
            pltpu.VMEM((2 * rows, 2 * hidden), BF),
            pltpu.VMEM((2 * rows, 2 * hidden), BF),
            pltpu.VMEM((rows, width), F32),
            pltpu.VMEM((rows, width), F32),
            pltpu.VMEM((rows, width), BF),
            pltpu.VMEM((rows, width), BF),
            pltpu.VMEM((rows, width), BF),
            pltpu.VMEM((rows, width), BF),
            pltpu.VMEM((4, 8, tile, hidden), BF),
            pltpu.VMEM((4, 7, tile, hidden), BF),
            pltpu.VMEM((2, tile, hidden), BF),
            pltpu.SemaphoreType.DMA((4,)),
            pltpu.SemaphoreType.DMA((copies,)),
            pltpu.SemaphoreType.DMA((copies,)),
        ],
        compiler_params=pltpu.CompilerParams(
            collective_id=2, has_side_effects=True, vmem_limit_bytes=60 * 2**20
        ),
        name="layer",
    )(tokens, cotangent, routes.T, gate_probs.T, w_up[0], w_down[0], decay_rate)
    return layer_out, token_grad, gate_grad.T, up_grad[None], down_grad.T[None]


def solution(mesh):
    rows = P(("dp", "expert"), None)
    local = local_fused if mesh.shape["expert"] == 4 and mesh.shape["dp"] == 8 else local_wide
    return jax.shard_map(
        local,
        mesh=mesh,
        in_specs=(rows, rows, rows, rows, P("expert", None, None), P("expert", None, None), P("expert", None)),
        out_specs=(rows, rows, rows, P("expert", "dp", None), P("expert", None, "dp")),
        check_vma=False,
    )
```

```python
from functools import partial

import jax
import jax.numpy as jnp
from jax import lax
from jax.experimental import pallas as pl
from jax.experimental.pallas import tpu as pltpu
from jax.sharding import PartitionSpec as P

STEPS = 4
SHARP = 4.0

BF = jnp.bfloat16
F32 = jnp.float32


def rate_and_slope(current, decay):
    v = jnp.zeros_like(current)
    dv = jnp.zeros_like(current)
    total = jnp.zeros_like(current)
    slope = jnp.zeros_like(current)
    for _ in range(STEPS):
        v = decay * v + current
        dv = decay * dv + 1.0
        s = jax.nn.sigmoid(SHARP * (v - 1.0))
        ds = SHARP * s * (1.0 - s) * dv
        v = v - s
        dv = dv - ds
        total = total + s
        slope = slope + ds
    return total / STEPS, slope / STEPS


def mm(a, b, dims):
    return lax.dot_general(a, b, (dims, ((), ())), preferred_element_type=F32)


def expert_block(x, cot, gate, w_up, w_down, decay):
    rates, slope = rate_and_slope(mm(x, w_up, ((1,), (0,))), decay)
    rates = rates.astype(BF)
    cot32 = cot.astype(F32)
    scaled = (gate[:, None] * cot32).astype(BF)
    out = mm(rates, w_down, ((1,), (0,))).astype(BF).astype(F32)
    layer = gate[:, None] * out
    dots = jnp.sum(cot32 * out, axis=1)
    rate_grad = mm(scaled, w_down, ((1,), (1,)))
    current_grad = (rate_grad * slope).astype(BF)
    back = mm(current_grad, w_up, ((1,), (1,))).astype(BF).astype(F32)
    return layer, dots, back, rates, scaled, current_grad


def flip(pos, mask):
    for k in range(mask.bit_length()):
        b = 1 << k
        if mask & b:
            pos = pos + b * (1 - 2 * ((pos // b) % 2))
    return pos


def bit_orders(parts):
    bits = [1 << k for k in range(parts.bit_length() - 1)]
    rest = bits[1:]
    cut = len(rest) // 2
    return bits[:1] + rest[:cut] + rest[cut:], bits[:1] + rest[cut:] + rest[:cut]


def greet(n, parts):
    ex, dp = lax.axis_index("expert"), lax.axis_index("dp")
    barrier = pltpu.get_barrier_semaphore()
    masks = list(range(1, n // 2 + 1))
    for d in masks:
        pl.semaphore_signal(barrier, inc=1, device_id={"expert": flip(ex, d)}, device_id_type=pl.DeviceIdType.MESH)
    bits = bit_orders(parts)[0]
    for b in bits:
        pl.semaphore_signal(barrier, inc=1, device_id={"dp": flip(dp, b)}, device_id_type=pl.DeviceIdType.MESH)
    pl.semaphore_wait(barrier, len(masks) + len(bits))
    return ex, dp


class Sender:
    def __init__(self, send, recv):
        self.send, self.recv, self.count, self.all = send, recv, 0, []

    def start(self, src, dst, axis, target):
        k = self.count
        self.count += 1
        copy = pltpu.make_async_remote_copy(
            src_ref=src, dst_ref=dst, send_sem=self.send.at[k], recv_sem=self.recv.at[k],
            device_id={axis: target}, device_id_type=pl.DeviceIdType.MESH,
        )
        copy.start()
        self.all.append(copy)
        return copy

    def sent(self, copy):
        copy.wait_send()
        self.all = [other for other in self.all if other is not copy]

    def drain(self):
        for copy in self.all:
            copy.wait_send()


def dispatch_kernel(n, parts, x, c, t, up, down, dec, xo, co, to, upo, downo, deco, send, recv):
    ex, dp = greet(n, parts)
    half = n // 2
    s = Sender(send, recv)
    mate = flip(ex, half)
    first_up = s.start(up.at[dp], upo.at[dp], "expert", mate)
    first_down = s.start(down.at[dp], downo.at[dp], "expert", mate)
    late = [s.start(dec, deco, "expert", mate)]
    for d in range(1, half):
        to_dev = flip(ex, d)
        late.append(s.start(t, to.at[d - 1], "expert", to_dev))
        late.append(s.start(x, xo.at[d - 1], "expert", to_dev))
        late.append(s.start(c, co.at[d - 1], "expert", to_dev))
    orders = [o[::-1] for o in bit_orders(parts)]
    waiting = [[first_up], [first_down]]
    held = [[0], [0]]
    for stage in range(len(orders[0])):
        for a, buf in ((0, upo), (1, downo)):
            for copy in waiting[a]:
                copy.wait_recv()
            b = orders[a][stage]
            waiting[a] = []
            for r in held[a]:
                place = flip(dp, r)
                waiting[a].append(s.start(buf.at[place], buf.at[place], "dp", flip(dp, b)))
            held[a] = held[a] + [r ^ b for r in held[a]]
    for copy in waiting[0] + waiting[1] + late:
        copy.wait_recv()
    s.drain()


def dispatch(n, parts, x, c, t, up, down, dec):
    half = n // 2
    stack = lambda v: jax.ShapeDtypeStruct((half - 1,) + v.shape, v.dtype)
    same = lambda v: jax.ShapeDtypeStruct(v.shape, v.dtype)
    copies = 3 + 3 * (half - 1) + 2 * (parts - 1)
    anywhere = pl.BlockSpec(memory_space=pl.ANY)
    return pl.pallas_call(
        partial(dispatch_kernel, n, parts),
        out_shape=(stack(x), stack(c), stack(t), same(up), same(down), same(dec)),
        in_specs=[anywhere] * 6,
        out_specs=[anywhere] * 6,
        scratch_shapes=[pltpu.SemaphoreType.DMA((copies,)), pltpu.SemaphoreType.DMA((copies,))],
        compiler_params=pltpu.CompilerParams(collective_id=0, has_side_effects=True),
        name="dispatch",
    )(x, c, t, up, down, dec)


def add_rows(rows, read_a, read_b, write):
    step = 32 if rows % 32 == 0 else rows

    @pl.loop(0, rows // step)
    def _(i):
        cut = pl.ds(pl.multiple_of(i * step, step), step)
        write(cut, read_a(cut).astype(F32) + read_b(cut).astype(F32))


def return_kernel(n, parts, x, cg1, sc1, rt1, cg2, sc2, rt2, lay, bak, dots, upo, downo, layo, bako,
                  dotso, products, slots, far, send, recv):
    ex, dp = greet(n, parts)
    half = n // 2
    s = Sender(send, recv)
    rows = slots.shape[2]
    grads = [products.at[a] for a in range(4)]
    pairs = ((x, cg1), (sc1, rt1), (x, cg2), (sc2, rt2))
    tile = 256
    per = tile // rows

    def multiply(a):
        left, right = pairs[a]

        @pl.loop(0, left.shape[1] // tile)
        def _(i):
            cols = pl.ds(pl.multiple_of(i * tile, tile), tile)
            res = mm(left[:, cols], right[...], ((0,), (0,))).astype(BF)
            for k in range(per):
                products[a, i * per + k] = res[k * rows:(k + 1) * rows]

    orders = bit_orders(parts)
    orders = (orders[0], orders[1], orders[0], orders[1])
    stages = len(orders[0])
    place, keep = [], []
    for a in range(4):
        ids, kept, live, k = {}, [], list(range(parts)), 0
        for st in range(stages):
            live = [r for r in live if not r & orders[a][st]]
            kept.append(live)
            for r in live:
                ids[(st, r)] = k
                k += 1
        place.append(ids)
        keep.append(kept)

    def begin(a, st):
        b = orders[a][st]
        out = []
        for r in keep[a][st]:
            far_r = r ^ b
            src = grads[a].at[flip(dp, far_r)] if st == 0 else slots.at[a, place[a][(st - 1, far_r)]]
            out.append(s.start(src, slots.at[a, place[a][(st, r)]], "dp", flip(dp, b)))
        return out

    def finish(a, st, copies):
        for copy in copies:
            copy.wait_recv()
        for r in keep[a][st]:
            k = place[a][(st, r)]
            if st == 0:
                chunk = flip(dp, r)
                other = lambda cut: products[a, chunk, cut, :]
            else:
                old = place[a][(st - 1, r)]
                other = lambda cut: slots[a, old, cut, :]
            if st == stages - 1 and a < 2:
                out = (upo, downo)[a]
                def write(cut, v):
                    out[cut, :] = v
            else:
                def write(cut, v):
                    slots[a, k, cut, :] = v.astype(BF)
            add_rows(rows, lambda cut: slots[a, k, cut, :], other, write)

    late = []
    run = {}
    for d in range(1, half):
        to_dev = flip(ex, d)
        late.append(s.start(lay.at[d - 1], layo.at[d - 1], "expert", to_dev))
        late.append(s.start(bak.at[d - 1], bako.at[d - 1], "expert", to_dev))
        late.append(s.start(dots.at[d - 1], dotso.at[d - 1], "expert", to_dev))
    for a in (2, 3):
        multiply(a)
        run[a] = begin(a, 0)
    swaps = []
    for st in range(stages):
        for a in (2, 3):
            finish(a, st, run[a])
            if st + 1 < stages:
                run[a] = begin(a, st + 1)
            else:
                k = place[a][(st, 0)]
                swaps.append(s.start(slots.at[a, k], far.at[a - 2], "expert", flip(ex, half)))
        for a in (0, 1):
            if st == 0:
                multiply(a)
                run[a] = begin(a, 0)
            else:
                finish(a, st - 1, run[a])
                run[a] = begin(a, st)
    for a in (0, 1):
        finish(a, stages - 1, run[a])
    for a, out in ((0, upo), (1, downo)):
        swaps[a].wait_recv()

        def write(cut, v, out=out):
            out[cut, :] = v

        add_rows(rows, lambda cut: out[cut, :], lambda cut: far[a, cut, :], write)
    for copy in late:
        copy.wait_recv()
    s.drain()


def give_back(n, parts, factors, lay, bak, dots):
    half = n // 2
    same = lambda v: jax.ShapeDtypeStruct(v.shape, v.dtype)
    rows, cols = factors[0].shape[1] // parts, factors[1].shape[1]
    copies = 4 * (parts - 1) + 2 + 3 * (half - 1)
    anywhere = pl.BlockSpec(memory_space=pl.ANY)
    vmem = pl.BlockSpec(memory_space=pltpu.VMEM)
    shard = jax.ShapeDtypeStruct((rows, cols), F32)
    return pl.pallas_call(
        partial(return_kernel, n, parts),
        out_shape=(shard, shard, same(lay), same(bak), same(dots)),
        in_specs=[vmem] * 7 + [anywhere] * 3,
        out_specs=[vmem] * 2 + [anywhere] * 3,
        scratch_shapes=[
            pltpu.VMEM((4, parts, rows, cols), BF),
            pltpu.VMEM((4, parts - 1, rows, cols), BF),
            pltpu.VMEM((2, rows, cols), BF),
            pltpu.SemaphoreType.DMA((copies,)),
            pltpu.SemaphoreType.DMA((copies,)),
        ],
        compiler_params=pltpu.CompilerParams(
            collective_id=1, has_side_effects=True, vmem_limit_bytes=50 * 2**20
        ),
        name="give_back",
    )(*factors, lay, bak, dots)


def local_wide(tokens, cotangent, routes, gate_probs, w_up, w_down, decay_rate):
    rows, width = tokens.shape
    n = lax.axis_size("expert")
    parts = lax.axis_size("dp")
    half = n // 2
    me = lax.axis_index("expert")
    w_up, w_down, decay = w_up[0], w_down[0], decay_rate[0]
    hidden = w_up.shape[1]
    ids = jnp.arange(n, dtype=jnp.int32)
    hit = routes[None, :, :] == ids[:, None, None]
    table = jnp.sum(jnp.where(hit, gate_probs[None, :, :], 0.0), axis=2)
    x_far, cot_far, tab_far, w_up2, w_down2, decay2 = dispatch(
        n, parts, tokens, cotangent, table,
        w_up.reshape(parts, width // parts, hidden),
        w_down.reshape(parts, hidden // parts, width),
        decay[None],
    )
    w_up2 = w_up2.reshape(width, hidden)
    w_down2 = w_down2.reshape(hidden, width)
    decay2 = decay2[0]
    x_all = jnp.concatenate([tokens, x_far.reshape(-1, width)], axis=0)
    cot_all = jnp.concatenate([cotangent, cot_far.reshape(-1, width)], axis=0)
    tabs = jnp.concatenate([table[None], tab_far], axis=0)
    other = me ^ half

    def gate_of(expert):
        pick = (ids == expert)[None, :, None]
        return jnp.sum(jnp.where(pick, tabs, 0.0), axis=1).reshape(-1)

    layer1, dots1, back1, rates1, scaled1, cg1 = expert_block(
        x_all, cot_all, gate_of(me), w_up, w_down, decay
    )
    layer2, dots2, back2, rates2, scaled2, cg2 = expert_block(
        x_all, cot_all, gate_of(other), w_up2, w_down2, decay2
    )
    factors = (x_all, cg1, scaled1, rates1, cg2, scaled2, rates2)
    layer = (layer1 + layer2).reshape(half, rows, width)
    back = (back1 + back2).reshape(half, rows, width)
    dots = jnp.where((ids == me)[None, :, None], dots1.reshape(half, 1, rows), 0.0) + jnp.where(
        (ids == other)[None, :, None], dots2.reshape(half, 1, rows), 0.0
    )
    up_grad, down_grad, layer_far, back_far, dots_far = give_back(
        n, parts, factors, layer[1:].astype(BF), back[1:].astype(BF), dots[1:]
    )
    layer_out = layer[0] + jnp.sum(layer_far.astype(F32), axis=0)
    token_grad = back[0] + jnp.sum(back_far.astype(F32), axis=0)
    own = dots[0] + jnp.sum(dots_far, axis=0)
    gate_grad = jnp.sum(jnp.where(hit, own[:, :, None], 0.0), axis=0)
    return (layer_out.astype(BF), token_grad.astype(BF), gate_grad, up_grad[None], down_grad.T[None])


def lif(current, decay):
    two = current + current
    k = decay + (two - 2.0)
    a = two - 2.0
    dv = None
    for step in range(STEPS):
        if step > 0:
            a = decay * q + k
        t = jnp.tanh(a)
        q = a - t
        t2 = t * t
        if step == 0:
            e = t2
            total, slope = t, 1.0 - t2
        else:
            dv = decay * e + 1.0
            e = t2 * dv
            total, slope = total + t, slope + (dv - e)
    return 0.5 + (0.5 / STEPS) * total, (1.0 / STEPS) * slope


def fused_kernel(x, c, rt, gp, wu, wd, dec,
                 lay_out, tok_out, gg_out, upo, dno,
                 layv, tokv, upv, dnv, dnt, xall, call, wub, wdb, decf, tab_s, tab_r, dot_s, dot_r, gcol, dacc, s_cur, s_u,
                 gr, cg, lo, bo, ls, bs, lr, br, products, slots, far, lsem, send, recv):
    ex, dp = lax.axis_index("expert"), lax.axis_index("dp")
    pair, mate = flip(ex, 1), flip(ex, 2)
    rows, width = x.shape
    hidden = wu.shape[1]
    blk = rows // 2
    s = Sender(send, recv)

    loads = [
        pltpu.make_async_copy(x, xall.at[pl.ds(0, rows)], lsem.at[0]),
        pltpu.make_async_copy(wu, wub.at[0], lsem.at[1]),
        pltpu.make_async_copy(c, call.at[pl.ds(0, rows)], lsem.at[2]),
        pltpu.make_async_copy(wd, wdb.at[pl.ds(0, hidden)], lsem.at[3]),
    ]
    for copy in loads:
        copy.start()

    def gate_row(expert):
        return jnp.where(rt[0:1, :] == expert, gp[0:1, :], 0.0) + jnp.where(rt[1:2, :] == expert, gp[1:2, :], 0.0)

    tab_s[...] = jnp.zeros_like(tab_s)
    tab_s[0:1, :] = gate_row(pair)
    tab_s[1:2, :] = gate_row(flip(pair, 2))

    barrier = pltpu.get_barrier_semaphore()
    for axis, dev in (("expert", pair), ("expert", mate), ("dp", flip(dp, 1)), ("dp", flip(dp, 2)), ("dp", flip(dp, 4))):
        pl.semaphore_signal(barrier, inc=1, device_id={axis: dev}, device_id_type=pl.DeviceIdType.MESH)
    pl.semaphore_wait(barrier, 5)

    up_rows, dn_rows = width // 8, hidden // 8
    def up_cut(chunk, part):
        return pl.ds(pl.multiple_of(chunk * up_rows + part * (up_rows // 2), 16), up_rows // 2)

    def dn_cut(chunk, part, base=0):
        return pl.ds(pl.multiple_of(base + chunk * dn_rows + part * (dn_rows // 2), 16), dn_rows // 2)

    def send_weights(part):
        return [
            s.start(wu.at[up_cut(dp, part)], wub.at[1, up_cut(dp, part)], "expert", mate),
            s.start(wd.at[dn_cut(dp, part)], wdb.at[dn_cut(dp, part, hidden)], "expert", mate),
        ]

    def send_tokens(b):
        cut = pl.ds(b * blk, blk)
        there = pl.ds(rows + b * blk, blk)
        return [
            s.start(x.at[cut], xall.at[there], "expert", pair),
            s.start(c.at[cut], call.at[there], "expert", pair),
        ]

    first = s.start(dec, decf, "expert", mate)
    w_in = [send_weights(0), None]
    tab_in = s.start(tab_s, tab_r, "expert", pair)
    t_in = [send_tokens(0), None]

    def set_gates(slot, e, row):
        gcol[e, slot * rows:(slot + 1) * rows, :] = jnp.transpose(jnp.broadcast_to(row, (128, rows)))

    set_gates(0, 0, gate_row(ex))
    set_gates(0, 1, gate_row(mate))

    def half_pass(e, row0, m):
        @pl.loop(0, hidden // 256)
        def _(i):
            cols = pl.ds(pl.multiple_of(i * 256, 256), 256)
            far_cols = pl.ds(pl.multiple_of(e * hidden + i * 256, 256), 256)
            s_cur[0:m, cols] = mm(xall[row0:row0 + m, :], wub[e, :, cols], ((1,), (0,)))
            s_u[0:m, cols] = mm(call[row0:row0 + m, :], wdb[far_cols, :], ((1,), (1,)))

        d_ref = decf if e else dec

        @pl.loop(0, m // 16)
        def _(i):
            here = pl.ds(pl.multiple_of(i * 16, 16), 16)
            there = pl.ds(pl.multiple_of(row0 + i * 16, 16), 16)
            gate = gcol[e, there, :]
            dots = None
            for j in range(hidden // 128):
                cols = slice(j * 128, (j + 1) * 128)
                u = s_u[here, cols]
                rate, slope = lif(s_cur[here, cols], d_ref[0:1, cols])
                out = slice(e * hidden + j * 128, e * hidden + (j + 1) * 128)
                gr[there, out] = (gate * rate).astype(BF)
                cg[there, out] = (gate * u * slope).astype(BF)
                dots = rate * u if dots is None else dots + rate * u
            dacc[e, there, :] = dots

    def out_pass(row0, m, write):
        @pl.loop(0, width // 512)
        def _(i):
            cols = pl.ds(pl.multiple_of(i * 512, 512), 512)
            write(cols, mm(gr[row0:row0 + m, :], wdb[:, cols], ((1,), (0,))),
                  mm(cg[row0:row0 + m, 0:hidden], wub[0, cols, :], ((1,), (1,)))
                  + mm(cg[row0:row0 + m, hidden:2 * hidden], wub[1, cols, :], ((1,), (1,))))

    for copy in loads:
        copy.wait()
    half_pass(0, 0, rows)

    orders = ((4, 2), (2, 4))

    def forward(a, part, r, axes):
        chunk = flip(dp, r)
        ref = wub.at[1, up_cut(chunk, part)] if a == 0 else wdb.at[dn_cut(chunk, part, hidden)]
        return [s.start(ref, ref, "dp", flip(dp, b)) for b in axes]

    ring = {}

    def gather_first(part):
        for a in (0, 1):
            w_in[part][a].wait_recv()
            b1, b2 = orders[a]
            ring[a, part] = [forward(a, part, 0, (b1, b2, 1))]

    def gather_second(part):
        for a in (0, 1):
            b1, b2 = orders[a]
            ring[a, part][0][0].wait_recv()
            ring[a, part].append(forward(a, part, b1, (b2, 1)))

    def gather_third(part):
        for a in (0, 1):
            b1, b2 = orders[a]
            ring[a, part][0][1].wait_recv()
            ring[a, part].append(forward(a, part, b2, (1,)))
            ring[a, part][1][0].wait_recv()
            ring[a, part].append(forward(a, part, b1 | b2, (1,)))

    def gather_last(part):
        for a in (0, 1):
            for group in ring[a, part]:
                group[-1].wait_recv()

    for copy in w_in[0]:
        s.sent(copy)
    w_in[1] = send_weights(1)
    gather_first(0)
    gather_second(0)
    gather_first(1)
    t_in[1] = send_tokens(1)
    gather_third(0)
    gather_second(1)
    tab_in.wait_recv()
    set_gates(1, 0, tab_r[0:1, :])
    set_gates(1, 1, tab_r[1:2, :])
    for copy in t_in[0]:
        copy.wait_recv()
    half_pass(0, rows, blk)
    gather_third(1)
    first.wait_recv()
    gather_last(0)
    gather_last(1)
    half_pass(1, 0, rows + blk)

    def keep(cols, lay, back):
        lo[:, cols] = lay
        bo[:, cols] = back

    def leave(b):
        def write(cols, lay, back):
            ls[b * blk:(b + 1) * blk, cols] = lay.astype(BF)
            bs[b * blk:(b + 1) * blk, cols] = back.astype(BF)
        out_pass(rows + b * blk, blk, write)

    def send_back(b):
        cut = pl.ds(b * blk, blk)
        return [
            s.start(ls.at[cut], lr.at[cut], "expert", pair),
            s.start(bs.at[cut], br.at[cut], "expert", pair),
        ]

    leave(0)
    for copy in t_in[1]:
        copy.wait_recv()
    back_in = [send_back(0), None]
    half_pass(1, rows + blk, blk)

    tile = up_rows
    lefts = (xall, call, xall, call)
    part_rows = tile // 2
    parts = (pl.ds(0, part_rows), pl.ds(part_rows, part_rows))
    axes = ((2, 4), (4, 2))
    run = {}

    def product(a, r):
        cols = pl.ds(pl.multiple_of(flip_by(dp, r) * tile, tile), tile)
        right = gr if a % 2 else cg
        e = a // 2
        products[a, r] = mm(lefts[a][:, cols], right[:, e * hidden:(e + 1) * hidden], ((0,), (0,))).astype(BF)

    def multiply_far(a):
        base = s.count
        s.count += 4

        def copy_of(i, r):
            return pltpu.make_async_remote_copy(
                src_ref=products.at[a, r], dst_ref=slots.at[a, r // 2], send_sem=send.at[base + i],
                recv_sem=recv.at[base + i], device_id={"dp": flip(dp, 1)}, device_id_type=pl.DeviceIdType.MESH,
            )

        @pl.loop(0, 4)
        def _(i):
            r = 7 - 4 * (i % 2) - 2 * (i // 2)
            product(a, r)
            copy_of(i, r).start()

        for i in range(4):
            r = 7 - 4 * (i % 2) - 2 * (i // 2)
            copy = copy_of(i, r)
            s.all.append(copy)
            run[a, r - 1] = copy

    def multiply_near(a):
        @pl.loop(0, 4)
        def _(i):
            product(a, 6 - 4 * (i % 2) - 2 * (i // 2))

    def add_part(off, n, read_a, read_b, write):
        @pl.loop(0, n // 32)
        def _(i):
            cut = pl.ds(pl.multiple_of(off + i * 32, 32), 32)
            write(cut, read_a(cut).astype(F32) + read_b(cut).astype(F32))

    def total(a, k, off, n, other):
        def store(cut, v):
            slots[a, k, cut, :] = v.astype(BF)
        add_part(off, n, lambda cut: slots[a, k, cut, :], other, store)

    def near_sum(a, r):
        run[a, r].wait_recv()
        total(a, r // 2, 0, tile, lambda cut: products[a, r, cut, :])

    def stage0(a):
        for r in (6, 2, 4):
            near_sum(a, r)
            for h in (0, 1):
                b1 = axes[h][0]
                if r & b1:
                    far_r = r ^ b1
                    run[a, h, 1, far_r] = s.start(
                        slots.at[a, r // 2, parts[h]], slots.at[a, 4 + (far_r != 0), parts[h]], "dp", flip(dp, b1)
                    )

    def stage0_rest(a):
        near_sum(a, 0)

    def stage1(a):
        for i in (0, 1):
            for h in (0, 1):
                b2 = axes[h][1]
                r = 0 if i else b2
                run[a, h, 1, r].wait_recv()
                total(a, 4 + (r != 0), h * part_rows, part_rows, lambda cut: slots[a, r // 2, cut, :])
                if r:
                    run[a, h, 2] = s.start(slots.at[a, 5, parts[h]], slots.at[a, 6, parts[h]], "dp", flip(dp, b2))

    def stage2(a):
        for h in (0, 1):
            run[a, h, 2].wait_recv()
            if a < 2:
                out = (upv, dnv)[a]

                def write(cut, v):
                    out[cut, :] = v

                add_part(h * part_rows, part_rows, lambda cut: slots[a, 6, cut, :], lambda cut: slots[a, 4, cut, :], write)
            else:
                total(a, 6, h * part_rows, part_rows, lambda cut: slots[a, 4, cut, :])
                run[a, h, 3] = s.start(slots.at[a, 6, parts[h]], far.at[a - 2, parts[h]], "expert", mate)

    multiply_far(2)
    multiply_near(2)
    multiply_far(3)
    stage0(2)
    multiply_near(3)
    stage0(3)
    half_pass(0, rows + blk, blk)
    leave(1)
    dot_s[...] = jnp.zeros_like(dot_s)
    for e in (0, 1):
        dot_s[e:e + 1, :] = jnp.sum(jnp.transpose(dacc[e, rows:2 * rows, :]), axis=0, keepdims=True)
    back_in[1] = send_back(1)
    dots_in = s.start(dot_s, dot_r, "expert", pair)
    stage0_rest(2)
    stage0_rest(3)
    stage1(2)
    multiply_far(0)
    multiply_near(0)
    stage1(3)
    stage0(0)
    multiply_far(1)
    multiply_near(1)
    stage2(2)
    stage2(3)
    stage0(1)
    out_pass(0, rows, keep)
    stage0_rest(0)
    stage0_rest(1)
    stores = []

    def store_out(k, src, dst):
        copy = pltpu.make_async_copy(src, dst, lsem.at[4 + k])
        copy.start()
        stores.append(copy)

    def finish_rows(b):
        for copy in back_in[b]:
            copy.wait_recv()

        @pl.loop(0, blk // 16)
        def _(i):
            cut = pl.ds(pl.multiple_of(b * blk + i * 16, 16), 16)
            layv[cut, :] = (lo[cut, :] + lr[cut, :].astype(F32)).astype(BF)
            tokv[cut, :] = (bo[cut, :] + br[cut, :].astype(F32)).astype(BF)

        cut = pl.ds(b * blk, blk)
        store_out(2 * b, layv.at[cut], lay_out.at[cut])
        store_out(2 * b + 1, tokv.at[cut], tok_out.at[cut])

    own = [jnp.sum(jnp.transpose(dacc[e, 0:rows, :]), axis=0, keepdims=True) for e in (0, 1)]
    stage1(0)
    finish_rows(0)
    stage1(1)
    finish_rows(1)
    dots_in.wait_recv()
    for k in (0, 1):
        chosen = rt[k:k + 1, :]
        acc = jnp.zeros((1, rows), F32)
        for expert, d in ((ex, own[0]), (mate, own[1]), (pair, dot_r[0:1, :]), (flip(pair, 2), dot_r[1:2, :])):
            acc = acc + jnp.where(chosen == expert, d, 0.0)
        gg_out[k:k + 1, :] = acc
    stage2(0)
    stage2(1)
    for h in (0, 1):
        run[2, h, 3].wait_recv()

        def write(cut, v):
            upv[cut, :] = v

        add_part(h * part_rows, part_rows, lambda cut: upv[cut, :], lambda cut: far[0, cut, :], write)
        store_out(4 + h, upv.at[parts[h]], upo.at[parts[h]])
    for h in (0, 1):
        run[3, h, 3].wait_recv()
        here = slice(h * part_rows, (h + 1) * part_rows)

        @pl.loop(0, hidden // 128)
        def _(j):
            cols = pl.ds(pl.multiple_of(j * 128, 128), 128)
            dnt[cols, here] = jnp.transpose(dnv[here, cols] + far[1, here, cols].astype(F32))

    store_out(6, dnt, dno)
    s.drain()
    for copy in stores:
        copy.wait()


def move_kernel(*refs):
    n = (len(refs) - 2) // 3
    load, store = refs[-2:]
    pieces = []
    for i in range(n):
        count = refs[i].shape[0]
        cuts = 2 if count % 64 == 0 else 1
        for k in range(cuts):
            pieces.append((refs[i], refs[2 * n + i], refs[n + i], pl.ds(k * (count // cuts), count // cuts)))
    ins = [pltpu.make_async_copy(a.at[cut], b.at[cut], load.at[j]) for j, (a, b, _, cut) in enumerate(pieces)]
    outs = [pltpu.make_async_copy(b.at[cut], c.at[cut], store.at[j]) for j, (_, b, c, cut) in enumerate(pieces)]
    for copy in ins:
        copy.start()
    for before, after in zip(ins, outs):
        before.wait()
        after.start()
    for copy in outs:
        copy.wait()


def flip_by(pos, mask):
    out = pos
    for b in (1, 2, 4):
        out = out + b * ((mask // b) % 2) * (1 - 2 * ((pos // b) % 2))
    return out


def local_fused(tokens, cotangent, routes, gate_probs, w_up, w_down, decay_rate):
    rows, width = tokens.shape
    hidden = w_up.shape[2]
    tile = width // 8
    sds = jax.ShapeDtypeStruct
    copies = 1 + 4 + 1 + 4 + 4 * 7 + 6 + 4 * 7 - 2 + 4
    copies = copies + 40
    anywhere = pl.BlockSpec(memory_space=pl.ANY)
    vmem = pl.BlockSpec(memory_space=pltpu.VMEM)
    results = pl.pallas_call(
        fused_kernel,
        out_shape=(
            sds((rows, width), BF), sds((rows, width), BF), sds((2, rows), F32),
            sds((tile, hidden), F32), sds((hidden, tile), F32),
        ),
        in_specs=[anywhere, anywhere, vmem, vmem, anywhere, anywhere, vmem],
        out_specs=[anywhere, anywhere, vmem, anywhere, anywhere],
        scratch_shapes=[
            pltpu.VMEM((rows, width), BF),
            pltpu.VMEM((rows, width), BF),
            pltpu.VMEM((tile, hidden), F32),
            pltpu.VMEM((tile, hidden), F32),
            pltpu.VMEM((hidden, tile), F32),
            pltpu.VMEM((2 * rows, width), BF),
            pltpu.VMEM((2 * rows, width), BF),
            pltpu.VMEM((2, width, hidden), BF),
            pltpu.VMEM((2 * hidden, width), BF),
            pltpu.VMEM((1, hidden), F32),
            pltpu.VMEM((8, rows), F32),
            pltpu.VMEM((8, rows), F32),
            pltpu.VMEM((8, rows), F32),
            pltpu.VMEM((8, rows), F32),
            pltpu.VMEM((2, 2 * rows, 128), F32),
            pltpu.VMEM((2, 2 * rows, 128), F32),
            pltpu.VMEM((3 * rows // 2, hidden), F32),
            pltpu.VMEM((3 * rows // 2, hidden), F32),
            pltpu.VMEM((2 * rows, 2 * hidden), BF),
            pltpu.VMEM((2 * rows, 2 * hidden), BF),
            pltpu.VMEM((rows, width), F32),
            pltpu.VMEM((rows, width), F32),
            pltpu.VMEM((rows, width), BF),
            pltpu.VMEM((rows, width), BF),
            pltpu.VMEM((rows, width), BF),
            pltpu.VMEM((rows, width), BF),
            pltpu.VMEM((4, 8, tile, hidden), BF),
            pltpu.VMEM((4, 7, tile, hidden), BF),
            pltpu.VMEM((2, tile, hidden), BF),
            pltpu.SemaphoreType.DMA((11,)),
            pltpu.SemaphoreType.DMA((copies,)),
            pltpu.SemaphoreType.DMA((copies,)),
        ],
        compiler_params=pltpu.CompilerParams(
            collective_id=2, has_side_effects=True, vmem_limit_bytes=60 * 2**20
        ),
        name="layer",
    )(tokens, cotangent, routes.T, gate_probs.T, w_up[0], w_down[0], decay_rate)
    layer_out, token_grad, gate_grad, up_grad, down_grad = pl.pallas_call(
        move_kernel,
        out_shape=[sds(v.shape, v.dtype) for v in results],
        in_specs=[anywhere] * 5,
        out_specs=[anywhere] * 5,
        scratch_shapes=[pltpu.VMEM(v.shape, v.dtype) for v in results] + [pltpu.SemaphoreType.DMA((10,))] * 2,
        name="move",
    )(*results)
    return layer_out, token_grad, gate_grad.T, up_grad[None], down_grad[None]


def solution(mesh):
    rows = P(("dp", "expert"), None)
    local = local_fused if mesh.shape["expert"] == 4 and mesh.shape["dp"] == 8 else local_wide
    return jax.shard_map(
        local,
        mesh=mesh,
        in_specs=(rows, rows, rows, rows, P("expert", None, None), P("expert", None, None), P("expert", None)),
        out_specs=(rows, rows, rows, P("expert", "dp", None), P("expert", None, "dp")),
        check_vma=False,
    )
```

```python
from functools import partial

import jax
import jax.numpy as jnp
from jax import lax
from jax.experimental import pallas as pl
from jax.experimental.pallas import tpu as pltpu
from jax.sharding import PartitionSpec as P

STEPS = 4
SHARP = 4.0

BF = jnp.bfloat16
F32 = jnp.float32


def rate_and_slope(current, decay):
    v = jnp.zeros_like(current)
    dv = jnp.zeros_like(current)
    total = jnp.zeros_like(current)
    slope = jnp.zeros_like(current)
    for _ in range(STEPS):
        v = decay * v + current
        dv = decay * dv + 1.0
        s = jax.nn.sigmoid(SHARP * (v - 1.0))
        ds = SHARP * s * (1.0 - s) * dv
        v = v - s
        dv = dv - ds
        total = total + s
        slope = slope + ds
    return total / STEPS, slope / STEPS


def mm(a, b, dims):
    return lax.dot_general(a, b, (dims, ((), ())), preferred_element_type=F32)


def expert_block(x, cot, gate, w_up, w_down, decay):
    rates, slope = rate_and_slope(mm(x, w_up, ((1,), (0,))), decay)
    rates = rates.astype(BF)
    cot32 = cot.astype(F32)
    scaled = (gate[:, None] * cot32).astype(BF)
    out = mm(rates, w_down, ((1,), (0,))).astype(BF).astype(F32)
    layer = gate[:, None] * out
    dots = jnp.sum(cot32 * out, axis=1)
    rate_grad = mm(scaled, w_down, ((1,), (1,)))
    current_grad = (rate_grad * slope).astype(BF)
    back = mm(current_grad, w_up, ((1,), (1,))).astype(BF).astype(F32)
    return layer, dots, back, rates, scaled, current_grad


def flip(pos, mask):
    for k in range(mask.bit_length()):
        b = 1 << k
        if mask & b:
            pos = pos + b * (1 - 2 * ((pos // b) % 2))
    return pos


def bit_orders(parts):
    bits = [1 << k for k in range(parts.bit_length() - 1)]
    rest = bits[1:]
    cut = len(rest) // 2
    return bits[:1] + rest[:cut] + rest[cut:], bits[:1] + rest[cut:] + rest[:cut]


def greet(n, parts):
    ex, dp = lax.axis_index("expert"), lax.axis_index("dp")
    barrier = pltpu.get_barrier_semaphore()
    masks = list(range(1, n // 2 + 1))
    for d in masks:
        pl.semaphore_signal(barrier, inc=1, device_id={"expert": flip(ex, d)}, device_id_type=pl.DeviceIdType.MESH)
    bits = bit_orders(parts)[0]
    for b in bits:
        pl.semaphore_signal(barrier, inc=1, device_id={"dp": flip(dp, b)}, device_id_type=pl.DeviceIdType.MESH)
    pl.semaphore_wait(barrier, len(masks) + len(bits))
    return ex, dp


class Sender:
    def __init__(self, send, recv):
        self.send, self.recv, self.count, self.all = send, recv, 0, []

    def start(self, src, dst, axis, target):
        k = self.count
        self.count += 1
        copy = pltpu.make_async_remote_copy(
            src_ref=src, dst_ref=dst, send_sem=self.send.at[k], recv_sem=self.recv.at[k],
            device_id={axis: target}, device_id_type=pl.DeviceIdType.MESH,
        )
        copy.start()
        self.all.append(copy)
        return copy

    def sent(self, copy):
        copy.wait_send()
        self.all = [other for other in self.all if other is not copy]

    def drain(self):
        for copy in self.all:
            copy.wait_send()


def dispatch_kernel(n, parts, x, c, t, up, down, dec, xo, co, to, upo, downo, deco, send, recv):
    ex, dp = greet(n, parts)
    half = n // 2
    s = Sender(send, recv)
    mate = flip(ex, half)
    first_up = s.start(up.at[dp], upo.at[dp], "expert", mate)
    first_down = s.start(down.at[dp], downo.at[dp], "expert", mate)
    late = [s.start(dec, deco, "expert", mate)]
    for d in range(1, half):
        to_dev = flip(ex, d)
        late.append(s.start(t, to.at[d - 1], "expert", to_dev))
        late.append(s.start(x, xo.at[d - 1], "expert", to_dev))
        late.append(s.start(c, co.at[d - 1], "expert", to_dev))
    orders = [o[::-1] for o in bit_orders(parts)]
    waiting = [[first_up], [first_down]]
    held = [[0], [0]]
    for stage in range(len(orders[0])):
        for a, buf in ((0, upo), (1, downo)):
            for copy in waiting[a]:
                copy.wait_recv()
            b = orders[a][stage]
            waiting[a] = []
            for r in held[a]:
                place = flip(dp, r)
                waiting[a].append(s.start(buf.at[place], buf.at[place], "dp", flip(dp, b)))
            held[a] = held[a] + [r ^ b for r in held[a]]
    for copy in waiting[0] + waiting[1] + late:
        copy.wait_recv()
    s.drain()


def dispatch(n, parts, x, c, t, up, down, dec):
    half = n // 2
    stack = lambda v: jax.ShapeDtypeStruct((half - 1,) + v.shape, v.dtype)
    same = lambda v: jax.ShapeDtypeStruct(v.shape, v.dtype)
    copies = 3 + 3 * (half - 1) + 2 * (parts - 1)
    anywhere = pl.BlockSpec(memory_space=pl.ANY)
    return pl.pallas_call(
        partial(dispatch_kernel, n, parts),
        out_shape=(stack(x), stack(c), stack(t), same(up), same(down), same(dec)),
        in_specs=[anywhere] * 6,
        out_specs=[anywhere] * 6,
        scratch_shapes=[pltpu.SemaphoreType.DMA((copies,)), pltpu.SemaphoreType.DMA((copies,))],
        compiler_params=pltpu.CompilerParams(collective_id=0, has_side_effects=True),
        name="dispatch",
    )(x, c, t, up, down, dec)


def add_rows(rows, read_a, read_b, write):
    step = 32 if rows % 32 == 0 else rows

    @pl.loop(0, rows // step)
    def _(i):
        cut = pl.ds(pl.multiple_of(i * step, step), step)
        write(cut, read_a(cut).astype(F32) + read_b(cut).astype(F32))


def return_kernel(n, parts, x, cg1, sc1, rt1, cg2, sc2, rt2, lay, bak, dots, upo, downo, layo, bako,
                  dotso, products, slots, far, send, recv):
    ex, dp = greet(n, parts)
    half = n // 2
    s = Sender(send, recv)
    rows = slots.shape[2]
    grads = [products.at[a] for a in range(4)]
    pairs = ((x, cg1), (sc1, rt1), (x, cg2), (sc2, rt2))
    tile = 256
    per = tile // rows

    def multiply(a):
        left, right = pairs[a]

        @pl.loop(0, left.shape[1] // tile)
        def _(i):
            cols = pl.ds(pl.multiple_of(i * tile, tile), tile)
            res = mm(left[:, cols], right[...], ((0,), (0,))).astype(BF)
            for k in range(per):
                products[a, i * per + k] = res[k * rows:(k + 1) * rows]

    orders = bit_orders(parts)
    orders = (orders[0], orders[1], orders[0], orders[1])
    stages = len(orders[0])
    place, keep = [], []
    for a in range(4):
        ids, kept, live, k = {}, [], list(range(parts)), 0
        for st in range(stages):
            live = [r for r in live if not r & orders[a][st]]
            kept.append(live)
            for r in live:
                ids[(st, r)] = k
                k += 1
        place.append(ids)
        keep.append(kept)

    def begin(a, st):
        b = orders[a][st]
        out = []
        for r in keep[a][st]:
            far_r = r ^ b
            src = grads[a].at[flip(dp, far_r)] if st == 0 else slots.at[a, place[a][(st - 1, far_r)]]
            out.append(s.start(src, slots.at[a, place[a][(st, r)]], "dp", flip(dp, b)))
        return out

    def finish(a, st, copies):
        for copy in copies:
            copy.wait_recv()
        for r in keep[a][st]:
            k = place[a][(st, r)]
            if st == 0:
                chunk = flip(dp, r)
                other = lambda cut: products[a, chunk, cut, :]
            else:
                old = place[a][(st - 1, r)]
                other = lambda cut: slots[a, old, cut, :]
            if st == stages - 1 and a < 2:
                out = (upo, downo)[a]
                def write(cut, v):
                    out[cut, :] = v
            else:
                def write(cut, v):
                    slots[a, k, cut, :] = v.astype(BF)
            add_rows(rows, lambda cut: slots[a, k, cut, :], other, write)

    late = []
    run = {}
    for d in range(1, half):
        to_dev = flip(ex, d)
        late.append(s.start(lay.at[d - 1], layo.at[d - 1], "expert", to_dev))
        late.append(s.start(bak.at[d - 1], bako.at[d - 1], "expert", to_dev))
        late.append(s.start(dots.at[d - 1], dotso.at[d - 1], "expert", to_dev))
    for a in (2, 3):
        multiply(a)
        run[a] = begin(a, 0)
    swaps = []
    for st in range(stages):
        for a in (2, 3):
            finish(a, st, run[a])
            if st + 1 < stages:
                run[a] = begin(a, st + 1)
            else:
                k = place[a][(st, 0)]
                swaps.append(s.start(slots.at[a, k], far.at[a - 2], "expert", flip(ex, half)))
        for a in (0, 1):
            if st == 0:
                multiply(a)
                run[a] = begin(a, 0)
            else:
                finish(a, st - 1, run[a])
                run[a] = begin(a, st)
    for a in (0, 1):
        finish(a, stages - 1, run[a])
    for a, out in ((0, upo), (1, downo)):
        swaps[a].wait_recv()

        def write(cut, v, out=out):
            out[cut, :] = v

        add_rows(rows, lambda cut: out[cut, :], lambda cut: far[a, cut, :], write)
    for copy in late:
        copy.wait_recv()
    s.drain()


def give_back(n, parts, factors, lay, bak, dots):
    half = n // 2
    same = lambda v: jax.ShapeDtypeStruct(v.shape, v.dtype)
    rows, cols = factors[0].shape[1] // parts, factors[1].shape[1]
    copies = 4 * (parts - 1) + 2 + 3 * (half - 1)
    anywhere = pl.BlockSpec(memory_space=pl.ANY)
    vmem = pl.BlockSpec(memory_space=pltpu.VMEM)
    shard = jax.ShapeDtypeStruct((rows, cols), F32)
    return pl.pallas_call(
        partial(return_kernel, n, parts),
        out_shape=(shard, shard, same(lay), same(bak), same(dots)),
        in_specs=[vmem] * 7 + [anywhere] * 3,
        out_specs=[vmem] * 2 + [anywhere] * 3,
        scratch_shapes=[
            pltpu.VMEM((4, parts, rows, cols), BF),
            pltpu.VMEM((4, parts - 1, rows, cols), BF),
            pltpu.VMEM((2, rows, cols), BF),
            pltpu.SemaphoreType.DMA((copies,)),
            pltpu.SemaphoreType.DMA((copies,)),
        ],
        compiler_params=pltpu.CompilerParams(
            collective_id=1, has_side_effects=True, vmem_limit_bytes=50 * 2**20
        ),
        name="give_back",
    )(*factors, lay, bak, dots)


def local_wide(tokens, cotangent, routes, gate_probs, w_up, w_down, decay_rate):
    rows, width = tokens.shape
    n = lax.axis_size("expert")
    parts = lax.axis_size("dp")
    half = n // 2
    me = lax.axis_index("expert")
    w_up, w_down, decay = w_up[0], w_down[0], decay_rate[0]
    hidden = w_up.shape[1]
    ids = jnp.arange(n, dtype=jnp.int32)
    hit = routes[None, :, :] == ids[:, None, None]
    table = jnp.sum(jnp.where(hit, gate_probs[None, :, :], 0.0), axis=2)
    x_far, cot_far, tab_far, w_up2, w_down2, decay2 = dispatch(
        n, parts, tokens, cotangent, table,
        w_up.reshape(parts, width // parts, hidden),
        w_down.reshape(parts, hidden // parts, width),
        decay[None],
    )
    w_up2 = w_up2.reshape(width, hidden)
    w_down2 = w_down2.reshape(hidden, width)
    decay2 = decay2[0]
    x_all = jnp.concatenate([tokens, x_far.reshape(-1, width)], axis=0)
    cot_all = jnp.concatenate([cotangent, cot_far.reshape(-1, width)], axis=0)
    tabs = jnp.concatenate([table[None], tab_far], axis=0)
    other = me ^ half

    def gate_of(expert):
        pick = (ids == expert)[None, :, None]
        return jnp.sum(jnp.where(pick, tabs, 0.0), axis=1).reshape(-1)

    layer1, dots1, back1, rates1, scaled1, cg1 = expert_block(
        x_all, cot_all, gate_of(me), w_up, w_down, decay
    )
    layer2, dots2, back2, rates2, scaled2, cg2 = expert_block(
        x_all, cot_all, gate_of(other), w_up2, w_down2, decay2
    )
    factors = (x_all, cg1, scaled1, rates1, cg2, scaled2, rates2)
    layer = (layer1 + layer2).reshape(half, rows, width)
    back = (back1 + back2).reshape(half, rows, width)
    dots = jnp.where((ids == me)[None, :, None], dots1.reshape(half, 1, rows), 0.0) + jnp.where(
        (ids == other)[None, :, None], dots2.reshape(half, 1, rows), 0.0
    )
    up_grad, down_grad, layer_far, back_far, dots_far = give_back(
        n, parts, factors, layer[1:].astype(BF), back[1:].astype(BF), dots[1:]
    )
    layer_out = layer[0] + jnp.sum(layer_far.astype(F32), axis=0)
    token_grad = back[0] + jnp.sum(back_far.astype(F32), axis=0)
    own = dots[0] + jnp.sum(dots_far, axis=0)
    gate_grad = jnp.sum(jnp.where(hit, own[:, :, None], 0.0), axis=0)
    return (layer_out.astype(BF), token_grad.astype(BF), gate_grad, up_grad[None], down_grad.T[None])


def lif(current, decay):
    two = current + current
    k = decay + (two - 2.0)
    a = two - 2.0
    dv = None
    for step in range(STEPS):
        if step > 0:
            a = decay * q + k
        t = jnp.tanh(a)
        q = a - t
        t2 = t * t
        if step == 0:
            e = t2
            total, slope = t, 1.0 - t2
        else:
            dv = decay * e + 1.0
            e = t2 * dv
            total, slope = total + t, slope + (dv - e)
    return 0.5 + (0.5 / STEPS) * total, (1.0 / STEPS) * slope


def fused_kernel(x, c, routes, probs, wu, wd, decay,
                 layv, tokv, gg_out, upv, dnt,
                 rt, gp, dec, dnv, xall, call, wub, wdb, decf, tab_s, tab_r, dot_s, dot_r, gcol, dacc, s_cur, s_u,
                 gr, cg, lo, bo, ls, bs, lr, br, products, slots, far, lsem, send, recv):
    ex, dp = lax.axis_index("expert"), lax.axis_index("dp")
    pair, mate = flip(ex, 1), flip(ex, 2)
    rows, width = x.shape
    hidden = wu.shape[1]
    blk = rows // 2
    s = Sender(send, recv)

    barrier = pltpu.get_barrier_semaphore()
    for axis, dev in (("expert", pair), ("expert", mate), ("dp", flip(dp, 1)), ("dp", flip(dp, 2)), ("dp", flip(dp, 4))):
        pl.semaphore_signal(barrier, inc=1, device_id={axis: dev}, device_id_type=pl.DeviceIdType.MESH)

    small = [
        pltpu.make_async_copy(routes, rt, lsem.at[4]),
        pltpu.make_async_copy(probs, gp, lsem.at[5]),
        pltpu.make_async_copy(decay, dec, lsem.at[6]),
    ]
    loads = [
        pltpu.make_async_copy(x, xall.at[pl.ds(0, rows)], lsem.at[0]),
        pltpu.make_async_copy(wu, wub.at[0], lsem.at[1]),
        pltpu.make_async_copy(c, call.at[pl.ds(0, rows)], lsem.at[2]),
        pltpu.make_async_copy(wd, wdb.at[pl.ds(0, hidden)], lsem.at[3]),
    ]
    for copy in small + loads:
        copy.start()
    pl.semaphore_wait(barrier, 5)

    up_rows, dn_rows = width // 8, hidden // 8
    def up_cut(chunk, part):
        return pl.ds(pl.multiple_of(chunk * up_rows + part * (up_rows // 2), 16), up_rows // 2)

    def dn_cut(chunk, part, base=0):
        return pl.ds(pl.multiple_of(base + chunk * dn_rows + part * (dn_rows // 2), 16), dn_rows // 2)

    def send_weights(part):
        return [
            s.start(wu.at[up_cut(dp, part)], wub.at[1, up_cut(dp, part)], "expert", mate),
            s.start(wd.at[dn_cut(dp, part)], wdb.at[dn_cut(dp, part, hidden)], "expert", mate),
        ]

    def send_tokens(b):
        cut = pl.ds(b * blk, blk)
        there = pl.ds(rows + b * blk, blk)
        return [
            s.start(x.at[cut], xall.at[there], "expert", pair),
            s.start(c.at[cut], call.at[there], "expert", pair),
        ]

    w_in = [send_weights(0), None]
    t_in = [send_tokens(0), None]
    first = s.start(decay, decf, "expert", mate)
    for copy in small:
        copy.wait()

    def gate_row(expert):
        return jnp.where(rt[0:1, :] == expert, gp[0:1, :], 0.0) + jnp.where(rt[1:2, :] == expert, gp[1:2, :], 0.0)

    tab_s[...] = jnp.zeros_like(tab_s)
    tab_s[0:1, :] = gate_row(pair)
    tab_s[1:2, :] = gate_row(flip(pair, 2))
    tab_in = s.start(tab_s, tab_r, "expert", pair)

    def set_gates(slot, e, row):
        gcol[e, slot * rows:(slot + 1) * rows, :] = jnp.transpose(jnp.broadcast_to(row, (128, rows)))

    set_gates(0, 0, gate_row(ex))
    set_gates(0, 1, gate_row(mate))

    def half_pass(e, row0, m):
        @pl.loop(0, hidden // 256)
        def _(i):
            cols = pl.ds(pl.multiple_of(i * 256, 256), 256)
            far_cols = pl.ds(pl.multiple_of(e * hidden + i * 256, 256), 256)
            s_cur[0:m, cols] = mm(xall[row0:row0 + m, :], wub[e, :, cols], ((1,), (0,)))
            s_u[0:m, cols] = mm(call[row0:row0 + m, :], wdb[far_cols, :], ((1,), (1,)))

        d_ref = decf if e else dec

        @pl.loop(0, m // 16)
        def _(i):
            here = pl.ds(pl.multiple_of(i * 16, 16), 16)
            there = pl.ds(pl.multiple_of(row0 + i * 16, 16), 16)
            gate = gcol[e, there, :]
            dots = None
            for j in range(hidden // 128):
                cols = slice(j * 128, (j + 1) * 128)
                u = s_u[here, cols]
                rate, slope = lif(s_cur[here, cols], d_ref[0:1, cols])
                out = slice(e * hidden + j * 128, e * hidden + (j + 1) * 128)
                gr[there, out] = (gate * rate).astype(BF)
                cg[there, out] = (gate * u * slope).astype(BF)
                dots = rate * u if dots is None else dots + rate * u
            dacc[e, there, :] = dots

    def out_pass(row0, m, write):
        @pl.loop(0, width // 512)
        def _(i):
            cols = pl.ds(pl.multiple_of(i * 512, 512), 512)
            write(cols, mm(gr[row0:row0 + m, :], wdb[:, cols], ((1,), (0,))),
                  mm(cg[row0:row0 + m, 0:hidden], wub[0, cols, :], ((1,), (1,)))
                  + mm(cg[row0:row0 + m, hidden:2 * hidden], wub[1, cols, :], ((1,), (1,))))

    for copy in loads:
        copy.wait()
    half_pass(0, 0, rows)

    orders = ((4, 2), (2, 4))

    def forward(a, part, r, axes):
        chunk = flip(dp, r)
        ref = wub.at[1, up_cut(chunk, part)] if a == 0 else wdb.at[dn_cut(chunk, part, hidden)]
        return [s.start(ref, ref, "dp", flip(dp, b)) for b in axes]

    ring = {}

    def gather_first(part):
        for a in (0, 1):
            w_in[part][a].wait_recv()
            b1, b2 = orders[a]
            ring[a, part] = [forward(a, part, 0, (b1, b2, 1))]

    def gather_second(part):
        for a in (0, 1):
            b1, b2 = orders[a]
            ring[a, part][0][0].wait_recv()
            ring[a, part].append(forward(a, part, b1, (b2, 1)))

    def gather_third(part):
        for a in (0, 1):
            b1, b2 = orders[a]
            ring[a, part][0][1].wait_recv()
            ring[a, part].append(forward(a, part, b2, (1,)))
            ring[a, part][1][0].wait_recv()
            ring[a, part].append(forward(a, part, b1 | b2, (1,)))

    def gather_last(part):
        for a in (0, 1):
            for group in ring[a, part]:
                group[-1].wait_recv()

    for copy in w_in[0]:
        s.sent(copy)
    w_in[1] = send_weights(1)
    gather_first(0)
    gather_second(0)
    gather_first(1)
    for copy in w_in[1]:
        s.sent(copy)
    t_in[1] = send_tokens(1)
    gather_third(0)
    gather_second(1)
    tab_in.wait_recv()
    set_gates(1, 0, tab_r[0:1, :])
    set_gates(1, 1, tab_r[1:2, :])
    for copy in t_in[0]:
        copy.wait_recv()
    half_pass(0, rows, blk)
    gather_third(1)
    first.wait_recv()
    gather_last(0)
    gather_last(1)
    half_pass(1, 0, rows + blk)

    def keep(cols, lay, back):
        lo[:, cols] = lay
        bo[:, cols] = back

    def leave(b):
        def write(cols, lay, back):
            ls[b * blk:(b + 1) * blk, cols] = lay.astype(BF)
            bs[b * blk:(b + 1) * blk, cols] = back.astype(BF)
        out_pass(rows + b * blk, blk, write)

    def send_back(b):
        cut = pl.ds(b * blk, blk)
        return [
            s.start(ls.at[cut], lr.at[cut], "expert", pair),
            s.start(bs.at[cut], br.at[cut], "expert", pair),
        ]

    leave(0)
    for copy in t_in[1]:
        copy.wait_recv()
    back_in = [send_back(0), None]
    half_pass(1, rows + blk, blk)

    tile = up_rows
    lefts = (xall, call, xall, call)
    part_rows = tile // 2
    parts = (pl.ds(0, part_rows), pl.ds(part_rows, part_rows))
    axes = ((2, 4), (4, 2))
    run = {}

    def product(a, r):
        cols = pl.ds(pl.multiple_of(flip_by(dp, r) * tile, tile), tile)
        right = gr if a % 2 else cg
        e = a // 2
        products[a, r] = mm(lefts[a][:, cols], right[:, e * hidden:(e + 1) * hidden], ((0,), (0,))).astype(BF)

    def multiply_far(a):
        base = s.count
        s.count += 4

        def copy_of(i, r):
            return pltpu.make_async_remote_copy(
                src_ref=products.at[a, r], dst_ref=slots.at[a, r // 2], send_sem=send.at[base + i],
                recv_sem=recv.at[base + i], device_id={"dp": flip(dp, 1)}, device_id_type=pl.DeviceIdType.MESH,
            )

        @pl.loop(0, 4)
        def _(i):
            r = 7 - 4 * (i % 2) - 2 * (i // 2)
            product(a, r)
            copy_of(i, r).start()

        for i in range(4):
            r = 7 - 4 * (i % 2) - 2 * (i // 2)
            copy = copy_of(i, r)
            s.all.append(copy)
            run[a, r - 1] = copy

    def multiply_near(a):
        @pl.loop(0, 4)
        def _(i):
            product(a, 6 - 4 * (i % 2) - 2 * (i // 2))

    def add_part(off, n, read_a, read_b, write):
        @pl.loop(0, n // 32)
        def _(i):
            cut = pl.ds(pl.multiple_of(off + i * 32, 32), 32)
            write(cut, read_a(cut).astype(F32) + read_b(cut).astype(F32))

    def total(a, k, off, n, other):
        def store(cut, v):
            slots[a, k, cut, :] = v.astype(BF)
        add_part(off, n, lambda cut: slots[a, k, cut, :], other, store)

    def near_sum(a, r):
        run[a, r].wait_recv()
        total(a, r // 2, 0, tile, lambda cut: products[a, r, cut, :])

    def stage0(a):
        for r in (6, 2, 4):
            near_sum(a, r)
            for h in (0, 1):
                b1 = axes[h][0]
                if r & b1:
                    far_r = r ^ b1
                    run[a, h, 1, far_r] = s.start(
                        slots.at[a, r // 2, parts[h]], slots.at[a, 4 + (far_r != 0), parts[h]], "dp", flip(dp, b1)
                    )

    def stage0_rest(a):
        near_sum(a, 0)

    def stage1(a):
        for i in (0, 1):
            for h in (0, 1):
                b2 = axes[h][1]
                r = 0 if i else b2
                run[a, h, 1, r].wait_recv()
                total(a, 4 + (r != 0), h * part_rows, part_rows, lambda cut: slots[a, r // 2, cut, :])
                if r:
                    run[a, h, 2] = s.start(slots.at[a, 5, parts[h]], slots.at[a, 6, parts[h]], "dp", flip(dp, b2))

    def stage2(a):
        for h in (0, 1):
            run[a, h, 2].wait_recv()
            if a < 2:
                out = (upv, dnv)[a]

                def write(cut, v):
                    out[cut, :] = v

                add_part(h * part_rows, part_rows, lambda cut: slots[a, 6, cut, :], lambda cut: slots[a, 4, cut, :], write)
            else:
                total(a, 6, h * part_rows, part_rows, lambda cut: slots[a, 4, cut, :])
                run[a, h, 3] = s.start(slots.at[a, 6, parts[h]], far.at[a - 2, parts[h]], "expert", mate)

    multiply_far(2)
    multiply_near(2)
    multiply_far(3)
    stage0(2)
    multiply_near(3)
    stage0(3)
    half_pass(0, rows + blk, blk)
    leave(1)
    dot_s[...] = jnp.zeros_like(dot_s)
    for e in (0, 1):
        dot_s[e:e + 1, :] = jnp.sum(jnp.transpose(dacc[e, rows:2 * rows, :]), axis=0, keepdims=True)
    back_in[1] = send_back(1)
    dots_in = s.start(dot_s, dot_r, "expert", pair)
    stage0_rest(2)
    stage0_rest(3)
    stage1(2)
    multiply_far(0)
    multiply_near(0)
    stage1(3)
    stage0(0)
    multiply_far(1)
    multiply_near(1)
    stage2(2)
    stage2(3)
    stage0(1)
    out_pass(0, rows, keep)
    stage0_rest(0)
    stage0_rest(1)
    def finish_rows(b):
        for copy in back_in[b]:
            copy.wait_recv()

        @pl.loop(0, blk // 16)
        def _(i):
            cut = pl.ds(pl.multiple_of(b * blk + i * 16, 16), 16)
            layv[cut, :] = (lo[cut, :] + lr[cut, :].astype(F32)).astype(BF)
            tokv[cut, :] = (bo[cut, :] + br[cut, :].astype(F32)).astype(BF)

    own = [jnp.sum(jnp.transpose(dacc[e, 0:rows, :]), axis=0, keepdims=True) for e in (0, 1)]
    stage1(0)
    finish_rows(0)
    stage1(1)
    finish_rows(1)
    dots_in.wait_recv()
    for k in (0, 1):
        chosen = rt[k:k + 1, :]
        acc = jnp.zeros((1, rows), F32)
        for expert, d in ((ex, own[0]), (mate, own[1]), (pair, dot_r[0:1, :]), (flip(pair, 2), dot_r[1:2, :])):
            acc = acc + jnp.where(chosen == expert, d, 0.0)
        gg_out[k:k + 1, :] = acc
    stage2(0)
    stage2(1)
    for h in (0, 1):
        run[2, h, 3].wait_recv()

        def write(cut, v):
            upv[cut, :] = v

        add_part(h * part_rows, part_rows, lambda cut: upv[cut, :], lambda cut: far[0, cut, :], write)
    for h in (0, 1):
        run[3, h, 3].wait_recv()
        here = slice(h * part_rows, (h + 1) * part_rows)

        @pl.loop(0, hidden // 128)
        def _(j):
            cols = pl.ds(pl.multiple_of(j * 128, 128), 128)
            dnt[cols, here] = jnp.transpose(dnv[here, cols] + far[1, here, cols].astype(F32))

    s.drain()


def move_kernel(*refs):
    n = len(refs) // 2
    copies = [pltpu.make_async_copy(refs[i], refs[n + i], refs[-1].at[i]) for i in range(n)]
    for copy in copies:
        copy.start()
    for copy in copies:
        copy.wait()


def flip_by(pos, mask):
    out = pos
    for b in (1, 2, 4):
        out = out + b * ((mask // b) % 2) * (1 - 2 * ((pos // b) % 2))
    return out


def local_fused(tokens, cotangent, routes, gate_probs, w_up, w_down, decay_rate):
    rows, width = tokens.shape
    hidden = w_up.shape[2]
    tile = width // 8
    sds = jax.ShapeDtypeStruct
    copies = 1 + 4 + 1 + 4 + 4 * 7 + 6 + 4 * 7 - 2 + 4
    copies = copies + 40
    anywhere = pl.BlockSpec(memory_space=pl.ANY)
    vmem = pl.BlockSpec(memory_space=pltpu.VMEM)
    results = pl.pallas_call(
        fused_kernel,
        out_shape=(
            pltpu.VMEM((rows, width), BF), pltpu.VMEM((rows, width), BF), pltpu.VMEM((2, rows), F32),
            pltpu.VMEM((tile, hidden), F32), pltpu.VMEM((hidden, tile), F32),
        ),
        in_specs=[anywhere] * 7,
        out_specs=[vmem] * 5,
        scratch_shapes=[
            pltpu.VMEM((2, rows), routes.dtype),
            pltpu.VMEM((2, rows), F32),
            pltpu.VMEM((1, hidden), F32),
            pltpu.VMEM((tile, hidden), F32),
            pltpu.VMEM((2 * rows, width), BF),
            pltpu.VMEM((2 * rows, width), BF),
            pltpu.VMEM((2, width, hidden), BF),
            pltpu.VMEM((2 * hidden, width), BF),
            pltpu.VMEM((1, hidden), F32),
            pltpu.VMEM((8, rows), F32),
            pltpu.VMEM((8, rows), F32),
            pltpu.VMEM((8, rows), F32),
            pltpu.VMEM((8, rows), F32),
            pltpu.VMEM((2, 2 * rows, 128), F32),
            pltpu.VMEM((2, 2 * rows, 128), F32),
            pltpu.VMEM((3 * rows // 2, hidden), F32),
            pltpu.VMEM((3 * rows // 2, hidden), F32),
            pltpu.VMEM((2 * rows, 2 * hidden), BF),
            pltpu.VMEM((2 * rows, 2 * hidden), BF),
            pltpu.VMEM((rows, width), F32),
            pltpu.VMEM((rows, width), F32),
            pltpu.VMEM((rows, width), BF),
            pltpu.VMEM((rows, width), BF),
            pltpu.VMEM((rows, width), BF),
            pltpu.VMEM((rows, width), BF),
            pltpu.VMEM((4, 8, tile, hidden), BF),
            pltpu.VMEM((4, 7, tile, hidden), BF),
            pltpu.VMEM((2, tile, hidden), BF),
            pltpu.SemaphoreType.DMA((7,)),
            pltpu.SemaphoreType.DMA((copies,)),
            pltpu.SemaphoreType.DMA((copies,)),
        ],
        compiler_params=pltpu.CompilerParams(
            collective_id=2, has_side_effects=True, vmem_limit_bytes=56 * 2**20
        ),
        name="layer",
    )(tokens, cotangent, routes.T, gate_probs.T, w_up[0], w_down[0], decay_rate)
    layer_out, token_grad, gate_grad, up_grad, down_grad = pl.pallas_call(
        move_kernel,
        out_shape=[sds(v.shape, v.dtype) for v in results],
        in_specs=[vmem] * 5,
        out_specs=[anywhere] * 5,
        scratch_shapes=[pltpu.SemaphoreType.DMA((5,))],
        compiler_params=pltpu.CompilerParams(vmem_limit_bytes=2**20),
        name="move",
    )(*[pltpu.with_memory_space_constraint(v, pltpu.VMEM) for v in results])
    return layer_out, token_grad, gate_grad.T, up_grad[None], down_grad[None]


def solution(mesh):
    rows = P(("dp", "expert"), None)
    local = local_fused if mesh.shape["expert"] == 4 and mesh.shape["dp"] == 8 else local_wide
    return jax.shard_map(
        local,
        mesh=mesh,
        in_specs=(rows, rows, rows, rows, P("expert", None, None), P("expert", None, None), P("expert", None)),
        out_specs=(rows, rows, rows, P("expert", "dp", None), P("expert", None, "dp")),
        check_vma=False,
    )
```

```python
from functools import partial

import jax
import jax.numpy as jnp
from jax import lax
from jax.experimental import pallas as pl
from jax.experimental.pallas import tpu as pltpu
from jax.sharding import PartitionSpec as P

STEPS = 4
SHARP = 4.0

BF = jnp.bfloat16
F32 = jnp.float32


def rate_and_slope(current, decay):
    v = jnp.zeros_like(current)
    dv = jnp.zeros_like(current)
    total = jnp.zeros_like(current)
    slope = jnp.zeros_like(current)
    for _ in range(STEPS):
        v = decay * v + current
        dv = decay * dv + 1.0
        s = jax.nn.sigmoid(SHARP * (v - 1.0))
        ds = SHARP * s * (1.0 - s) * dv
        v = v - s
        dv = dv - ds
        total = total + s
        slope = slope + ds
    return total / STEPS, slope / STEPS


def mm(a, b, dims):
    return lax.dot_general(a, b, (dims, ((), ())), preferred_element_type=F32)


def expert_block(x, cot, gate, w_up, w_down, decay):
    rates, slope = rate_and_slope(mm(x, w_up, ((1,), (0,))), decay)
    rates = rates.astype(BF)
    cot32 = cot.astype(F32)
    scaled = (gate[:, None] * cot32).astype(BF)
    out = mm(rates, w_down, ((1,), (0,))).astype(BF).astype(F32)
    layer = gate[:, None] * out
    dots = jnp.sum(cot32 * out, axis=1)
    rate_grad = mm(scaled, w_down, ((1,), (1,)))
    current_grad = (rate_grad * slope).astype(BF)
    back = mm(current_grad, w_up, ((1,), (1,))).astype(BF).astype(F32)
    return layer, dots, back, rates, scaled, current_grad


def flip(pos, mask):
    for k in range(mask.bit_length()):
        b = 1 << k
        if mask & b:
            pos = pos + b * (1 - 2 * ((pos // b) % 2))
    return pos


def bit_orders(parts):
    bits = [1 << k for k in range(parts.bit_length() - 1)]
    rest = bits[1:]
    cut = len(rest) // 2
    return bits[:1] + rest[:cut] + rest[cut:], bits[:1] + rest[cut:] + rest[:cut]


def greet(n, parts):
    ex, dp = lax.axis_index("expert"), lax.axis_index("dp")
    barrier = pltpu.get_barrier_semaphore()
    masks = list(range(1, n // 2 + 1))
    for d in masks:
        pl.semaphore_signal(barrier, inc=1, device_id={"expert": flip(ex, d)}, device_id_type=pl.DeviceIdType.MESH)
    bits = bit_orders(parts)[0]
    for b in bits:
        pl.semaphore_signal(barrier, inc=1, device_id={"dp": flip(dp, b)}, device_id_type=pl.DeviceIdType.MESH)
    pl.semaphore_wait(barrier, len(masks) + len(bits))
    return ex, dp


class Sender:
    def __init__(self, send, recv):
        self.send, self.recv, self.count, self.all = send, recv, 0, []

    def start(self, src, dst, axis, target):
        copy = self.plan(src, dst, axis, target)
        copy.start()
        return copy

    def plan(self, src, dst, axis, target):
        k = self.count
        self.count += 1
        copy = pltpu.make_async_remote_copy(
            src_ref=src, dst_ref=dst, send_sem=self.send.at[k], recv_sem=self.recv.at[k],
            device_id={axis: target}, device_id_type=pl.DeviceIdType.MESH,
        )
        self.all.append(copy)
        return copy

    def sent(self, copy):
        copy.wait_send()
        self.all = [other for other in self.all if other is not copy]

    def drain(self):
        for copy in self.all:
            copy.wait_send()


def dispatch_kernel(n, parts, x, c, t, up, down, dec, xo, co, to, upo, downo, deco, send, recv):
    ex, dp = greet(n, parts)
    half = n // 2
    s = Sender(send, recv)
    mate = flip(ex, half)
    first_up = s.start(up.at[dp], upo.at[dp], "expert", mate)
    first_down = s.start(down.at[dp], downo.at[dp], "expert", mate)
    late = [s.start(dec, deco, "expert", mate)]
    for d in range(1, half):
        to_dev = flip(ex, d)
        late.append(s.start(t, to.at[d - 1], "expert", to_dev))
        late.append(s.start(x, xo.at[d - 1], "expert", to_dev))
        late.append(s.start(c, co.at[d - 1], "expert", to_dev))
    orders = [o[::-1] for o in bit_orders(parts)]
    waiting = [[first_up], [first_down]]
    held = [[0], [0]]
    for stage in range(len(orders[0])):
        for a, buf in ((0, upo), (1, downo)):
            for copy in waiting[a]:
                copy.wait_recv()
            b = orders[a][stage]
            waiting[a] = []
            for r in held[a]:
                place = flip(dp, r)
                waiting[a].append(s.start(buf.at[place], buf.at[place], "dp", flip(dp, b)))
            held[a] = held[a] + [r ^ b for r in held[a]]
    for copy in waiting[0] + waiting[1] + late:
        copy.wait_recv()
    s.drain()


def dispatch(n, parts, x, c, t, up, down, dec):
    half = n // 2
    stack = lambda v: jax.ShapeDtypeStruct((half - 1,) + v.shape, v.dtype)
    same = lambda v: jax.ShapeDtypeStruct(v.shape, v.dtype)
    copies = 3 + 3 * (half - 1) + 2 * (parts - 1)
    anywhere = pl.BlockSpec(memory_space=pl.ANY)
    return pl.pallas_call(
        partial(dispatch_kernel, n, parts),
        out_shape=(stack(x), stack(c), stack(t), same(up), same(down), same(dec)),
        in_specs=[anywhere] * 6,
        out_specs=[anywhere] * 6,
        scratch_shapes=[pltpu.SemaphoreType.DMA((copies,)), pltpu.SemaphoreType.DMA((copies,))],
        compiler_params=pltpu.CompilerParams(collective_id=0, has_side_effects=True),
        name="dispatch",
    )(x, c, t, up, down, dec)


def add_rows(rows, read_a, read_b, write):
    step = 32 if rows % 32 == 0 else rows

    @pl.loop(0, rows // step)
    def _(i):
        cut = pl.ds(pl.multiple_of(i * step, step), step)
        write(cut, read_a(cut).astype(F32) + read_b(cut).astype(F32))


def return_kernel(n, parts, x, cg1, sc1, rt1, cg2, sc2, rt2, lay, bak, dots, upo, downo, layo, bako,
                  dotso, products, slots, far, send, recv):
    ex, dp = greet(n, parts)
    half = n // 2
    s = Sender(send, recv)
    rows = slots.shape[2]
    grads = [products.at[a] for a in range(4)]
    pairs = ((x, cg1), (sc1, rt1), (x, cg2), (sc2, rt2))
    tile = 256
    per = tile // rows

    def multiply(a):
        left, right = pairs[a]

        @pl.loop(0, left.shape[1] // tile)
        def _(i):
            cols = pl.ds(pl.multiple_of(i * tile, tile), tile)
            res = mm(left[:, cols], right[...], ((0,), (0,))).astype(BF)
            for k in range(per):
                products[a, i * per + k] = res[k * rows:(k + 1) * rows]

    orders = bit_orders(parts)
    orders = (orders[0], orders[1], orders[0], orders[1])
    stages = len(orders[0])
    place, keep = [], []
    for a in range(4):
        ids, kept, live, k = {}, [], list(range(parts)), 0
        for st in range(stages):
            live = [r for r in live if not r & orders[a][st]]
            kept.append(live)
            for r in live:
                ids[(st, r)] = k
                k += 1
        place.append(ids)
        keep.append(kept)

    def begin(a, st):
        b = orders[a][st]
        out = []
        for r in keep[a][st]:
            far_r = r ^ b
            src = grads[a].at[flip(dp, far_r)] if st == 0 else slots.at[a, place[a][(st - 1, far_r)]]
            out.append(s.start(src, slots.at[a, place[a][(st, r)]], "dp", flip(dp, b)))
        return out

    def finish(a, st, copies):
        for copy in copies:
            copy.wait_recv()
        for r in keep[a][st]:
            k = place[a][(st, r)]
            if st == 0:
                chunk = flip(dp, r)
                other = lambda cut: products[a, chunk, cut, :]
            else:
                old = place[a][(st - 1, r)]
                other = lambda cut: slots[a, old, cut, :]
            if st == stages - 1 and a < 2:
                out = (upo, downo)[a]
                def write(cut, v):
                    out[cut, :] = v
            else:
                def write(cut, v):
                    slots[a, k, cut, :] = v.astype(BF)
            add_rows(rows, lambda cut: slots[a, k, cut, :], other, write)

    late = []
    run = {}
    for d in range(1, half):
        to_dev = flip(ex, d)
        late.append(s.start(lay.at[d - 1], layo.at[d - 1], "expert", to_dev))
        late.append(s.start(bak.at[d - 1], bako.at[d - 1], "expert", to_dev))
        late.append(s.start(dots.at[d - 1], dotso.at[d - 1], "expert", to_dev))
    for a in (2, 3):
        multiply(a)
        run[a] = begin(a, 0)
    swaps = []
    for st in range(stages):
        for a in (2, 3):
            finish(a, st, run[a])
            if st + 1 < stages:
                run[a] = begin(a, st + 1)
            else:
                k = place[a][(st, 0)]
                swaps.append(s.start(slots.at[a, k], far.at[a - 2], "expert", flip(ex, half)))
        for a in (0, 1):
            if st == 0:
                multiply(a)
                run[a] = begin(a, 0)
            else:
                finish(a, st - 1, run[a])
                run[a] = begin(a, st)
    for a in (0, 1):
        finish(a, stages - 1, run[a])
    for a, out in ((0, upo), (1, downo)):
        swaps[a].wait_recv()

        def write(cut, v, out=out):
            out[cut, :] = v

        add_rows(rows, lambda cut: out[cut, :], lambda cut: far[a, cut, :], write)
    for copy in late:
        copy.wait_recv()
    s.drain()


def give_back(n, parts, factors, lay, bak, dots):
    half = n // 2
    same = lambda v: jax.ShapeDtypeStruct(v.shape, v.dtype)
    rows, cols = factors[0].shape[1] // parts, factors[1].shape[1]
    copies = 4 * (parts - 1) + 2 + 3 * (half - 1)
    anywhere = pl.BlockSpec(memory_space=pl.ANY)
    vmem = pl.BlockSpec(memory_space=pltpu.VMEM)
    shard = jax.ShapeDtypeStruct((rows, cols), F32)
    return pl.pallas_call(
        partial(return_kernel, n, parts),
        out_shape=(shard, shard, same(lay), same(bak), same(dots)),
        in_specs=[vmem] * 7 + [anywhere] * 3,
        out_specs=[vmem] * 2 + [anywhere] * 3,
        scratch_shapes=[
            pltpu.VMEM((4, parts, rows, cols), BF),
            pltpu.VMEM((4, parts - 1, rows, cols), BF),
            pltpu.VMEM((2, rows, cols), BF),
            pltpu.SemaphoreType.DMA((copies,)),
            pltpu.SemaphoreType.DMA((copies,)),
        ],
        compiler_params=pltpu.CompilerParams(
            collective_id=1, has_side_effects=True, vmem_limit_bytes=50 * 2**20
        ),
        name="give_back",
    )(*factors, lay, bak, dots)


def local_wide(tokens, cotangent, routes, gate_probs, w_up, w_down, decay_rate):
    rows, width = tokens.shape
    n = lax.axis_size("expert")
    parts = lax.axis_size("dp")
    half = n // 2
    me = lax.axis_index("expert")
    w_up, w_down, decay = w_up[0], w_down[0], decay_rate[0]
    hidden = w_up.shape[1]
    ids = jnp.arange(n, dtype=jnp.int32)
    hit = routes[None, :, :] == ids[:, None, None]
    table = jnp.sum(jnp.where(hit, gate_probs[None, :, :], 0.0), axis=2)
    x_far, cot_far, tab_far, w_up2, w_down2, decay2 = dispatch(
        n, parts, tokens, cotangent, table,
        w_up.reshape(parts, width // parts, hidden),
        w_down.reshape(parts, hidden // parts, width),
        decay[None],
    )
    w_up2 = w_up2.reshape(width, hidden)
    w_down2 = w_down2.reshape(hidden, width)
    decay2 = decay2[0]
    x_all = jnp.concatenate([tokens, x_far.reshape(-1, width)], axis=0)
    cot_all = jnp.concatenate([cotangent, cot_far.reshape(-1, width)], axis=0)
    tabs = jnp.concatenate([table[None], tab_far], axis=0)
    other = me ^ half

    def gate_of(expert):
        pick = (ids == expert)[None, :, None]
        return jnp.sum(jnp.where(pick, tabs, 0.0), axis=1).reshape(-1)

    layer1, dots1, back1, rates1, scaled1, cg1 = expert_block(
        x_all, cot_all, gate_of(me), w_up, w_down, decay
    )
    layer2, dots2, back2, rates2, scaled2, cg2 = expert_block(
        x_all, cot_all, gate_of(other), w_up2, w_down2, decay2
    )
    factors = (x_all, cg1, scaled1, rates1, cg2, scaled2, rates2)
    layer = (layer1 + layer2).reshape(half, rows, width)
    back = (back1 + back2).reshape(half, rows, width)
    dots = jnp.where((ids == me)[None, :, None], dots1.reshape(half, 1, rows), 0.0) + jnp.where(
        (ids == other)[None, :, None], dots2.reshape(half, 1, rows), 0.0
    )
    up_grad, down_grad, layer_far, back_far, dots_far = give_back(
        n, parts, factors, layer[1:].astype(BF), back[1:].astype(BF), dots[1:]
    )
    layer_out = layer[0] + jnp.sum(layer_far.astype(F32), axis=0)
    token_grad = back[0] + jnp.sum(back_far.astype(F32), axis=0)
    own = dots[0] + jnp.sum(dots_far, axis=0)
    gate_grad = jnp.sum(jnp.where(hit, own[:, :, None], 0.0), axis=0)
    return (layer_out.astype(BF), token_grad.astype(BF), gate_grad, up_grad[None], down_grad.T[None])


def lif(current, decay):
    two = current + current
    k = decay + (two - 2.0)
    a = two - 2.0
    dv = None
    for step in range(STEPS):
        if step > 0:
            a = decay * q + k
        t = jnp.tanh(a)
        q = a - t
        t2 = t * t
        if step == 0:
            e = t2
            total, slope = t, 1.0 - t2
        else:
            dv = decay * e + 1.0
            e = t2 * dv
            total, slope = total + t, slope + (dv - e)
    return 0.5 + (0.5 / STEPS) * total, (1.0 / STEPS) * slope


def fused_kernel(x, c, routes, probs, wu, wd, decay,
                 layv, tokv, gg_out, upv, dnt,
                 rt, gp, dec, dnv, xall, call, wub, wdb, decf, tab_s, tab_r, dot_s, dot_r, gcol, dacc, s_cur, s_u,
                 gr, cg, lo, bo, ls, bs, lr, br, products, slots, far, lsem, send, recv):
    ex, dp = lax.axis_index("expert"), lax.axis_index("dp")
    pair, mate = flip(ex, 1), flip(ex, 2)
    rows, width = x.shape
    hidden = wu.shape[1]
    blk = rows // 2
    s = Sender(send, recv)

    barrier = pltpu.get_barrier_semaphore()
    for axis, dev in (("expert", pair), ("expert", mate), ("dp", flip(dp, 1)), ("dp", flip(dp, 2)), ("dp", flip(dp, 4))):
        pl.semaphore_signal(barrier, inc=1, device_id={axis: dev}, device_id_type=pl.DeviceIdType.MESH)

    small = [
        pltpu.make_async_copy(routes, rt, lsem.at[4]),
        pltpu.make_async_copy(probs, gp, lsem.at[5]),
        pltpu.make_async_copy(decay, dec, lsem.at[6]),
    ]
    loads = [
        pltpu.make_async_copy(x, xall.at[pl.ds(0, rows)], lsem.at[0]),
        pltpu.make_async_copy(wu, wub.at[0], lsem.at[1]),
        pltpu.make_async_copy(c, call.at[pl.ds(0, rows)], lsem.at[2]),
        pltpu.make_async_copy(wd, wdb.at[pl.ds(0, hidden)], lsem.at[3]),
    ]
    for copy in small + loads:
        copy.start()
    pl.semaphore_wait(barrier, 5)

    up_rows, dn_rows = width // 8, hidden // 8
    def up_cut(chunk, part):
        return pl.ds(pl.multiple_of(chunk * up_rows + part * (up_rows // 2), 16), up_rows // 2)

    def dn_cut(chunk, part, base=0):
        return pl.ds(pl.multiple_of(base + chunk * dn_rows + part * (dn_rows // 2), 16), dn_rows // 2)

    def send_weights(part):
        return [
            s.start(wu.at[up_cut(dp, part)], wub.at[1, up_cut(dp, part)], "expert", mate),
            s.start(wd.at[dn_cut(dp, part)], wdb.at[dn_cut(dp, part, hidden)], "expert", mate),
        ]

    def plan_tokens(b):
        cut = pl.ds(b * blk, blk)
        there = pl.ds(rows + b * blk, blk)
        return [
            s.plan(x.at[cut], xall.at[there], "expert", pair),
            s.plan(c.at[cut], call.at[there], "expert", pair),
        ]

    w_in = [send_weights(0), None]
    t_in = [plan_tokens(0), plan_tokens(1)]
    for copy in t_in[0]:
        copy.start()
    first = s.start(decay, decf, "expert", mate)
    for copy in small:
        copy.wait()

    def gate_row(expert):
        return jnp.where(rt[0:1, :] == expert, gp[0:1, :], 0.0) + jnp.where(rt[1:2, :] == expert, gp[1:2, :], 0.0)

    tab_s[0:1, :] = gate_row(pair)
    tab_s[1:2, :] = gate_row(flip(pair, 2))
    tab_in = s.start(tab_s, tab_r, "expert", pair)

    def set_gates(slot, e, row):
        gcol[e, slot * rows:(slot + 1) * rows, :] = jnp.transpose(jnp.broadcast_to(row, (128, rows)))

    set_gates(0, 0, gate_row(ex))
    set_gates(0, 1, gate_row(mate))

    def half_pass(e, row0, m):
        @pl.loop(0, hidden // 256)
        def _(i):
            cols = pl.ds(pl.multiple_of(i * 256, 256), 256)
            far_cols = pl.ds(pl.multiple_of(e * hidden + i * 256, 256), 256)
            s_cur[0:m, cols] = mm(xall[row0:row0 + m, :], wub[e, :, cols], ((1,), (0,)))
            s_u[0:m, cols] = mm(call[row0:row0 + m, :], wdb[far_cols, :], ((1,), (1,)))

        d_ref = decf if e else dec

        @pl.loop(0, m // 16)
        def _(i):
            here = pl.ds(pl.multiple_of(i * 16, 16), 16)
            there = pl.ds(pl.multiple_of(row0 + i * 16, 16), 16)
            gate = gcol[e, there, :]
            dots = None
            for j in range(hidden // 128):
                cols = slice(j * 128, (j + 1) * 128)
                u = s_u[here, cols]
                rate, slope = lif(s_cur[here, cols], d_ref[0:1, cols])
                out = slice(e * hidden + j * 128, e * hidden + (j + 1) * 128)
                gr[there, out] = (gate * rate).astype(BF)
                cg[there, out] = (gate * u * slope).astype(BF)
                dots = rate * u if dots is None else dots + rate * u
            dacc[e, there, :] = dots

    def out_pass(row0, m, write):
        @pl.loop(0, width // 512)
        def _(i):
            cols = pl.ds(pl.multiple_of(i * 512, 512), 512)
            write(cols, mm(gr[row0:row0 + m, :], wdb[:, cols], ((1,), (0,))),
                  mm(cg[row0:row0 + m, 0:hidden], wub[0, cols, :], ((1,), (1,)))
                  + mm(cg[row0:row0 + m, hidden:2 * hidden], wub[1, cols, :], ((1,), (1,))))

    for copy in loads:
        copy.wait()
    half_pass(0, 0, rows)

    orders = ((4, 2), (2, 4))

    def forward(a, part, r, axes):
        chunk = flip(dp, r)
        ref = wub.at[1, up_cut(chunk, part)] if a == 0 else wdb.at[dn_cut(chunk, part, hidden)]
        return [s.start(ref, ref, "dp", flip(dp, b)) for b in axes]

    ring = {}

    def gather_first(part):
        for a in (0, 1):
            w_in[part][a].wait_recv()
            b1, b2 = orders[a]
            ring[a, part] = [forward(a, part, 0, (b1, b2, 1))]

    def gather_second(part):
        for a in (0, 1):
            b1, b2 = orders[a]
            ring[a, part][0][0].wait_recv()
            ring[a, part].append(forward(a, part, b1, (b2, 1)))

    def gather_third(part):
        for a in (0, 1):
            b1, b2 = orders[a]
            ring[a, part][0][1].wait_recv()
            ring[a, part].append(forward(a, part, b2, (1,)))
            ring[a, part][1][0].wait_recv()
            ring[a, part].append(forward(a, part, b1 | b2, (1,)))

    def gather_last(part):
        for a in (0, 1):
            for group in ring[a, part]:
                group[-1].wait_recv()

    for copy in w_in[0]:
        s.sent(copy)
    w_in[1] = send_weights(1)
    gather_first(0)
    gather_second(0)
    inner = jnp.logical_or(ex == 1, ex == 2)

    @pl.when(inner)
    def _():
        t_in[1][0].start()

    gather_first(1)
    for copy in w_in[1]:
        s.sent(copy)

    @pl.when(jnp.logical_not(inner))
    def _():
        t_in[1][0].start()

    t_in[1][1].start()
    gather_third(0)
    gather_second(1)
    tab_in.wait_recv()
    set_gates(1, 0, tab_r[0:1, :])
    set_gates(1, 1, tab_r[1:2, :])
    for copy in t_in[0]:
        copy.wait_recv()
    half_pass(0, rows, blk)
    gather_third(1)
    first.wait_recv()
    gather_last(0)
    gather_last(1)
    half_pass(1, 0, rows + blk)

    def keep(cols, lay, back):
        lo[:, cols] = lay
        bo[:, cols] = back

    def leave(b):
        def write(cols, lay, back):
            ls[b * blk:(b + 1) * blk, cols] = lay.astype(BF)
            bs[b * blk:(b + 1) * blk, cols] = back.astype(BF)
        out_pass(rows + b * blk, blk, write)

    def send_back(b):
        cut = pl.ds(b * blk, blk)
        return [
            s.start(ls.at[cut], lr.at[cut], "expert", pair),
            s.start(bs.at[cut], br.at[cut], "expert", pair),
        ]

    leave(0)
    for copy in t_in[1]:
        copy.wait_recv()
    back_in = [send_back(0), None]
    half_pass(1, rows + blk, blk)

    tile = up_rows
    lefts = (xall, call, xall, call)
    part_rows = tile // 2
    parts = (pl.ds(0, part_rows), pl.ds(part_rows, part_rows))
    axes = ((2, 4), (4, 2))
    run = {}

    def product(a, r):
        cols = pl.ds(pl.multiple_of(flip_by(dp, r) * tile, tile), tile)
        right = gr if a % 2 else cg
        e = a // 2
        products[a, r] = mm(lefts[a][:, cols], right[:, e * hidden:(e + 1) * hidden], ((0,), (0,))).astype(BF)

    def multiply_far(a):
        base = s.count
        s.count += 4

        def copy_of(i, r):
            return pltpu.make_async_remote_copy(
                src_ref=products.at[a, r], dst_ref=slots.at[a, r // 2], send_sem=send.at[base + i],
                recv_sem=recv.at[base + i], device_id={"dp": flip(dp, 1)}, device_id_type=pl.DeviceIdType.MESH,
            )

        @pl.loop(0, 4)
        def _(i):
            r = 7 - 4 * (i % 2) - 2 * (i // 2)
            product(a, r)
            copy_of(i, r).start()

        for i in range(4):
            r = 7 - 4 * (i % 2) - 2 * (i // 2)
            copy = copy_of(i, r)
            s.all.append(copy)
            run[a, r - 1] = copy

    def add_part(off, n, read_a, read_b, write):
        @pl.loop(0, n // 32)
        def _(i):
            cut = pl.ds(pl.multiple_of(off + i * 32, 32), 32)
            write(cut, read_a(cut).astype(F32) + read_b(cut).astype(F32))

    def total(a, k, off, n, other):
        def store(cut, v):
            slots[a, k, cut, :] = v.astype(BF)
        add_part(off, n, lambda cut: slots[a, k, cut, :], other, store)

    def near_sum(a, r):
        run[a, r].wait_recv()
        total(a, r // 2, 0, tile, lambda cut: products[a, r, cut, :])

    def stage0(a):
        for r in (6, 2, 4):
            product(a, r)
            near_sum(a, r)
            for h in (0, 1):
                b1 = axes[h][0]
                if r & b1:
                    far_r = r ^ b1
                    run[a, h, 1, far_r] = s.start(
                        slots.at[a, r // 2, parts[h]], slots.at[a, 4 + (far_r != 0), parts[h]], "dp", flip(dp, b1)
                    )

    def stage0_rest(a):
        product(a, 0)
        near_sum(a, 0)

    def stage1(a):
        for i in (0, 1):
            for h in (0, 1):
                b2 = axes[h][1]
                r = 0 if i else b2
                run[a, h, 1, r].wait_recv()
                total(a, 4 + (r != 0), h * part_rows, part_rows, lambda cut: slots[a, r // 2, cut, :])
                if r:
                    run[a, h, 2] = s.start(slots.at[a, 5, parts[h]], slots.at[a, 6, parts[h]], "dp", flip(dp, b2))

    def stage2(a):
        for h in (0, 1):
            run[a, h, 2].wait_recv()
            if a < 2:
                out = (upv, dnv)[a]

                def write(cut, v):
                    out[cut, :] = v

                add_part(h * part_rows, part_rows, lambda cut: slots[a, 6, cut, :], lambda cut: slots[a, 4, cut, :], write)
            else:
                total(a, 6, h * part_rows, part_rows, lambda cut: slots[a, 4, cut, :])
                run[a, h, 3] = s.start(slots.at[a, 6, parts[h]], far.at[a - 2, parts[h]], "expert", mate)

    multiply_far(2)
    stage0(2)
    multiply_far(3)
    stage0(3)
    half_pass(0, rows + blk, blk)
    stage0_rest(2)
    stage0_rest(3)
    stage1(2)
    leave(1)
    for e in (0, 1):
        dot_s[e:e + 1, :] = jnp.sum(jnp.transpose(dacc[e, rows:2 * rows, :]), axis=0, keepdims=True)
    back_in[1] = send_back(1)
    dots_in = s.start(dot_s, dot_r, "expert", pair)
    multiply_far(0)
    stage2(2)
    stage1(3)
    stage0(0)
    multiply_far(1)
    stage2(3)
    stage0(1)
    stage0_rest(0)
    stage0_rest(1)
    out_pass(0, rows, keep)

    def finish_rows(b):
        for copy in back_in[b]:
            copy.wait_recv()

        @pl.loop(0, blk // 16)
        def _(i):
            cut = pl.ds(pl.multiple_of(b * blk + i * 16, 16), 16)
            layv[cut, :] = (lo[cut, :] + lr[cut, :].astype(F32)).astype(BF)
            tokv[cut, :] = (bo[cut, :] + br[cut, :].astype(F32)).astype(BF)

    own = [jnp.sum(jnp.transpose(dacc[e, 0:rows, :]), axis=0, keepdims=True) for e in (0, 1)]
    stage1(0)
    finish_rows(0)
    stage1(1)
    finish_rows(1)
    dots_in.wait_recv()
    for k in (0, 1):
        chosen = rt[k:k + 1, :]
        acc = jnp.zeros((1, rows), F32)
        for expert, d in ((ex, own[0]), (mate, own[1]), (pair, dot_r[0:1, :]), (flip(pair, 2), dot_r[1:2, :])):
            acc = acc + jnp.where(chosen == expert, d, 0.0)
        gg_out[k:k + 1, :] = acc
    stage2(0)
    stage2(1)
    for h in (0, 1):
        run[2, h, 3].wait_recv()

        def write(cut, v):
            upv[cut, :] = v

        add_part(h * part_rows, part_rows, lambda cut: upv[cut, :], lambda cut: far[0, cut, :], write)
    for h in (0, 1):
        run[3, h, 3].wait_recv()
        here = slice(h * part_rows, (h + 1) * part_rows)

        @pl.loop(0, hidden // 128)
        def _(j):
            cols = pl.ds(pl.multiple_of(j * 128, 128), 128)
            dnt[cols, here] = jnp.transpose(dnv[here, cols] + far[1, here, cols].astype(F32))

    s.drain()


def move_kernel(*refs):
    n = len(refs) // 2
    copies = [pltpu.make_async_copy(refs[i], refs[n + i], refs[-1].at[i]) for i in range(n)]
    for copy in copies:
        copy.start()
    for copy in copies:
        copy.wait()


def flip_by(pos, mask):
    out = pos
    for b in (1, 2, 4):
        out = out + b * ((mask // b) % 2) * (1 - 2 * ((pos // b) % 2))
    return out


def local_fused(tokens, cotangent, routes, gate_probs, w_up, w_down, decay_rate):
    rows, width = tokens.shape
    hidden = w_up.shape[2]
    tile = width // 8
    sds = jax.ShapeDtypeStruct
    copies = 1 + 4 + 1 + 4 + 4 * 7 + 6 + 4 * 7 - 2 + 4
    copies = copies + 40
    anywhere = pl.BlockSpec(memory_space=pl.ANY)
    vmem = pl.BlockSpec(memory_space=pltpu.VMEM)
    results = pl.pallas_call(
        fused_kernel,
        out_shape=(
            pltpu.VMEM((rows, width), BF), pltpu.VMEM((rows, width), BF), pltpu.VMEM((2, rows), F32),
            pltpu.VMEM((tile, hidden), F32), pltpu.VMEM((hidden, tile), F32),
        ),
        in_specs=[anywhere] * 7,
        out_specs=[vmem] * 5,
        scratch_shapes=[
            pltpu.VMEM((2, rows), routes.dtype),
            pltpu.VMEM((2, rows), F32),
            pltpu.VMEM((1, hidden), F32),
            pltpu.VMEM((tile, hidden), F32),
            pltpu.VMEM((2 * rows, width), BF),
            pltpu.VMEM((2 * rows, width), BF),
            pltpu.VMEM((2, width, hidden), BF),
            pltpu.VMEM((2 * hidden, width), BF),
            pltpu.VMEM((1, hidden), F32),
            pltpu.VMEM((2, rows), F32),
            pltpu.VMEM((2, rows), F32),
            pltpu.VMEM((2, rows), F32),
            pltpu.VMEM((2, rows), F32),
            pltpu.VMEM((2, 2 * rows, 128), F32),
            pltpu.VMEM((2, 2 * rows, 128), F32),
            pltpu.VMEM((3 * rows // 2, hidden), F32),
            pltpu.VMEM((3 * rows // 2, hidden), F32),
            pltpu.VMEM((2 * rows, 2 * hidden), BF),
            pltpu.VMEM((2 * rows, 2 * hidden), BF),
            pltpu.VMEM((rows, width), F32),
            pltpu.VMEM((rows, width), F32),
            pltpu.VMEM((rows, width), BF),
            pltpu.VMEM((rows, width), BF),
            pltpu.VMEM((rows, width), BF),
            pltpu.VMEM((rows, width), BF),
            pltpu.VMEM((4, 8, tile, hidden), BF),
            pltpu.VMEM((4, 7, tile, hidden), BF),
            pltpu.VMEM((2, tile, hidden), BF),
            pltpu.SemaphoreType.DMA((7,)),
            pltpu.SemaphoreType.DMA((copies,)),
            pltpu.SemaphoreType.DMA((copies,)),
        ],
        compiler_params=pltpu.CompilerParams(
            collective_id=2, has_side_effects=True, vmem_limit_bytes=56 * 2**20
        ),
        name="layer",
    )(tokens, cotangent, routes.T, gate_probs.T, w_up[0], w_down[0], decay_rate)
    layer_out, token_grad, gate_grad, up_grad, down_grad = pl.pallas_call(
        move_kernel,
        out_shape=[sds(v.shape, v.dtype) for v in results],
        in_specs=[vmem] * 5,
        out_specs=[anywhere] * 5,
        scratch_shapes=[pltpu.SemaphoreType.DMA((5,))],
        compiler_params=pltpu.CompilerParams(vmem_limit_bytes=2**20),
        name="move",
    )(*[pltpu.with_memory_space_constraint(v, pltpu.VMEM) for v in results])
    return layer_out, token_grad, gate_grad.T, up_grad[None], down_grad[None]


def solution(mesh):
    rows = P(("dp", "expert"), None)
    local = local_fused if mesh.shape["expert"] == 4 and mesh.shape["dp"] == 8 else local_wide
    return jax.shard_map(
        local,
        mesh=mesh,
        in_specs=(rows, rows, rows, rows, P("expert", None, None), P("expert", None, None), P("expert", None)),
        out_specs=(rows, rows, rows, P("expert", "dp", None), P("expert", None, "dp")),
        check_vma=False,
    )
```

```python
from functools import partial

import jax
import jax.numpy as jnp
from jax import lax
from jax.experimental import pallas as pl
from jax.experimental.pallas import tpu as pltpu
from jax.sharding import PartitionSpec as P

STEPS = 4
SHARP = 4.0

BF = jnp.bfloat16
F32 = jnp.float32


def rate_and_slope(current, decay):
    v = jnp.zeros_like(current)
    dv = jnp.zeros_like(current)
    total = jnp.zeros_like(current)
    slope = jnp.zeros_like(current)
    for _ in range(STEPS):
        v = decay * v + current
        dv = decay * dv + 1.0
        s = jax.nn.sigmoid(SHARP * (v - 1.0))
        ds = SHARP * s * (1.0 - s) * dv
        v = v - s
        dv = dv - ds
        total = total + s
        slope = slope + ds
    return total / STEPS, slope / STEPS


def mm(a, b, dims):
    return lax.dot_general(a, b, (dims, ((), ())), preferred_element_type=F32)


def expert_block(x, cot, gate, w_up, w_down, decay):
    rates, slope = rate_and_slope(mm(x, w_up, ((1,), (0,))), decay)
    rates = rates.astype(BF)
    cot32 = cot.astype(F32)
    scaled = (gate[:, None] * cot32).astype(BF)
    out = mm(rates, w_down, ((1,), (0,))).astype(BF).astype(F32)
    layer = gate[:, None] * out
    dots = jnp.sum(cot32 * out, axis=1)
    rate_grad = mm(scaled, w_down, ((1,), (1,)))
    current_grad = (rate_grad * slope).astype(BF)
    back = mm(current_grad, w_up, ((1,), (1,))).astype(BF).astype(F32)
    return layer, dots, back, rates, scaled, current_grad


def flip(pos, mask):
    for k in range(mask.bit_length()):
        b = 1 << k
        if mask & b:
            pos = pos + b * (1 - 2 * ((pos // b) % 2))
    return pos


def bit_orders(parts):
    bits = [1 << k for k in range(parts.bit_length() - 1)]
    rest = bits[1:]
    cut = len(rest) // 2
    return bits[:1] + rest[:cut] + rest[cut:], bits[:1] + rest[cut:] + rest[:cut]


def greet(n, parts):
    ex, dp = lax.axis_index("expert"), lax.axis_index("dp")
    barrier = pltpu.get_barrier_semaphore()
    masks = list(range(1, n // 2 + 1))
    for d in masks:
        pl.semaphore_signal(barrier, inc=1, device_id={"expert": flip(ex, d)}, device_id_type=pl.DeviceIdType.MESH)
    bits = bit_orders(parts)[0]
    for b in bits:
        pl.semaphore_signal(barrier, inc=1, device_id={"dp": flip(dp, b)}, device_id_type=pl.DeviceIdType.MESH)
    pl.semaphore_wait(barrier, len(masks) + len(bits))
    return ex, dp


class Sender:
    def __init__(self, send, recv):
        self.send, self.recv, self.count, self.all = send, recv, 0, []

    def start(self, src, dst, axis, target):
        k = self.count
        self.count += 1
        copy = pltpu.make_async_remote_copy(
            src_ref=src, dst_ref=dst, send_sem=self.send.at[k], recv_sem=self.recv.at[k],
            device_id={axis: target}, device_id_type=pl.DeviceIdType.MESH,
        )
        copy.start()
        self.all.append(copy)
        return copy

    def drain(self):
        for copy in self.all:
            copy.wait_send()


def dispatch_kernel(n, parts, x, c, t, up, down, dec, xo, co, to, upo, downo, deco, send, recv):
    ex, dp = greet(n, parts)
    half = n // 2
    s = Sender(send, recv)
    mate = flip(ex, half)
    first_up = s.start(up.at[dp], upo.at[dp], "expert", mate)
    first_down = s.start(down.at[dp], downo.at[dp], "expert", mate)
    late = [s.start(dec, deco, "expert", mate)]
    for d in range(1, half):
        to_dev = flip(ex, d)
        late.append(s.start(t, to.at[d - 1], "expert", to_dev))
        late.append(s.start(x, xo.at[d - 1], "expert", to_dev))
        late.append(s.start(c, co.at[d - 1], "expert", to_dev))
    orders = [o[::-1] for o in bit_orders(parts)]
    waiting = [[first_up], [first_down]]
    held = [[0], [0]]
    for stage in range(len(orders[0])):
        for a, buf in ((0, upo), (1, downo)):
            for copy in waiting[a]:
                copy.wait_recv()
            b = orders[a][stage]
            waiting[a] = []
            for r in held[a]:
                place = flip(dp, r)
                waiting[a].append(s.start(buf.at[place], buf.at[place], "dp", flip(dp, b)))
            held[a] = held[a] + [r ^ b for r in held[a]]
    for copy in waiting[0] + waiting[1] + late:
        copy.wait_recv()
    s.drain()


def dispatch(n, parts, x, c, t, up, down, dec):
    half = n // 2
    stack = lambda v: jax.ShapeDtypeStruct((half - 1,) + v.shape, v.dtype)
    same = lambda v: jax.ShapeDtypeStruct(v.shape, v.dtype)
    copies = 3 + 3 * (half - 1) + 2 * (parts - 1)
    anywhere = pl.BlockSpec(memory_space=pl.ANY)
    return pl.pallas_call(
        partial(dispatch_kernel, n, parts),
        out_shape=(stack(x), stack(c), stack(t), same(up), same(down), same(dec)),
        in_specs=[anywhere] * 6,
        out_specs=[anywhere] * 6,
        scratch_shapes=[pltpu.SemaphoreType.DMA((copies,)), pltpu.SemaphoreType.DMA((copies,))],
        compiler_params=pltpu.CompilerParams(collective_id=0, has_side_effects=True),
        name="dispatch",
    )(x, c, t, up, down, dec)


def add_rows(rows, read_a, read_b, write):
    step = 32 if rows % 32 == 0 else rows

    @pl.loop(0, rows // step)
    def _(i):
        cut = pl.ds(pl.multiple_of(i * step, step), step)
        write(cut, read_a(cut).astype(F32) + read_b(cut).astype(F32))


def return_kernel(n, parts, x, cg1, sc1, rt1, cg2, sc2, rt2, lay, bak, dots, upo, downo, layo, bako,
                  dotso, products, slots, far, send, recv):
    ex, dp = greet(n, parts)
    half = n // 2
    s = Sender(send, recv)
    rows = slots.shape[2]
    grads = [products.at[a] for a in range(4)]
    pairs = ((x, cg1), (sc1, rt1), (x, cg2), (sc2, rt2))
    tile = 256
    per = tile // rows

    def multiply(a):
        left, right = pairs[a]

        @pl.loop(0, left.shape[1] // tile)
        def _(i):
            cols = pl.ds(pl.multiple_of(i * tile, tile), tile)
            res = mm(left[:, cols], right[...], ((0,), (0,))).astype(BF)
            for k in range(per):
                products[a, i * per + k] = res[k * rows:(k + 1) * rows]

    orders = bit_orders(parts)
    orders = (orders[0], orders[1], orders[0], orders[1])
    stages = len(orders[0])
    place, keep = [], []
    for a in range(4):
        ids, kept, live, k = {}, [], list(range(parts)), 0
        for st in range(stages):
            live = [r for r in live if not r & orders[a][st]]
            kept.append(live)
            for r in live:
                ids[(st, r)] = k
                k += 1
        place.append(ids)
        keep.append(kept)

    def begin(a, st):
        b = orders[a][st]
        out = []
        for r in keep[a][st]:
            far_r = r ^ b
            src = grads[a].at[flip(dp, far_r)] if st == 0 else slots.at[a, place[a][(st - 1, far_r)]]
            out.append(s.start(src, slots.at[a, place[a][(st, r)]], "dp", flip(dp, b)))
        return out

    def finish(a, st, copies):
        for copy in copies:
            copy.wait_recv()
        for r in keep[a][st]:
            k = place[a][(st, r)]
            if st == 0:
                chunk = flip(dp, r)
                other = lambda cut: products[a, chunk, cut, :]
            else:
                old = place[a][(st - 1, r)]
                other = lambda cut: slots[a, old, cut, :]
            if st == stages - 1 and a < 2:
                out = (upo, downo)[a]
                def write(cut, v):
                    out[cut, :] = v
            else:
                def write(cut, v):
                    slots[a, k, cut, :] = v.astype(BF)
            add_rows(rows, lambda cut: slots[a, k, cut, :], other, write)

    late = []
    run = {}
    for d in range(1, half):
        to_dev = flip(ex, d)
        late.append(s.start(lay.at[d - 1], layo.at[d - 1], "expert", to_dev))
        late.append(s.start(bak.at[d - 1], bako.at[d - 1], "expert", to_dev))
        late.append(s.start(dots.at[d - 1], dotso.at[d - 1], "expert", to_dev))
    for a in (2, 3):
        multiply(a)
        run[a] = begin(a, 0)
    swaps = []
    for st in range(stages):
        for a in (2, 3):
            finish(a, st, run[a])
            if st + 1 < stages:
                run[a] = begin(a, st + 1)
            else:
                k = place[a][(st, 0)]
                swaps.append(s.start(slots.at[a, k], far.at[a - 2], "expert", flip(ex, half)))
        for a in (0, 1):
            if st == 0:
                multiply(a)
                run[a] = begin(a, 0)
            else:
                finish(a, st - 1, run[a])
                run[a] = begin(a, st)
    for a in (0, 1):
        finish(a, stages - 1, run[a])
    for a, out in ((0, upo), (1, downo)):
        swaps[a].wait_recv()

        def write(cut, v, out=out):
            out[cut, :] = v

        add_rows(rows, lambda cut: out[cut, :], lambda cut: far[a, cut, :], write)
    for copy in late:
        copy.wait_recv()
    s.drain()


def give_back(n, parts, factors, lay, bak, dots):
    half = n // 2
    same = lambda v: jax.ShapeDtypeStruct(v.shape, v.dtype)
    rows, cols = factors[0].shape[1] // parts, factors[1].shape[1]
    copies = 4 * (parts - 1) + 2 + 3 * (half - 1)
    anywhere = pl.BlockSpec(memory_space=pl.ANY)
    vmem = pl.BlockSpec(memory_space=pltpu.VMEM)
    shard = jax.ShapeDtypeStruct((rows, cols), F32)
    return pl.pallas_call(
        partial(return_kernel, n, parts),
        out_shape=(shard, shard, same(lay), same(bak), same(dots)),
        in_specs=[vmem] * 7 + [anywhere] * 3,
        out_specs=[vmem] * 2 + [anywhere] * 3,
        scratch_shapes=[
            pltpu.VMEM((4, parts, rows, cols), BF),
            pltpu.VMEM((4, parts - 1, rows, cols), BF),
            pltpu.VMEM((2, rows, cols), BF),
            pltpu.SemaphoreType.DMA((copies,)),
            pltpu.SemaphoreType.DMA((copies,)),
        ],
        compiler_params=pltpu.CompilerParams(
            collective_id=1, has_side_effects=True, vmem_limit_bytes=50 * 2**20
        ),
        name="give_back",
    )(*factors, lay, bak, dots)


def local_wide(tokens, cotangent, routes, gate_probs, w_up, w_down, decay_rate):
    rows, width = tokens.shape
    n = lax.axis_size("expert")
    parts = lax.axis_size("dp")
    half = n // 2
    me = lax.axis_index("expert")
    w_up, w_down, decay = w_up[0], w_down[0], decay_rate[0]
    hidden = w_up.shape[1]
    ids = jnp.arange(n, dtype=jnp.int32)
    hit = routes[None, :, :] == ids[:, None, None]
    table = jnp.sum(jnp.where(hit, gate_probs[None, :, :], 0.0), axis=2)
    x_far, cot_far, tab_far, w_up2, w_down2, decay2 = dispatch(
        n, parts, tokens, cotangent, table,
        w_up.reshape(parts, width // parts, hidden),
        w_down.reshape(parts, hidden // parts, width),
        decay[None],
    )
    w_up2 = w_up2.reshape(width, hidden)
    w_down2 = w_down2.reshape(hidden, width)
    decay2 = decay2[0]
    x_all = jnp.concatenate([tokens, x_far.reshape(-1, width)], axis=0)
    cot_all = jnp.concatenate([cotangent, cot_far.reshape(-1, width)], axis=0)
    tabs = jnp.concatenate([table[None], tab_far], axis=0)
    other = me ^ half

    def gate_of(expert):
        pick = (ids == expert)[None, :, None]
        return jnp.sum(jnp.where(pick, tabs, 0.0), axis=1).reshape(-1)

    layer1, dots1, back1, rates1, scaled1, cg1 = expert_block(
        x_all, cot_all, gate_of(me), w_up, w_down, decay
    )
    layer2, dots2, back2, rates2, scaled2, cg2 = expert_block(
        x_all, cot_all, gate_of(other), w_up2, w_down2, decay2
    )
    factors = (x_all, cg1, scaled1, rates1, cg2, scaled2, rates2)
    layer = (layer1 + layer2).reshape(half, rows, width)
    back = (back1 + back2).reshape(half, rows, width)
    dots = jnp.where((ids == me)[None, :, None], dots1.reshape(half, 1, rows), 0.0) + jnp.where(
        (ids == other)[None, :, None], dots2.reshape(half, 1, rows), 0.0
    )
    up_grad, down_grad, layer_far, back_far, dots_far = give_back(
        n, parts, factors, layer[1:].astype(BF), back[1:].astype(BF), dots[1:]
    )
    layer_out = layer[0] + jnp.sum(layer_far.astype(F32), axis=0)
    token_grad = back[0] + jnp.sum(back_far.astype(F32), axis=0)
    own = dots[0] + jnp.sum(dots_far, axis=0)
    gate_grad = jnp.sum(jnp.where(hit, own[:, :, None], 0.0), axis=0)
    return (layer_out.astype(BF), token_grad.astype(BF), gate_grad, up_grad[None], down_grad.T[None])


class Courier:
    def __init__(self, send, recv):
        self.send, self.recv, self.sends, self.recvs, self.all = send, recv, 0, 0, []

    def new_send(self):
        self.sends += 1
        return self.sends - 1

    def new_recv(self):
        self.recvs += 1
        return self.recvs - 1

    def plan(self, src, dst, axis, target, send=None, recv=None):
        alone = send is None
        copy = pltpu.make_async_remote_copy(
            src_ref=src, dst_ref=dst, send_sem=self.send.at[self.new_send() if alone else send],
            recv_sem=self.recv.at[self.new_recv() if recv is None else recv],
            device_id={axis: target}, device_id_type=pl.DeviceIdType.MESH,
        )
        if alone:
            self.all.append(copy)
        return copy

    def start(self, src, dst, axis, target, send=None, recv=None):
        copy = self.plan(src, dst, axis, target, send, recv)
        copy.start()
        return copy

    def whole(self, ref, axis, target, send=0, recv=0):
        return pltpu.make_async_remote_copy(
            src_ref=ref, dst_ref=ref, send_sem=self.send.at[send], recv_sem=self.recv.at[recv],
            device_id={axis: target}, device_id_type=pl.DeviceIdType.MESH,
        )

    def sent(self, copy):
        copy.wait_send()
        self.all = [other for other in self.all if other is not copy]

    def drain(self):
        for copy in self.all:
            copy.wait_send()


def lif(current, decay):
    two = current + current
    k = decay + (two - 2.0)
    a = two - 2.0
    dv = None
    for step in range(STEPS):
        if step > 0:
            a = decay * q + k
        t = jnp.tanh(a)
        q = a - t
        t2 = t * t
        if step == 0:
            e = t2
            total, slope = t, 1.0 - t2
        else:
            dv = decay * e + 1.0
            e = t2 * dv
            total, slope = total + t, slope + (dv - e)
    return 0.5 + (0.5 / STEPS) * total, (1.0 / STEPS) * slope


def fused_kernel(x, c, routes, probs, wu, wd, decay,
                 layv, tokv, gg_out, upv, dnt,
                 rt, gp, dec, dnv, xall, call, wub, wdb, decf, tab_s, tab_r, dot_s, dot_r, gcol, dacc, s_cur, s_u,
                 gr, cg, lo, bo, ls, bs, lr, br, products, slots, far, lsem, send, recv):
    ex, dp = lax.axis_index("expert"), lax.axis_index("dp")
    pair, mate = flip(ex, 1), flip(ex, 2)
    rows, width = x.shape
    hidden = wu.shape[1]
    blk = rows // 2
    s = Courier(send, recv)
    gather_send, core_send, link_send, token_send, back_send = [s.new_send() for _ in range(5)]
    core_recv = [s.new_recv() for _ in range(2)]
    token_recv = [s.new_recv() for _ in range(2)]
    back_recv = [s.new_recv() for _ in range(2)]

    barrier = pltpu.get_barrier_semaphore()
    for axis, dev in (("expert", pair), ("expert", mate), ("dp", flip(dp, 1)), ("dp", flip(dp, 2)), ("dp", flip(dp, 4))):
        pl.semaphore_signal(barrier, inc=1, device_id={axis: dev}, device_id_type=pl.DeviceIdType.MESH)

    small = [
        pltpu.make_async_copy(routes, rt, lsem.at[4]),
        pltpu.make_async_copy(probs, gp, lsem.at[5]),
        pltpu.make_async_copy(decay, dec, lsem.at[6]),
    ]
    loads = [
        pltpu.make_async_copy(x, xall.at[pl.ds(0, rows)], lsem.at[0]),
        pltpu.make_async_copy(wu, wub.at[0], lsem.at[1]),
        pltpu.make_async_copy(c, call.at[pl.ds(0, rows)], lsem.at[2]),
        pltpu.make_async_copy(wd, wdb.at[pl.ds(0, hidden)], lsem.at[3]),
    ]
    for copy in small + loads:
        copy.start()
    pl.semaphore_wait(barrier, 5)

    up_rows, dn_rows = width // 8, hidden // 8
    def up_cut(chunk, part):
        return pl.ds(pl.multiple_of(chunk * up_rows + part * (up_rows // 2), 16), up_rows // 2)

    def dn_cut(chunk, part, base=0):
        return pl.ds(pl.multiple_of(base + chunk * dn_rows + part * (dn_rows // 2), 16), dn_rows // 2)

    def send_weights(part):
        return [
            s.start(wu.at[up_cut(dp, part)], wub.at[1, up_cut(dp, part)], "expert", mate),
            s.start(wd.at[dn_cut(dp, part)], wdb.at[dn_cut(dp, part, hidden)], "expert", mate),
        ]

    def plan_tokens(b):
        cut = pl.ds(b * blk, blk)
        there = pl.ds(rows + b * blk, blk)
        return [
            s.plan(x.at[cut], xall.at[there], "expert", pair, token_send, token_recv[b]),
            s.plan(c.at[cut], call.at[there], "expert", pair, token_send, token_recv[b]),
        ]

    w_in = [send_weights(0), None]
    t_in = [plan_tokens(0), plan_tokens(1)]
    for copy in t_in[0]:
        copy.start()
    first = s.start(decay, decf, "expert", mate)
    for copy in small:
        copy.wait()

    def gate_row(expert):
        return jnp.where(rt[0:1, :] == expert, gp[0:1, :], 0.0) + jnp.where(rt[1:2, :] == expert, gp[1:2, :], 0.0)

    tab_s[0:1, :] = gate_row(pair)
    tab_s[1:2, :] = gate_row(flip(pair, 2))
    tab_in = s.start(tab_s, tab_r, "expert", pair)

    def set_gates(slot, e, row):
        gcol[e, slot * rows:(slot + 1) * rows, :] = jnp.transpose(jnp.broadcast_to(row, (128, rows)))

    set_gates(0, 0, gate_row(ex))
    set_gates(0, 1, gate_row(mate))

    def half_pass(e, row0, m):
        @pl.loop(0, hidden // 256)
        def _(i):
            cols = pl.ds(pl.multiple_of(i * 256, 256), 256)
            far_cols = pl.ds(pl.multiple_of(e * hidden + i * 256, 256), 256)
            s_cur[0:m, cols] = mm(xall[row0:row0 + m, :], wub[e, :, cols], ((1,), (0,)))
            s_u[0:m, cols] = mm(call[row0:row0 + m, :], wdb[far_cols, :], ((1,), (1,)))

        d_ref = decf if e else dec

        @pl.loop(0, m // 16)
        def _(i):
            here = pl.ds(pl.multiple_of(i * 16, 16), 16)
            there = pl.ds(pl.multiple_of(row0 + i * 16, 16), 16)
            gate = gcol[e, there, :]
            dots = None
            for j in range(hidden // 128):
                cols = slice(j * 128, (j + 1) * 128)
                u = s_u[here, cols]
                rate, slope = lif(s_cur[here, cols], d_ref[0:1, cols])
                out = slice(e * hidden + j * 128, e * hidden + (j + 1) * 128)
                gr[there, out] = (gate * rate).astype(BF)
                cg[there, out] = (gate * u * slope).astype(BF)
                dots = rate * u if dots is None else dots + rate * u
            dacc[e, there, :] = dots

    def out_pass(row0, m, write):
        @pl.loop(0, width // 512)
        def _(i):
            cols = pl.ds(pl.multiple_of(i * 512, 512), 512)
            write(cols, mm(gr[row0:row0 + m, :], wdb[:, cols], ((1,), (0,))),
                  mm(cg[row0:row0 + m, 0:hidden], wub[0, cols, :], ((1,), (1,)))
                  + mm(cg[row0:row0 + m, hidden:2 * hidden], wub[1, cols, :], ((1,), (1,))))

    for copy in loads:
        copy.wait()
    half_pass(0, 0, rows)

    orders = ((4, 2), (2, 4))

    def forward(a, part, r, axes):
        chunk = flip(dp, r)
        ref = wub.at[1, up_cut(chunk, part)] if a == 0 else wdb.at[dn_cut(chunk, part, hidden)]
        return [
            s.start(ref, ref, "dp", flip(dp, b), gather_send, core_recv[a] if b == 1 else None) for b in axes
        ]

    ring = {}

    def gather_first(part):
        for a in (0, 1):
            w_in[part][a].wait_recv()
            b1, b2 = orders[a]
            ring[a, part] = [forward(a, part, 0, (b1, b2, 1))]

    def gather_second(part):
        for a in (0, 1):
            b1, b2 = orders[a]
            ring[a, part][0][0].wait_recv()
            ring[a, part].append(forward(a, part, b1, (b2, 1)))

    def gather_third(part):
        for a in (0, 1):
            b1, b2 = orders[a]
            ring[a, part][0][1].wait_recv()
            ring[a, part].append(forward(a, part, b2, (1,)))
            ring[a, part][1][0].wait_recv()
            ring[a, part].append(forward(a, part, b1 | b2, (1,)))

    def gather_last():
        s.whole(wub.at[1, pl.ds(0, width // 2)], "dp", flip(dp, 1), recv=core_recv[0]).wait_recv()
        s.whole(wdb.at[pl.ds(0, hidden // 2)], "dp", flip(dp, 1), recv=core_recv[1]).wait_recv()

    for copy in w_in[0]:
        s.sent(copy)
    w_in[1] = send_weights(1)
    gather_first(0)
    gather_second(0)
    inner = jnp.logical_or(ex == 1, ex == 2)

    @pl.when(inner)
    def _():
        t_in[1][0].start()

    gather_first(1)
    for copy in w_in[1]:
        s.sent(copy)

    @pl.when(jnp.logical_not(inner))
    def _():
        t_in[1][0].start()

    t_in[1][1].start()
    gather_third(0)
    gather_second(1)
    tab_in.wait_recv()
    set_gates(1, 0, tab_r[0:1, :])
    set_gates(1, 1, tab_r[1:2, :])
    s.whole(xall.at[pl.ds(0, 2 * blk)], "expert", pair, recv=token_recv[0]).wait_recv()
    half_pass(0, rows, blk)
    gather_third(1)
    first.wait_recv()
    gather_last()
    half_pass(1, 0, rows + blk)

    def keep(cols, lay, back):
        lo[:, cols] = lay
        bo[:, cols] = back

    def leave(b):
        def write(cols, lay, back):
            ls[b * blk:(b + 1) * blk, cols] = lay.astype(BF)
            bs[b * blk:(b + 1) * blk, cols] = back.astype(BF)
        out_pass(rows + b * blk, blk, write)

    def send_back(b):
        cut = pl.ds(b * blk, blk)
        return [
            s.start(ls.at[cut], lr.at[cut], "expert", pair, back_send, back_recv[b]),
            s.start(bs.at[cut], br.at[cut], "expert", pair, back_send, back_recv[b]),
        ]

    leave(0)
    s.whole(xall.at[pl.ds(0, 2 * blk)], "expert", pair, recv=token_recv[1]).wait_recv()
    back_in = [send_back(0), None]
    half_pass(1, rows + blk, blk)

    tile = up_rows
    lefts = (xall, call, xall, call)
    part_rows = tile // 2
    parts = (pl.ds(0, part_rows), pl.ds(part_rows, part_rows))
    axes = ((2, 4), (4, 2))
    run = {}

    def product(a, r):
        cols = pl.ds(pl.multiple_of(flip_by(dp, r) * tile, tile), tile)
        right = gr if a % 2 else cg
        e = a // 2
        products[a, r] = mm(lefts[a][:, cols], right[:, e * hidden:(e + 1) * hidden], ((0,), (0,))).astype(BF)

    def multiply_far(a):
        base = s.recvs
        s.recvs += 4

        def copy_of(i, r):
            return pltpu.make_async_remote_copy(
                src_ref=products.at[a, r], dst_ref=slots.at[a, r // 2], send_sem=send.at[core_send],
                recv_sem=recv.at[base + i], device_id={"dp": flip(dp, 1)}, device_id_type=pl.DeviceIdType.MESH,
            )

        @pl.loop(0, 4)
        def _(i):
            r = 7 - 4 * (i % 2) - 2 * (i // 2)
            product(a, r)
            copy_of(i, r).start()

        for i in range(4):
            r = 7 - 4 * (i % 2) - 2 * (i // 2)
            run[a, r - 1] = copy_of(i, r)

    def add_part(off, n, read_a, read_b, write):
        @pl.loop(0, n // 32)
        def _(i):
            cut = pl.ds(pl.multiple_of(off + i * 32, 32), 32)
            write(cut, read_a(cut).astype(F32) + read_b(cut).astype(F32))

    def total(a, k, off, n, other):
        def store(cut, v):
            slots[a, k, cut, :] = v.astype(BF)
        add_part(off, n, lambda cut: slots[a, k, cut, :], other, store)

    def near_sum(a, r):
        run[a, r].wait_recv()
        total(a, r // 2, 0, tile, lambda cut: products[a, r, cut, :])

    def stage0(a):
        for r in (6, 2, 4):
            product(a, r)
            near_sum(a, r)
            for h in (0, 1):
                b1 = axes[h][0]
                if r & b1:
                    far_r = r ^ b1
                    run[a, h, 1, far_r] = s.start(
                        slots.at[a, r // 2, parts[h]], slots.at[a, 4 + (far_r != 0), parts[h]], "dp", flip(dp, b1),
                        link_send,
                    )

    def stage0_rest(a):
        product(a, 0)
        near_sum(a, 0)

    def stage1(a):
        for i in (0, 1):
            for h in (0, 1):
                b2 = axes[h][1]
                r = 0 if i else b2
                run[a, h, 1, r].wait_recv()
                total(a, 4 + (r != 0), h * part_rows, part_rows, lambda cut: slots[a, r // 2, cut, :])
                if r:
                    run[a, h, 2] = s.start(slots.at[a, 5, parts[h]], slots.at[a, 6, parts[h]], "dp", flip(dp, b2), link_send)

    def stage2(a):
        for h in (0, 1):
            run[a, h, 2].wait_recv()
            if a < 2:
                out = (upv, dnv)[a]

                def write(cut, v):
                    out[cut, :] = v

                add_part(h * part_rows, part_rows, lambda cut: slots[a, 6, cut, :], lambda cut: slots[a, 4, cut, :], write)
            else:
                total(a, 6, h * part_rows, part_rows, lambda cut: slots[a, 4, cut, :])
                run[a, h, 3] = s.start(slots.at[a, 6, parts[h]], far.at[a - 2, parts[h]], "expert", mate, link_send)

    multiply_far(2)
    stage0(2)
    multiply_far(3)
    stage0(3)
    half_pass(0, rows + blk, blk)
    stage0_rest(2)
    stage0_rest(3)
    stage1(2)
    leave(1)
    for e in (0, 1):
        dot_s[e:e + 1, :] = jnp.sum(jnp.transpose(dacc[e, rows:2 * rows, :]), axis=0, keepdims=True)
    back_in[1] = send_back(1)
    dots_in = s.start(dot_s, dot_r, "expert", pair)
    multiply_far(0)
    stage2(2)
    stage1(3)
    stage0(0)
    multiply_far(1)
    stage2(3)
    stage0(1)
    stage0_rest(0)
    stage0_rest(1)
    out_pass(0, rows, keep)

    def finish_rows(b):
        s.whole(lr.at[pl.ds(0, 2 * blk)], "expert", pair, recv=back_recv[b]).wait_recv()

        @pl.loop(0, blk // 16)
        def _(i):
            cut = pl.ds(pl.multiple_of(b * blk + i * 16, 16), 16)
            layv[cut, :] = (lo[cut, :] + lr[cut, :].astype(F32)).astype(BF)
            tokv[cut, :] = (bo[cut, :] + br[cut, :].astype(F32)).astype(BF)

    own = [jnp.sum(jnp.transpose(dacc[e, 0:rows, :]), axis=0, keepdims=True) for e in (0, 1)]
    stage1(0)
    finish_rows(0)
    stage1(1)
    stage2(0)
    stage2(1)
    for h in (0, 1):
        run[2, h, 3].wait_recv()

        def write(cut, v):
            upv[cut, :] = v

        add_part(h * part_rows, part_rows, lambda cut: upv[cut, :], lambda cut: far[0, cut, :], write)
    for h in (0, 1):
        run[3, h, 3].wait_recv()
        here = slice(h * part_rows, (h + 1) * part_rows)

        @pl.loop(0, hidden // 128)
        def _(j):
            cols = pl.ds(pl.multiple_of(j * 128, 128), 128)
            dnt[cols, here] = jnp.transpose(dnv[here, cols] + far[1, here, cols].astype(F32))

    dots_in.wait_recv()
    for k in (0, 1):
        chosen = rt[k:k + 1, :]
        acc = jnp.zeros((1, rows), F32)
        for expert, d in ((ex, own[0]), (mate, own[1]), (pair, dot_r[0:1, :]), (flip(pair, 2), dot_r[1:2, :])):
            acc = acc + jnp.where(chosen == expert, d, 0.0)
        gg_out[k:k + 1, :] = acc
    finish_rows(1)
    s.drain()
    for ref, k in (
        (slots.at[pl.ds(0, 2)], gather_send), (products.at[:, pl.ds(0, 4)], core_send), (slots.at[pl.ds(0, 2)], link_send),
        (xall, token_send), (xall, back_send),
    ):
        s.whole(ref, "dp", flip(dp, 1), send=k).wait_send()


def move_kernel(*refs):
    n = len(refs) // 2
    copies = [pltpu.make_async_copy(refs[i], refs[n + i], refs[-1].at[i]) for i in range(n)]
    for copy in copies:
        copy.start()
    for copy in copies:
        copy.wait()


def flip_by(pos, mask):
    out = pos
    for b in (1, 2, 4):
        out = out + b * ((mask // b) % 2) * (1 - 2 * ((pos // b) % 2))
    return out


def local_fused(tokens, cotangent, routes, gate_probs, w_up, w_down, decay_rate):
    rows, width = tokens.shape
    hidden = w_up.shape[2]
    tile = width // 8
    sds = jax.ShapeDtypeStruct
    sends, recvs = 5 + 4 + 3, 6 + 4 + 4 * 3 + 3 + 4 * 10 + 4
    anywhere = pl.BlockSpec(memory_space=pl.ANY)
    vmem = pl.BlockSpec(memory_space=pltpu.VMEM)
    results = pl.pallas_call(
        fused_kernel,
        out_shape=(
            pltpu.VMEM((rows, width), BF), pltpu.VMEM((rows, width), BF), pltpu.VMEM((2, rows), F32),
            pltpu.VMEM((tile, hidden), F32), pltpu.VMEM((hidden, tile), F32),
        ),
        in_specs=[anywhere] * 7,
        out_specs=[vmem] * 5,
        scratch_shapes=[
            pltpu.VMEM((2, rows), routes.dtype),
            pltpu.VMEM((2, rows), F32),
            pltpu.VMEM((1, hidden), F32),
            pltpu.VMEM((tile, hidden), F32),
            pltpu.VMEM((2 * rows, width), BF),
            pltpu.VMEM((2 * rows, width), BF),
            pltpu.VMEM((2, width, hidden), BF),
            pltpu.VMEM((2 * hidden, width), BF),
            pltpu.VMEM((1, hidden), F32),
            pltpu.VMEM((2, rows), F32),
            pltpu.VMEM((2, rows), F32),
            pltpu.VMEM((2, rows), F32),
            pltpu.VMEM((2, rows), F32),
            pltpu.VMEM((2, 2 * rows, 128), F32),
            pltpu.VMEM((2, 2 * rows, 128), F32),
            pltpu.VMEM((3 * rows // 2, hidden), F32),
            pltpu.VMEM((3 * rows // 2, hidden), F32),
            pltpu.VMEM((2 * rows, 2 * hidden), BF),
            pltpu.VMEM((2 * rows, 2 * hidden), BF),
            pltpu.VMEM((rows, width), F32),
            pltpu.VMEM((rows, width), F32),
            pltpu.VMEM((rows, width), BF),
            pltpu.VMEM((rows, width), BF),
            pltpu.VMEM((rows, width), BF),
            pltpu.VMEM((rows, width), BF),
            pltpu.VMEM((4, 8, tile, hidden), BF),
            pltpu.VMEM((4, 7, tile, hidden), BF),
            pltpu.VMEM((2, tile, hidden), BF),
            pltpu.SemaphoreType.DMA((7,)),
            pltpu.SemaphoreType.DMA((sends,)),
            pltpu.SemaphoreType.DMA((recvs,)),
        ],
        compiler_params=pltpu.CompilerParams(
            collective_id=2, has_side_effects=True, vmem_limit_bytes=56 * 2**20
        ),
        name="layer",
    )(tokens, cotangent, routes.T, gate_probs.T, w_up[0], w_down[0], decay_rate)
    layer_out, token_grad, gate_grad, up_grad, down_grad = pl.pallas_call(
        move_kernel,
        out_shape=[sds(v.shape, v.dtype) for v in results],
        in_specs=[vmem] * 5,
        out_specs=[anywhere] * 5,
        scratch_shapes=[pltpu.SemaphoreType.DMA((5,))],
        compiler_params=pltpu.CompilerParams(vmem_limit_bytes=2**20),
        name="move",
    )(*[pltpu.with_memory_space_constraint(v, pltpu.VMEM) for v in results])
    return layer_out, token_grad, gate_grad.T, up_grad[None], down_grad[None]


def solution(mesh):
    rows = P(("dp", "expert"), None)
    local = local_fused if mesh.shape["expert"] == 4 and mesh.shape["dp"] == 8 else local_wide
    return jax.shard_map(
        local,
        mesh=mesh,
        in_specs=(rows, rows, rows, rows, P("expert", None, None), P("expert", None, None), P("expert", None)),
        out_specs=(rows, rows, rows, P("expert", "dp", None), P("expert", None, "dp")),
        check_vma=False,
    )
```

```python
from functools import partial

import jax
import jax.numpy as jnp
from jax import lax
from jax.experimental import pallas as pl
from jax.experimental.pallas import tpu as pltpu
from jax.sharding import PartitionSpec as P

STEPS = 4
SHARP = 4.0

BF = jnp.bfloat16
F32 = jnp.float32


def rate_and_slope(current, decay):
    v = jnp.zeros_like(current)
    dv = jnp.zeros_like(current)
    total = jnp.zeros_like(current)
    slope = jnp.zeros_like(current)
    for _ in range(STEPS):
        v = decay * v + current
        dv = decay * dv + 1.0
        s = jax.nn.sigmoid(SHARP * (v - 1.0))
        ds = SHARP * s * (1.0 - s) * dv
        v = v - s
        dv = dv - ds
        total = total + s
        slope = slope + ds
    return total / STEPS, slope / STEPS


def mm(a, b, dims):
    return lax.dot_general(a, b, (dims, ((), ())), preferred_element_type=F32)


def expert_block(x, cot, gate, w_up, w_down, decay):
    rates, slope = rate_and_slope(mm(x, w_up, ((1,), (0,))), decay)
    rates = rates.astype(BF)
    cot32 = cot.astype(F32)
    scaled = (gate[:, None] * cot32).astype(BF)
    out = mm(rates, w_down, ((1,), (0,))).astype(BF).astype(F32)
    layer = gate[:, None] * out
    dots = jnp.sum(cot32 * out, axis=1)
    rate_grad = mm(scaled, w_down, ((1,), (1,)))
    current_grad = (rate_grad * slope).astype(BF)
    back = mm(current_grad, w_up, ((1,), (1,))).astype(BF).astype(F32)
    return layer, dots, back, rates, scaled, current_grad


def flip(pos, mask):
    for k in range(mask.bit_length()):
        b = 1 << k
        if mask & b:
            pos = pos + b * (1 - 2 * ((pos // b) % 2))
    return pos


def bit_orders(parts):
    bits = [1 << k for k in range(parts.bit_length() - 1)]
    rest = bits[1:]
    cut = len(rest) // 2
    return bits[:1] + rest[:cut] + rest[cut:], bits[:1] + rest[cut:] + rest[:cut]


def greet(n, parts):
    ex, dp = lax.axis_index("expert"), lax.axis_index("dp")
    barrier = pltpu.get_barrier_semaphore()
    masks = list(range(1, n // 2 + 1))
    for d in masks:
        pl.semaphore_signal(barrier, inc=1, device_id={"expert": flip(ex, d)}, device_id_type=pl.DeviceIdType.MESH)
    bits = bit_orders(parts)[0]
    for b in bits:
        pl.semaphore_signal(barrier, inc=1, device_id={"dp": flip(dp, b)}, device_id_type=pl.DeviceIdType.MESH)
    pl.semaphore_wait(barrier, len(masks) + len(bits))
    return ex, dp


class Sender:
    def __init__(self, send, recv):
        self.send, self.recv, self.count, self.all = send, recv, 0, []

    def start(self, src, dst, axis, target):
        k = self.count
        self.count += 1
        copy = pltpu.make_async_remote_copy(
            src_ref=src, dst_ref=dst, send_sem=self.send.at[k], recv_sem=self.recv.at[k],
            device_id={axis: target}, device_id_type=pl.DeviceIdType.MESH,
        )
        copy.start()
        self.all.append(copy)
        return copy

    def drain(self):
        for copy in self.all:
            copy.wait_send()


def dispatch_kernel(n, parts, x, c, t, up, down, dec, xo, co, to, upo, downo, deco, send, recv):
    ex, dp = greet(n, parts)
    half = n // 2
    s = Sender(send, recv)
    mate = flip(ex, half)
    first_up = s.start(up.at[dp], upo.at[dp], "expert", mate)
    first_down = s.start(down.at[dp], downo.at[dp], "expert", mate)
    late = [s.start(dec, deco, "expert", mate)]
    for d in range(1, half):
        to_dev = flip(ex, d)
        late.append(s.start(t, to.at[d - 1], "expert", to_dev))
        late.append(s.start(x, xo.at[d - 1], "expert", to_dev))
        late.append(s.start(c, co.at[d - 1], "expert", to_dev))
    orders = [o[::-1] for o in bit_orders(parts)]
    waiting = [[first_up], [first_down]]
    held = [[0], [0]]
    for stage in range(len(orders[0])):
        for a, buf in ((0, upo), (1, downo)):
            for copy in waiting[a]:
                copy.wait_recv()
            b = orders[a][stage]
            waiting[a] = []
            for r in held[a]:
                place = flip(dp, r)
                waiting[a].append(s.start(buf.at[place], buf.at[place], "dp", flip(dp, b)))
            held[a] = held[a] + [r ^ b for r in held[a]]
    for copy in waiting[0] + waiting[1] + late:
        copy.wait_recv()
    s.drain()


def dispatch(n, parts, x, c, t, up, down, dec):
    half = n // 2
    stack = lambda v: jax.ShapeDtypeStruct((half - 1,) + v.shape, v.dtype)
    same = lambda v: jax.ShapeDtypeStruct(v.shape, v.dtype)
    copies = 3 + 3 * (half - 1) + 2 * (parts - 1)
    anywhere = pl.BlockSpec(memory_space=pl.ANY)
    return pl.pallas_call(
        partial(dispatch_kernel, n, parts),
        out_shape=(stack(x), stack(c), stack(t), same(up), same(down), same(dec)),
        in_specs=[anywhere] * 6,
        out_specs=[anywhere] * 6,
        scratch_shapes=[pltpu.SemaphoreType.DMA((copies,)), pltpu.SemaphoreType.DMA((copies,))],
        compiler_params=pltpu.CompilerParams(collective_id=0, has_side_effects=True),
        name="dispatch",
    )(x, c, t, up, down, dec)


def add_rows(rows, read_a, read_b, write):
    step = 32 if rows % 32 == 0 else rows

    @pl.loop(0, rows // step)
    def _(i):
        cut = pl.ds(pl.multiple_of(i * step, step), step)
        write(cut, read_a(cut).astype(F32) + read_b(cut).astype(F32))


def return_kernel(n, parts, x, cg1, sc1, rt1, cg2, sc2, rt2, lay, bak, dots, upo, downo, layo, bako,
                  dotso, products, slots, far, send, recv):
    ex, dp = greet(n, parts)
    half = n // 2
    s = Sender(send, recv)
    rows = slots.shape[2]
    grads = [products.at[a] for a in range(4)]
    pairs = ((x, cg1), (sc1, rt1), (x, cg2), (sc2, rt2))
    tile = 256
    per = tile // rows

    def multiply(a):
        left, right = pairs[a]

        @pl.loop(0, left.shape[1] // tile)
        def _(i):
            cols = pl.ds(pl.multiple_of(i * tile, tile), tile)
            res = mm(left[:, cols], right[...], ((0,), (0,))).astype(BF)
            for k in range(per):
                products[a, i * per + k] = res[k * rows:(k + 1) * rows]

    orders = bit_orders(parts)
    orders = (orders[0], orders[1], orders[0], orders[1])
    stages = len(orders[0])
    place, keep = [], []
    for a in range(4):
        ids, kept, live, k = {}, [], list(range(parts)), 0
        for st in range(stages):
            live = [r for r in live if not r & orders[a][st]]
            kept.append(live)
            for r in live:
                ids[(st, r)] = k
                k += 1
        place.append(ids)
        keep.append(kept)

    def begin(a, st):
        b = orders[a][st]
        out = []
        for r in keep[a][st]:
            far_r = r ^ b
            src = grads[a].at[flip(dp, far_r)] if st == 0 else slots.at[a, place[a][(st - 1, far_r)]]
            out.append(s.start(src, slots.at[a, place[a][(st, r)]], "dp", flip(dp, b)))
        return out

    def finish(a, st, copies):
        for copy in copies:
            copy.wait_recv()
        for r in keep[a][st]:
            k = place[a][(st, r)]
            if st == 0:
                chunk = flip(dp, r)
                other = lambda cut: products[a, chunk, cut, :]
            else:
                old = place[a][(st - 1, r)]
                other = lambda cut: slots[a, old, cut, :]
            if st == stages - 1 and a < 2:
                out = (upo, downo)[a]
                def write(cut, v):
                    out[cut, :] = v
            else:
                def write(cut, v):
                    slots[a, k, cut, :] = v.astype(BF)
            add_rows(rows, lambda cut: slots[a, k, cut, :], other, write)

    late = []
    run = {}
    for d in range(1, half):
        to_dev = flip(ex, d)
        late.append(s.start(lay.at[d - 1], layo.at[d - 1], "expert", to_dev))
        late.append(s.start(bak.at[d - 1], bako.at[d - 1], "expert", to_dev))
        late.append(s.start(dots.at[d - 1], dotso.at[d - 1], "expert", to_dev))
    for a in (2, 3):
        multiply(a)
        run[a] = begin(a, 0)
    swaps = []
    for st in range(stages):
        for a in (2, 3):
            finish(a, st, run[a])
            if st + 1 < stages:
                run[a] = begin(a, st + 1)
            else:
                k = place[a][(st, 0)]
                swaps.append(s.start(slots.at[a, k], far.at[a - 2], "expert", flip(ex, half)))
        for a in (0, 1):
            if st == 0:
                multiply(a)
                run[a] = begin(a, 0)
            else:
                finish(a, st - 1, run[a])
                run[a] = begin(a, st)
    for a in (0, 1):
        finish(a, stages - 1, run[a])
    for a, out in ((0, upo), (1, downo)):
        swaps[a].wait_recv()

        def write(cut, v, out=out):
            out[cut, :] = v

        add_rows(rows, lambda cut: out[cut, :], lambda cut: far[a, cut, :], write)
    for copy in late:
        copy.wait_recv()
    s.drain()


def give_back(n, parts, factors, lay, bak, dots):
    half = n // 2
    same = lambda v: jax.ShapeDtypeStruct(v.shape, v.dtype)
    rows, cols = factors[0].shape[1] // parts, factors[1].shape[1]
    copies = 4 * (parts - 1) + 2 + 3 * (half - 1)
    anywhere = pl.BlockSpec(memory_space=pl.ANY)
    vmem = pl.BlockSpec(memory_space=pltpu.VMEM)
    shard = jax.ShapeDtypeStruct((rows, cols), F32)
    return pl.pallas_call(
        partial(return_kernel, n, parts),
        out_shape=(shard, shard, same(lay), same(bak), same(dots)),
        in_specs=[vmem] * 7 + [anywhere] * 3,
        out_specs=[vmem] * 2 + [anywhere] * 3,
        scratch_shapes=[
            pltpu.VMEM((4, parts, rows, cols), BF),
            pltpu.VMEM((4, parts - 1, rows, cols), BF),
            pltpu.VMEM((2, rows, cols), BF),
            pltpu.SemaphoreType.DMA((copies,)),
            pltpu.SemaphoreType.DMA((copies,)),
        ],
        compiler_params=pltpu.CompilerParams(
            collective_id=1, has_side_effects=True, vmem_limit_bytes=50 * 2**20
        ),
        name="give_back",
    )(*factors, lay, bak, dots)


def local_wide(tokens, cotangent, routes, gate_probs, w_up, w_down, decay_rate):
    rows, width = tokens.shape
    n = lax.axis_size("expert")
    parts = lax.axis_size("dp")
    half = n // 2
    me = lax.axis_index("expert")
    w_up, w_down, decay = w_up[0], w_down[0], decay_rate[0]
    hidden = w_up.shape[1]
    ids = jnp.arange(n, dtype=jnp.int32)
    hit = routes[None, :, :] == ids[:, None, None]
    table = jnp.sum(jnp.where(hit, gate_probs[None, :, :], 0.0), axis=2)
    x_far, cot_far, tab_far, w_up2, w_down2, decay2 = dispatch(
        n, parts, tokens, cotangent, table,
        w_up.reshape(parts, width // parts, hidden),
        w_down.reshape(parts, hidden // parts, width),
        decay[None],
    )
    w_up2 = w_up2.reshape(width, hidden)
    w_down2 = w_down2.reshape(hidden, width)
    decay2 = decay2[0]
    x_all = jnp.concatenate([tokens, x_far.reshape(-1, width)], axis=0)
    cot_all = jnp.concatenate([cotangent, cot_far.reshape(-1, width)], axis=0)
    tabs = jnp.concatenate([table[None], tab_far], axis=0)
    other = me ^ half

    def gate_of(expert):
        pick = (ids == expert)[None, :, None]
        return jnp.sum(jnp.where(pick, tabs, 0.0), axis=1).reshape(-1)

    layer1, dots1, back1, rates1, scaled1, cg1 = expert_block(
        x_all, cot_all, gate_of(me), w_up, w_down, decay
    )
    layer2, dots2, back2, rates2, scaled2, cg2 = expert_block(
        x_all, cot_all, gate_of(other), w_up2, w_down2, decay2
    )
    factors = (x_all, cg1, scaled1, rates1, cg2, scaled2, rates2)
    layer = (layer1 + layer2).reshape(half, rows, width)
    back = (back1 + back2).reshape(half, rows, width)
    dots = jnp.where((ids == me)[None, :, None], dots1.reshape(half, 1, rows), 0.0) + jnp.where(
        (ids == other)[None, :, None], dots2.reshape(half, 1, rows), 0.0
    )
    up_grad, down_grad, layer_far, back_far, dots_far = give_back(
        n, parts, factors, layer[1:].astype(BF), back[1:].astype(BF), dots[1:]
    )
    layer_out = layer[0] + jnp.sum(layer_far.astype(F32), axis=0)
    token_grad = back[0] + jnp.sum(back_far.astype(F32), axis=0)
    own = dots[0] + jnp.sum(dots_far, axis=0)
    gate_grad = jnp.sum(jnp.where(hit, own[:, :, None], 0.0), axis=0)
    return (layer_out.astype(BF), token_grad.astype(BF), gate_grad, up_grad[None], down_grad.T[None])


class Courier:
    def __init__(self, send, recv):
        self.send, self.recv, self.sends, self.recvs, self.all = send, recv, 0, 0, []

    def new_send(self):
        self.sends += 1
        return self.sends - 1

    def new_recv(self):
        self.recvs += 1
        return self.recvs - 1

    def plan(self, src, dst, axis, target, send=None, recv=None):
        alone = send is None
        copy = pltpu.make_async_remote_copy(
            src_ref=src, dst_ref=dst, send_sem=self.send.at[self.new_send() if alone else send],
            recv_sem=self.recv.at[self.new_recv() if recv is None else recv],
            device_id={axis: target}, device_id_type=pl.DeviceIdType.MESH,
        )
        if alone:
            self.all.append(copy)
        return copy

    def start(self, src, dst, axis, target, send=None, recv=None):
        copy = self.plan(src, dst, axis, target, send, recv)
        copy.start()
        return copy

    def whole(self, ref, axis, target, send=0, recv=0):
        return pltpu.make_async_remote_copy(
            src_ref=ref, dst_ref=ref, send_sem=self.send.at[send], recv_sem=self.recv.at[recv],
            device_id={axis: target}, device_id_type=pl.DeviceIdType.MESH,
        )

    def sent(self, copy):
        copy.wait_send()
        self.all = [other for other in self.all if other is not copy]

    def drain(self):
        for copy in self.all:
            copy.wait_send()


def lif(current, decay):
    two = current + current
    k = decay + (two - 2.0)
    a = two - 2.0
    dv = None
    for step in range(STEPS):
        if step > 0:
            a = decay * q + k
        t = jnp.tanh(a)
        q = a - t
        t2 = t * t
        if step == 0:
            e = t2
            total, slope = t, 1.0 - t2
        else:
            dv = decay * e + 1.0
            e = t2 * dv
            total, slope = total + t, slope + (dv - e)
    return 0.5 + (0.5 / STEPS) * total, (1.0 / STEPS) * slope


def fused_kernel(x, c, routes, probs, wu, wd, decay,
                 layv, tokv, gg_out, upv, dnt,
                 rt, gp, dec, dnv, xall, call, wub, wdb, decf, tab_s, tab_r, dot_s, dot_r, gcol, dacc, s_cur, s_u,
                 gr, cg, lo, bo, ls, bs, lr, br, products, slots, far, lsem, send, recv):
    ex, dp = lax.axis_index("expert"), lax.axis_index("dp")
    pair, mate = flip(ex, 1), flip(ex, 2)
    rows, width = x.shape
    hidden = wu.shape[1]
    blk = rows // 2
    s = Courier(send, recv)
    gather_send, core_send, link_send, token_send, back_send = [s.new_send() for _ in range(5)]
    core_recv = [s.new_recv() for _ in range(2)]
    token_recv = [s.new_recv() for _ in range(2)]
    back_recv = [s.new_recv() for _ in range(2)]

    barrier = pltpu.get_barrier_semaphore()
    for axis, dev in (("expert", pair), ("expert", mate), ("dp", flip(dp, 1)), ("dp", flip(dp, 2)), ("dp", flip(dp, 4))):
        pl.semaphore_signal(barrier, inc=1, device_id={axis: dev}, device_id_type=pl.DeviceIdType.MESH)

    small = [
        pltpu.make_async_copy(routes, rt, lsem.at[4]),
        pltpu.make_async_copy(probs, gp, lsem.at[5]),
        pltpu.make_async_copy(decay, dec, lsem.at[6]),
    ]
    loads = [
        pltpu.make_async_copy(x, xall.at[pl.ds(0, rows)], lsem.at[0]),
        pltpu.make_async_copy(wu, wub.at[0], lsem.at[1]),
        pltpu.make_async_copy(c, call.at[pl.ds(0, rows)], lsem.at[2]),
        pltpu.make_async_copy(wd, wdb.at[pl.ds(0, hidden)], lsem.at[3]),
    ]
    for copy in small + loads:
        copy.start()
    pl.semaphore_wait(barrier, 5)

    up_rows, dn_rows = width // 8, hidden // 8
    def up_cut(chunk, part):
        return pl.ds(pl.multiple_of(chunk * up_rows + part * (up_rows // 2), 16), up_rows // 2)

    def dn_cut(chunk, part, base=0):
        return pl.ds(pl.multiple_of(base + chunk * dn_rows + part * (dn_rows // 2), 16), dn_rows // 2)

    def send_weights(part):
        return [
            s.start(wu.at[up_cut(dp, part)], wub.at[1, up_cut(dp, part)], "expert", mate),
            s.start(wd.at[dn_cut(dp, part)], wdb.at[dn_cut(dp, part, hidden)], "expert", mate),
        ]

    def plan_tokens(b):
        cut = pl.ds(b * blk, blk)
        there = pl.ds(rows + b * blk, blk)
        return [
            s.plan(x.at[cut], xall.at[there], "expert", pair, token_send, token_recv[b]),
            s.plan(c.at[cut], call.at[there], "expert", pair, token_send, token_recv[b]),
        ]

    w_in = [send_weights(0), None]
    t_in = [plan_tokens(0), plan_tokens(1)]
    inner = jnp.logical_or(ex == 1, ex == 2)
    t_in[0][0].start()

    @pl.when(inner)
    def _():
        t_in[0][1].start()

    first = s.start(decay, decf, "expert", mate)
    for copy in small:
        copy.wait()

    def gate_row(expert):
        return jnp.where(rt[0:1, :] == expert, gp[0:1, :], 0.0) + jnp.where(rt[1:2, :] == expert, gp[1:2, :], 0.0)

    tab_s[0:1, :] = gate_row(pair)
    tab_s[1:2, :] = gate_row(flip(pair, 2))
    tab_in = s.start(tab_s, tab_r, "expert", pair)

    def set_gates(slot, e, row):
        gcol[e, slot * rows:(slot + 1) * rows, :] = jnp.transpose(jnp.broadcast_to(row, (128, rows)))

    set_gates(0, 0, gate_row(ex))
    set_gates(0, 1, gate_row(mate))

    def half_pass(e, row0, m):
        @pl.loop(0, hidden // 256)
        def _(i):
            cols = pl.ds(pl.multiple_of(i * 256, 256), 256)
            far_cols = pl.ds(pl.multiple_of(e * hidden + i * 256, 256), 256)
            s_cur[0:m, cols] = mm(xall[row0:row0 + m, :], wub[e, :, cols], ((1,), (0,)))
            s_u[0:m, cols] = mm(call[row0:row0 + m, :], wdb[far_cols, :], ((1,), (1,)))

        d_ref = decf if e else dec

        @pl.loop(0, m // 16)
        def _(i):
            here = pl.ds(pl.multiple_of(i * 16, 16), 16)
            there = pl.ds(pl.multiple_of(row0 + i * 16, 16), 16)
            gate = gcol[e, there, :]
            dots = None
            for j in range(hidden // 128):
                cols = slice(j * 128, (j + 1) * 128)
                u = s_u[here, cols]
                rate, slope = lif(s_cur[here, cols], d_ref[0:1, cols])
                out = slice(e * hidden + j * 128, e * hidden + (j + 1) * 128)
                gr[there, out] = (gate * rate).astype(BF)
                cg[there, out] = (gate * u * slope).astype(BF)
                dots = rate * u if dots is None else dots + rate * u
            dacc[e, there, :] = dots

    def out_pass(row0, m, write):
        @pl.loop(0, width // 512)
        def _(i):
            cols = pl.ds(pl.multiple_of(i * 512, 512), 512)
            write(cols, mm(gr[row0:row0 + m, :], wdb[:, cols], ((1,), (0,))),
                  mm(cg[row0:row0 + m, 0:hidden], wub[0, cols, :], ((1,), (1,)))
                  + mm(cg[row0:row0 + m, hidden:2 * hidden], wub[1, cols, :], ((1,), (1,))))

    for copy in loads:
        copy.wait()
    half_pass(0, 0, rows)

    orders = ((4, 2), (2, 4))

    def forward(a, part, r, axes):
        chunk = flip(dp, r)
        ref = wub.at[1, up_cut(chunk, part)] if a == 0 else wdb.at[dn_cut(chunk, part, hidden)]
        return [
            s.start(ref, ref, "dp", flip(dp, b), gather_send, core_recv[a] if b == 1 else None) for b in axes
        ]

    ring = {}

    def gather_first(part):
        for a in (0, 1):
            w_in[part][a].wait_recv()
            b1, b2 = orders[a]
            ring[a, part] = [forward(a, part, 0, (b1, b2, 1))]

    def gather_second(part):
        for a in (0, 1):
            b1, b2 = orders[a]
            ring[a, part][0][0].wait_recv()
            ring[a, part].append(forward(a, part, b1, (b2, 1)))

    def gather_third(part):
        for a in (0, 1):
            b1, b2 = orders[a]
            ring[a, part][0][1].wait_recv()
            ring[a, part].append(forward(a, part, b2, (1,)))
            ring[a, part][1][0].wait_recv()
            ring[a, part].append(forward(a, part, b1 | b2, (1,)))

    def gather_last():
        s.whole(wub.at[1, pl.ds(0, width // 2)], "dp", flip(dp, 1), recv=core_recv[0]).wait_recv()
        s.whole(wdb.at[pl.ds(0, hidden // 2)], "dp", flip(dp, 1), recv=core_recv[1]).wait_recv()

    for copy in w_in[0]:
        s.sent(copy)
    w_in[1] = send_weights(1)

    @pl.when(jnp.logical_not(inner))
    def _():
        t_in[0][1].start()

    gather_first(0)
    gather_second(0)

    @pl.when(inner)
    def _():
        t_in[1][0].start()

    gather_first(1)
    for copy in w_in[1]:
        s.sent(copy)

    @pl.when(jnp.logical_not(inner))
    def _():
        t_in[1][0].start()

    t_in[1][1].start()
    gather_third(0)
    gather_second(1)
    tab_in.wait_recv()
    set_gates(1, 0, tab_r[0:1, :])
    set_gates(1, 1, tab_r[1:2, :])
    s.whole(xall.at[pl.ds(0, 2 * blk)], "expert", pair, recv=token_recv[0]).wait_recv()
    half_pass(0, rows, blk)
    gather_third(1)
    first.wait_recv()
    gather_last()
    half_pass(1, 0, rows + blk)

    def keep(cols, lay, back):
        lo[:, cols] = lay
        bo[:, cols] = back

    def leave(b):
        def write(cols, lay, back):
            ls[b * blk:(b + 1) * blk, cols] = lay.astype(BF)
            bs[b * blk:(b + 1) * blk, cols] = back.astype(BF)
        out_pass(rows + b * blk, blk, write)

    def send_back(b):
        cut = pl.ds(b * blk, blk)
        return [
            s.start(ls.at[cut], lr.at[cut], "expert", pair, back_send, back_recv[b]),
            s.start(bs.at[cut], br.at[cut], "expert", pair, back_send, back_recv[b]),
        ]

    leave(0)
    s.whole(xall.at[pl.ds(0, 2 * blk)], "expert", pair, recv=token_recv[1]).wait_recv()
    back_in = [send_back(0), None]
    half_pass(1, rows + blk, blk)

    tile = up_rows
    lefts = (xall, call, xall, call)
    part_rows = tile // 2
    parts = (pl.ds(0, part_rows), pl.ds(part_rows, part_rows))
    axes = ((2, 4), (4, 2))
    run = {}

    def product(a, r):
        cols = pl.ds(pl.multiple_of(flip_by(dp, r) * tile, tile), tile)
        right = gr if a % 2 else cg
        e = a // 2
        products[a, r] = mm(lefts[a][:, cols], right[:, e * hidden:(e + 1) * hidden], ((0,), (0,))).astype(BF)

    def multiply_far(a):
        base = s.recvs
        s.recvs += 4

        def copy_of(i, r):
            return pltpu.make_async_remote_copy(
                src_ref=products.at[a, r], dst_ref=slots.at[a, r // 2], send_sem=send.at[core_send],
                recv_sem=recv.at[base + i], device_id={"dp": flip(dp, 1)}, device_id_type=pl.DeviceIdType.MESH,
            )

        @pl.loop(0, 4)
        def _(i):
            r = 7 - 4 * (i % 2) - 2 * (i // 2)
            product(a, r)
            copy_of(i, r).start()

        for i in range(4):
            r = 7 - 4 * (i % 2) - 2 * (i // 2)
            run[a, r - 1] = copy_of(i, r)

    def add_part(off, n, read_a, read_b, write):
        @pl.loop(0, n // 32)
        def _(i):
            cut = pl.ds(pl.multiple_of(off + i * 32, 32), 32)
            write(cut, read_a(cut).astype(F32) + read_b(cut).astype(F32))

    def total(a, k, off, n, other):
        def store(cut, v):
            slots[a, k, cut, :] = v.astype(BF)
        add_part(off, n, lambda cut: slots[a, k, cut, :], other, store)

    def near_sum(a, r):
        run[a, r].wait_recv()
        total(a, r // 2, 0, tile, lambda cut: products[a, r, cut, :])

    def stage0(a):
        for r in (6, 2, 4):
            product(a, r)
            near_sum(a, r)
            for h in (0, 1):
                b1 = axes[h][0]
                if r & b1:
                    far_r = r ^ b1
                    run[a, h, 1, far_r] = s.start(
                        slots.at[a, r // 2, parts[h]], slots.at[a, 4 + (far_r != 0), parts[h]], "dp", flip(dp, b1),
                        link_send,
                    )

    def stage0_rest(a):
        product(a, 0)
        near_sum(a, 0)

    def stage1(a):
        for i in (0, 1):
            for h in (0, 1):
                b2 = axes[h][1]
                r = 0 if i else b2
                run[a, h, 1, r].wait_recv()
                total(a, 4 + (r != 0), h * part_rows, part_rows, lambda cut: slots[a, r // 2, cut, :])
                if r:
                    run[a, h, 2] = s.start(slots.at[a, 5, parts[h]], slots.at[a, 6, parts[h]], "dp", flip(dp, b2), link_send)

    def stage2(a):
        for h in (0, 1):
            run[a, h, 2].wait_recv()
            if a < 2:
                out = (upv, dnv)[a]

                def write(cut, v):
                    out[cut, :] = v

                add_part(h * part_rows, part_rows, lambda cut: slots[a, 6, cut, :], lambda cut: slots[a, 4, cut, :], write)
            else:
                total(a, 6, h * part_rows, part_rows, lambda cut: slots[a, 4, cut, :])
                run[a, h, 3] = s.start(slots.at[a, 6, parts[h]], far.at[a - 2, parts[h]], "expert", mate, link_send)

    multiply_far(2)
    stage0(2)
    multiply_far(3)
    stage0(3)
    half_pass(0, rows + blk, blk)
    stage0_rest(2)
    stage0_rest(3)
    stage1(2)
    leave(1)
    for e in (0, 1):
        dot_s[e:e + 1, :] = jnp.sum(jnp.transpose(dacc[e, rows:2 * rows, :]), axis=0, keepdims=True)
    back_in[1] = send_back(1)
    dots_in = s.start(dot_s, dot_r, "expert", pair)
    multiply_far(0)
    stage2(2)
    stage1(3)
    stage0(0)
    multiply_far(1)
    stage2(3)
    stage0(1)
    stage0_rest(0)
    stage0_rest(1)
    out_pass(0, rows, keep)

    def finish_rows(b):
        s.whole(lr.at[pl.ds(0, 2 * blk)], "expert", pair, recv=back_recv[b]).wait_recv()

        @pl.loop(0, blk // 16)
        def _(i):
            cut = pl.ds(pl.multiple_of(b * blk + i * 16, 16), 16)
            layv[cut, :] = (lo[cut, :] + lr[cut, :].astype(F32)).astype(BF)
            tokv[cut, :] = (bo[cut, :] + br[cut, :].astype(F32)).astype(BF)

    own = [jnp.sum(jnp.transpose(dacc[e, 0:rows, :]), axis=0, keepdims=True) for e in (0, 1)]
    stage1(0)
    finish_rows(0)
    stage1(1)
    stage2(0)
    stage2(1)
    for h in (0, 1):
        run[2, h, 3].wait_recv()

        def write(cut, v):
            upv[cut, :] = v

        add_part(h * part_rows, part_rows, lambda cut: upv[cut, :], lambda cut: far[0, cut, :], write)
    for h in (0, 1):
        run[3, h, 3].wait_recv()
        here = slice(h * part_rows, (h + 1) * part_rows)

        @pl.loop(0, hidden // 128)
        def _(j):
            cols = pl.ds(pl.multiple_of(j * 128, 128), 128)
            dnt[cols, here] = jnp.transpose(dnv[here, cols] + far[1, here, cols].astype(F32))

    dots_in.wait_recv()
    for k in (0, 1):
        chosen = rt[k:k + 1, :]
        acc = jnp.zeros((1, rows), F32)
        for expert, d in ((ex, own[0]), (mate, own[1]), (pair, dot_r[0:1, :]), (flip(pair, 2), dot_r[1:2, :])):
            acc = acc + jnp.where(chosen == expert, d, 0.0)
        gg_out[k:k + 1, :] = acc
    finish_rows(1)
    s.drain()
    for ref, k in (
        (slots.at[pl.ds(0, 2)], gather_send), (products.at[:, pl.ds(0, 4)], core_send), (slots.at[pl.ds(0, 2)], link_send),
        (xall, token_send), (xall, back_send),
    ):
        s.whole(ref, "dp", flip(dp, 1), send=k).wait_send()


def move_kernel(*refs):
    n = len(refs) // 2
    copies = [pltpu.make_async_copy(refs[i], refs[n + i], refs[-1].at[i]) for i in range(n)]
    for copy in copies:
        copy.start()
    for copy in copies:
        copy.wait()


def flip_by(pos, mask):
    out = pos
    for b in (1, 2, 4):
        out = out + b * ((mask // b) % 2) * (1 - 2 * ((pos // b) % 2))
    return out


def local_fused(tokens, cotangent, routes, gate_probs, w_up, w_down, decay_rate):
    rows, width = tokens.shape
    hidden = w_up.shape[2]
    tile = width // 8
    sds = jax.ShapeDtypeStruct
    sends, recvs = 5 + 4 + 3, 6 + 4 + 4 * 3 + 3 + 4 * 10 + 4
    anywhere = pl.BlockSpec(memory_space=pl.ANY)
    vmem = pl.BlockSpec(memory_space=pltpu.VMEM)
    results = pl.pallas_call(
        fused_kernel,
        out_shape=(
            pltpu.VMEM((rows, width), BF), pltpu.VMEM((rows, width), BF), pltpu.VMEM((2, rows), F32),
            pltpu.VMEM((tile, hidden), F32), pltpu.VMEM((hidden, tile), F32),
        ),
        in_specs=[anywhere] * 7,
        out_specs=[vmem] * 5,
        scratch_shapes=[
            pltpu.VMEM((2, rows), routes.dtype),
            pltpu.VMEM((2, rows), F32),
            pltpu.VMEM((1, hidden), F32),
            pltpu.VMEM((tile, hidden), F32),
            pltpu.VMEM((2 * rows, width), BF),
            pltpu.VMEM((2 * rows, width), BF),
            pltpu.VMEM((2, width, hidden), BF),
            pltpu.VMEM((2 * hidden, width), BF),
            pltpu.VMEM((1, hidden), F32),
            pltpu.VMEM((2, rows), F32),
            pltpu.VMEM((2, rows), F32),
            pltpu.VMEM((2, rows), F32),
            pltpu.VMEM((2, rows), F32),
            pltpu.VMEM((2, 2 * rows, 128), F32),
            pltpu.VMEM((2, 2 * rows, 128), F32),
            pltpu.VMEM((3 * rows // 2, hidden), F32),
            pltpu.VMEM((3 * rows // 2, hidden), F32),
            pltpu.VMEM((2 * rows, 2 * hidden), BF),
            pltpu.VMEM((2 * rows, 2 * hidden), BF),
            pltpu.VMEM((rows, width), F32),
            pltpu.VMEM((rows, width), F32),
            pltpu.VMEM((rows, width), BF),
            pltpu.VMEM((rows, width), BF),
            pltpu.VMEM((rows, width), BF),
            pltpu.VMEM((rows, width), BF),
            pltpu.VMEM((4, 8, tile, hidden), BF),
            pltpu.VMEM((4, 7, tile, hidden), BF),
            pltpu.VMEM((2, tile, hidden), BF),
            pltpu.SemaphoreType.DMA((7,)),
            pltpu.SemaphoreType.DMA((sends,)),
            pltpu.SemaphoreType.DMA((recvs,)),
        ],
        compiler_params=pltpu.CompilerParams(
            collective_id=2, has_side_effects=True, vmem_limit_bytes=56 * 2**20
        ),
        name="layer",
    )(tokens, cotangent, routes.T, gate_probs.T, w_up[0], w_down[0], decay_rate)
    layer_out, token_grad, gate_grad, up_grad, down_grad = pl.pallas_call(
        move_kernel,
        out_shape=[sds(v.shape, v.dtype) for v in results],
        in_specs=[vmem] * 5,
        out_specs=[anywhere] * 5,
        scratch_shapes=[pltpu.SemaphoreType.DMA((5,))],
        compiler_params=pltpu.CompilerParams(vmem_limit_bytes=2**20),
        name="move",
    )(*[pltpu.with_memory_space_constraint(v, pltpu.VMEM) for v in results])
    return layer_out, token_grad, gate_grad.T, up_grad[None], down_grad[None]


def solution(mesh):
    rows = P(("dp", "expert"), None)
    local = local_fused if mesh.shape["expert"] == 4 and mesh.shape["dp"] == 8 else local_wide
    return jax.shard_map(
        local,
        mesh=mesh,
        in_specs=(rows, rows, rows, rows, P("expert", None, None), P("expert", None, None), P("expert", None)),
        out_specs=(rows, rows, rows, P("expert", "dp", None), P("expert", None, "dp")),
        check_vma=False,
    )
```
